256 devices in a mesh: section: 2 (over core), expert: 32 (over z, y), dp: 4 (over x).
Axes of the slice: x: 4, y: 4, z: 8, core: 2. Of those that a mesh axis runs over, the one named last changes fastest.
Arguments:
- x_in: bfloat16 [2, 128, 64, 3584], P(None, ('expert', 'dp')), may hold values from -6 to 6
- dy_out: bfloat16 [2, 128, 64, 3584], P(None, ('expert', 'dp')), may hold values from -6 to 6
- routes: int32 [2, 2, 128, 64, 1], P('section', None, ('expert', 'dp')), may hold values from 0 to 31; in each aligned block of 64 rows (0 to 63, 64 to 127, ..., all dimensions but the last counted through in order) at most 3 rows name the same one
- gates: float32 [2, 2, 128, 64, 1], P('section', None, ('expert', 'dp')), may hold values from 0.2 to 1
- w_down: bfloat16 [2, 3584, 256], P('section'), may hold values from -0.09375 to 0.09375
- w_qk: bfloat16 [2, 256, 256], P('section'), may hold values from -0.375 to 0.375
- w_up: bfloat16 [2, 256, 3584], P('section'), may hold values from -0.375 to 0.375
- e_gate: bfloat16 [2, 32, 3584, 1024], P('section', 'expert', None, 'dp'), may hold values from -0.09375 to 0.09375
- e_up: bfloat16 [2, 32, 3584, 1024], P('section', 'expert', None, 'dp'), may hold values from -0.09375 to 0.09375
- e_down: bfloat16 [2, 32, 1024, 3584], P('section', 'expert', 'dp'), may hold values from -0.1875 to 0.1875
Outputs:
- activations: bfloat16 [2, 2, 128, 64, 3584], P('section', None, ('expert', 'dp'))
- grads_in: bfloat16 [2, 2, 128, 64, 3584], P('section', None, ('expert', 'dp'))
- g_down: float32 [2, 3584, 256], P('section', ('expert', 'dp'))
- g_qk: float32 [2, 256, 256], P('section', ('expert', 'dp'))
- g_up_t: float32 [2, 3584, 256], P('section', ('expert', 'dp'))
The draws below stay inside these ranges and needn't reach their ends.
Inputs may be any that keep to these rules, and one draw needn't show every extreme that they name: `routes`: within each sequence of one micro-batch and layer, every expert is named by at most 3 tokens, a bound that some block reaches.
All inputs are finite; a program needn't handle non-finite values.
Results may differ from the reference program's by a relative error of at most 0.035.
Values may be sent and summed in bfloat16 or wider, within the bound.
A program may use at most 128 MiB of HBM per device.

```python
import math
import jax
import jax.numpy as jnp
import numpy as np
from jax import lax

D = 3584
LAT = 256
FF = 1024
SEQ = 64
MICRO = 2
TOPK = 1
EXPERTS = 32
BATCH = 128
CAP = 3
N_SECTION = 2
N_DP = 4


def shard_levels(own_key, extent, pieces, least, largest):
    def one(dim, blocks):
        heights = jax.random.uniform(jax.random.fold_in(jax.random.fold_in(own_key, 6), dim), (blocks,), jnp.float32, least / len(pieces), largest / len(pieces))
        return jnp.repeat(jnp.exp(heights), extent[dim] // blocks).reshape((-1,) + (1,) * (len(extent) - dim - 1))

    factor_of = one(*pieces[0])
    for cut in pieces[1:]:
        factor_of = factor_of * one(*cut)
    return factor_of


def shared_out(rng, own, number, rows, count, top, reach, skew):
    ranking = jax.random.permutation(rng, count)
    crowded, usual = shares(count, rows * top, reach, skew, True), shares(count, rows * top, reach, skew, False)
    places = jnp.arange(count)

    def named(sizes, rotation):
        used = int((sizes > 0).sum())
        fixed = max(1, used // 4)
        shifted = fixed + (places - fixed + rotation * (used - fixed)) % max(1, count - fixed)
        return jnp.zeros((count,), jnp.int32).at[ranking[jnp.where(places < fixed, places, shifted)]].set(jnp.asarray(sizes, jnp.int32))

    sizes = jnp.where(number % 4 == 0, named(crowded, number // 4), named(usual, number - number // 4 - 1))
    mixed = jax.random.permutation(jax.random.fold_in(own, 3), count)
    giver, taker = mixed[0:count // 2 * 2:2], mixed[1:count // 2 * 2:2]
    slack = jnp.minimum(sizes[giver] - 1, reach - sizes[taker]) // 2
    slack = jnp.where((giver == ranking[0]) | (taker == ranking[0]) | (sizes[taker] == 0), 0, jnp.maximum(slack, 0))
    shifted = jax.random.randint(jax.random.fold_in(own, 4), (count // 2,), 0, 1 << 20) % (slack + 1)
    sizes = sizes.at[giver].add(-shifted).at[taker].add(shifted)
    items = jnp.searchsorted(jnp.cumsum(sizes), jnp.arange(rows * top), side="right").astype(jnp.int32)
    listing = items.reshape(top, rows).T
    listing = listing[jax.random.permutation(jax.random.fold_in(own, 1), rows)]
    rotation = jax.random.randint(jax.random.fold_in(own, 2), (rows, 1), 0, top)
    return jnp.take_along_axis(listing, (jnp.arange(top)[None, :] + rotation) % top, axis=1)


def shares(count, total, limit, skew, full):
    loads = [(1 << 20) // math.isqrt(rank ** skew) + 1 for rank in range(1, count + 1)]
    largest = limit if full else min(limit, max(-(-total // count), total * loads[0] // sum(loads)))
    least = 1 if total - largest >= count - 1 else 0
    given, spare = [largest] + [least] * (count - 1), total - largest - least * (count - 1)
    while spare > 0:
        free = [i for i in range(1, count) if given[i] < largest] or [i for i in range(1, count) if given[i] < limit]
        pool, left = sum([loads[i] for i in free]), spare
        for i in free:
            more = min(limit - given[i], max(1, left * loads[i] // pool), spare)
            given[i] = given[i] + more
            spare = spare - more
    return np.array(given)


def scatter_about(rng, shape, width, reach, pieces=(), held_as=jnp.bfloat16):
    array = width * jax.random.normal(rng, shape, jnp.float32)
    if pieces:
        array = array * shard_levels(rng, shape, pieces, -0.22, 0.18)
    return jnp.clip(array, -reach, reach).astype(held_as)


def setup_inputs(seed: int = 0) -> dict:
    keys = jax.random.split(jax.random.key(seed), 11)
    x_in = scatter_about(keys[0], (MICRO, BATCH, SEQ, D), 1.0, 6.0, ((1, 128),))
    dy_out = scatter_about(keys[1], (MICRO, BATCH, SEQ, D), 1.0, 6.0, ((1, 128),))
    routes_keys = jax.random.split(jax.random.fold_in(keys[2], 1), N_SECTION * MICRO * BATCH * SEQ // SEQ)
    routes_turns = jax.random.permutation(jax.random.fold_in(keys[2], 3), N_SECTION * MICRO * BATCH * SEQ // SEQ)
    routes = jax.vmap(lambda own, number: shared_out(jax.random.fold_in(keys[2], 2), own, number, SEQ, EXPERTS, TOPK, CAP, 2))(routes_keys, routes_turns).reshape((N_SECTION, MICRO, BATCH, SEQ, TOPK))
    gates = jnp.clip(0.2 + 0.8 * jax.random.uniform(keys[3], (N_SECTION, MICRO, BATCH, SEQ, TOPK), jnp.float32) ** shard_levels(keys[3], (N_SECTION, MICRO, BATCH, SEQ, TOPK), ((0, 2), (2, 128)), -0.2, 0.2), 0.2, 1.0)
    w_down = scatter_about(keys[4], (N_SECTION, D, LAT), D ** -0.5, 0.09375, ((0, 2),))
    w_qk = scatter_about(keys[5], (N_SECTION, LAT, LAT), LAT ** -0.5, 0.375, ((0, 2),))
    w_up = scatter_about(keys[6], (N_SECTION, LAT, D), LAT ** -0.5, 0.375, ((0, 2),))
    e_gate = scatter_about(keys[7], (N_SECTION, EXPERTS, D, FF), D ** -0.5, 0.09375, ((0, 2), (1, 32), (3, 4)))
    e_up = scatter_about(keys[8], (N_SECTION, EXPERTS, D, FF), D ** -0.5, 0.09375, ((0, 2), (1, 32), (3, 4)))
    e_down = scatter_about(keys[9], (N_SECTION, EXPERTS, FF, D), FF ** -0.5, 0.1875, ((0, 2), (1, 32), (2, 4)))
    return dict(x_in=x_in, dy_out=dy_out, routes=routes, gates=gates, w_down=w_down, w_qk=w_qk, w_up=w_up, e_gate=e_gate, e_up=e_up, e_down=e_down)


epsilon = 1e-06

def times_t(left, right):
    return lax.dot_general(left, right, (((left.ndim - 1,), (right.ndim - 1,)), ((), ())), preferred_element_type=jnp.float32)

def t_times(left, right):
    return lax.dot_general(left, right, (((0,), (0,)), ((), ())), preferred_element_type=jnp.float32)

def rms_norm(values):
    inv_rms = lax.rsqrt(lax.optimization_barrier(jnp.mean(values * values, axis=-1, keepdims=True)) + epsilon)
    return (values * inv_rms, inv_rms)

def rms_back(normed, inv_rms, upstream):
    return inv_rms * (upstream - normed * lax.optimization_barrier(jnp.mean(upstream * normed, axis=-1, keepdims=True)))

def silu_parts(gate_pre):
    sigmoid = jax.nn.sigmoid(gate_pre)
    return (gate_pre * sigmoid, sigmoid * (1.0 + gate_pre * (1.0 - sigmoid)))

def attend_forward(inputs, w_down, w_qk, w_up):
    normed, inv_rms = rms_norm(inputs.astype(jnp.float32))
    normed_b = normed.astype(jnp.bfloat16)
    latent = jnp.dot(normed_b, w_down, preferred_element_type=jnp.float32).astype(jnp.bfloat16)
    queries = jnp.dot(latent, w_qk, preferred_element_type=jnp.float32).astype(jnp.bfloat16)
    length = inputs.shape[0]
    scale_qk = latent.shape[1] ** (-0.5)
    scores = times_t(queries, latent) * scale_qk
    causal = lax.broadcasted_iota(jnp.int32, (length, length), 0) >= lax.broadcasted_iota(jnp.int32, (length, length), 1)
    scores = jnp.where(causal, scores, -1e+30)
    row_max = lax.optimization_barrier(jnp.max(scores, axis=-1, keepdims=True))
    exponent = jnp.exp(scores - row_max)
    attn_probs = exponent / lax.optimization_barrier(jnp.sum(exponent, axis=-1, keepdims=True))
    probs_b = attn_probs.astype(jnp.bfloat16)
    mixed_rows = jnp.dot(probs_b, latent, preferred_element_type=jnp.float32).astype(jnp.bfloat16)
    residual = (inputs.astype(jnp.float32) + jnp.dot(mixed_rows, w_up, preferred_element_type=jnp.float32)).astype(jnp.bfloat16)
    return (residual, (normed, inv_rms, normed_b, latent, queries, attn_probs, probs_b, mixed_rows))

def attend_backward(kept, upstream, w_down, w_qk, w_up):
    normed, inv_rms, normed_b, latent, queries, attn_probs, probs_b, mixed_rows = kept
    scale_qk = latent.shape[1] ** (-0.5)
    upstream_b = upstream.astype(jnp.bfloat16)
    d_mixed = times_t(upstream_b, w_up).astype(jnp.bfloat16)
    g_up_t = t_times(upstream_b, mixed_rows)
    d_probs = times_t(d_mixed, latent)
    d_scores = (attn_probs * (d_probs - lax.optimization_barrier(jnp.sum(d_probs * attn_probs, axis=-1, keepdims=True))) * scale_qk).astype(jnp.bfloat16)
    d_queries = jnp.dot(d_scores, latent, preferred_element_type=jnp.float32).astype(jnp.bfloat16)
    g_qk = t_times(latent, d_queries)
    d_latent = (t_times(probs_b, d_mixed) + t_times(d_scores, queries) + times_t(d_queries, w_qk)).astype(jnp.bfloat16)
    g_down = t_times(normed_b, d_latent)
    d_normed = times_t(d_latent, w_down)
    return (upstream + rms_back(normed, inv_rms, d_normed), g_down, g_qk, g_up_t)

def slot_table(route_ids, experts, capacity):
    one_hot = (route_ids[:, None] == jnp.arange(experts, dtype=jnp.int32)[None, :]).astype(jnp.int32)
    order_rank = lax.optimization_barrier(jnp.sum((jnp.cumsum(one_hot, axis=0) - one_hot) * one_hot, axis=1))
    return (route_ids * capacity + order_rank).astype(jnp.int32)

def pick_rows(table, slot_index):
    return table[slot_index]

def to_sequences(by_expert, batch_size, experts, model_width):
    return by_expert.reshape(experts, batch_size, CAP, model_width).transpose(1, 0, 2, 3).reshape(batch_size, experts * CAP, model_width)

def layer_forward(inputs, route_ids, gate_vals, w_down, w_qk, w_up, e_gate, e_up, e_down):
    batch_size, length, model_width = inputs.shape
    top_count = route_ids.shape[2]
    experts = e_gate.shape[0]
    hidden = e_gate.shape[2]
    quarters = N_DP
    split = hidden // quarters
    residual, kept_attn = jax.vmap(attend_forward, in_axes=(0, None, None, None))(inputs, w_down, w_qk, w_up)
    normed, inv_rms = rms_norm(residual.astype(jnp.float32))
    normed_b = normed.astype(jnp.bfloat16)
    slot_index = jax.vmap(slot_table, in_axes=(0, None, None))(route_ids.reshape(batch_size, length * top_count), experts, CAP)
    placement = (slot_index[:, None, :] == jnp.arange(experts * CAP, dtype=jnp.int32)[None, :, None]).astype(jnp.float32)
    rows_k = jnp.repeat(normed_b, top_count, axis=1).astype(jnp.float32)
    sent = jnp.einsum('bcs,bsd->bcd', placement, rows_k).astype(jnp.bfloat16)
    by_expert = sent.reshape(batch_size, experts, CAP, model_width).transpose(1, 0, 2, 3).reshape(experts, batch_size * CAP, model_width)

    def expert_forward(operands):
        expert_rows, gate_w, up_w, down_w = operands
        gate_pre = jnp.dot(expert_rows, gate_w, preferred_element_type=jnp.float32)
        up_pre = jnp.dot(expert_rows, up_w, preferred_element_type=jnp.float32)
        hidden_b = (silu_parts(gate_pre)[0] * up_pre).astype(jnp.bfloat16)
        row_count = expert_rows.shape[0]
        partial_value = jnp.einsum('rqf,qfd->rqd', hidden_b.reshape(row_count, quarters, split).astype(jnp.float32), down_w.reshape(quarters, split, model_width).astype(jnp.float32))
        partial_value = lax.optimization_barrier(partial_value.astype(jnp.bfloat16)).astype(jnp.float32)
        return (lax.optimization_barrier(jnp.sum(partial_value, axis=1)), gate_pre, up_pre)
    summed, gate_pre, up_pre = lax.map(expert_forward, (by_expert, e_gate, e_up, e_down))
    summed = to_sequences(summed, batch_size, experts, model_width)
    picked = jax.vmap(pick_rows)(summed, slot_index)
    mixture = lax.optimization_barrier(jnp.sum(picked.reshape(batch_size, length, top_count, model_width) * gate_vals[..., None], axis=2))
    output = (residual.astype(jnp.float32) + mixture).astype(jnp.bfloat16)
    return (output, (kept_attn, normed, inv_rms, slot_index, placement, gate_pre, up_pre))

def layer_backward(kept, upstream, gate_vals, w_down, w_qk, w_up, e_gate, e_up, e_down):
    kept_attn, normed, inv_rms, slot_index, placement, gate_pre, up_pre = kept
    batch_size, length, model_width = upstream.shape
    top_count = gate_vals.shape[2]
    experts = e_gate.shape[0]
    hidden = e_gate.shape[2]
    quarters = N_DP
    split = hidden // quarters
    scaled = (upstream[:, :, None, :] * gate_vals[..., None]).reshape(batch_size, length * top_count, model_width).astype(jnp.bfloat16)
    sent = jnp.einsum('bcs,bsd->bcd', placement, scaled.astype(jnp.float32)).astype(jnp.bfloat16)
    by_expert = sent.reshape(batch_size, experts, CAP, model_width).transpose(1, 0, 2, 3).reshape(experts, batch_size * CAP, model_width)

    def expert_backward(operands):
        expert_rows, gate_in, up_in, gate_w, up_w, down_w = operands
        d_hidden = times_t(expert_rows, down_w)
        activated, slope = silu_parts(gate_in)
        d_gate = (d_hidden * up_in * slope).astype(jnp.bfloat16)
        d_up = (d_hidden * activated).astype(jnp.bfloat16)
        row_count = expert_rows.shape[0]
        returned = jnp.einsum('rqf,dqf->rqd', d_gate.reshape(row_count, quarters, split).astype(jnp.float32), gate_w.reshape(model_width, quarters, split).astype(jnp.float32))
        returned = returned + jnp.einsum('rqf,dqf->rqd', d_up.reshape(row_count, quarters, split).astype(jnp.float32), up_w.reshape(model_width, quarters, split).astype(jnp.float32))
        returned = lax.optimization_barrier(returned.astype(jnp.bfloat16)).astype(jnp.float32)
        return lax.optimization_barrier(jnp.sum(returned, axis=1))
    summed = lax.map(expert_backward, (by_expert, gate_pre, up_pre, e_gate, e_up, e_down))
    summed = to_sequences(summed, batch_size, experts, model_width)
    picked = jax.vmap(pick_rows)(summed, slot_index)
    d_normed = lax.optimization_barrier(jnp.sum(picked.reshape(batch_size, length, top_count, model_width), axis=2))
    d_resid = upstream + rms_back(normed, inv_rms, d_normed)
    d_input, g_down, g_qk, g_up_t = jax.vmap(attend_backward, in_axes=(0, 0, None, None, None))(kept_attn, d_resid, w_down, w_qk, w_up)
    return (d_input, lax.optimization_barrier(jnp.sum(g_down, axis=0)), lax.optimization_barrier(jnp.sum(g_qk, axis=0)), lax.optimization_barrier(jnp.sum(g_up_t, axis=0)))

def reference(x_in, dy_out, routes, gates, w_down, w_qk, w_up, e_gate, e_up, e_down):
    layer_in = x_in
    activations = []
    kept_all = []
    for section_index in range(N_SECTION):
        outputs = []
        kept_section = []
        for micro_idx in range(MICRO):
            output, kept = layer_forward(layer_in[micro_idx], routes[section_index, micro_idx], gates[section_index, micro_idx], w_down[section_index], w_qk[section_index], w_up[section_index], e_gate[section_index], e_up[section_index], e_down[section_index])
            outputs.append(output)
            kept_section.append(kept)
        layer_in = jnp.stack(outputs)
        activations.append(layer_in)
        kept_all.append(kept_section)
    upstream_all = dy_out.astype(jnp.float32)
    grads_in = [None] * N_SECTION
    downs = [None] * N_SECTION
    querys = [None] * N_SECTION
    uppers = [None] * N_SECTION
    for section_index in reversed(range(N_SECTION)):
        d_list = []
        total_down = jnp.zeros((D, LAT), jnp.float32)
        total_qk = jnp.zeros((LAT, LAT), jnp.float32)
        total_up = jnp.zeros((D, LAT), jnp.float32)
        for micro_idx in range(MICRO):
            d_input, g_down, g_qk, g_up_t = layer_backward(kept_all[section_index][micro_idx], upstream_all[micro_idx], gates[section_index, micro_idx], w_down[section_index], w_qk[section_index], w_up[section_index], e_gate[section_index], e_up[section_index], e_down[section_index])
            d_list.append(d_input.astype(jnp.bfloat16))
            total_down = total_down + g_down
            total_qk = total_qk + g_qk
            total_up = total_up + g_up_t
        grads_in[section_index] = jnp.stack(d_list)
        downs[section_index] = total_down
        querys[section_index] = total_qk
        uppers[section_index] = total_up
        upstream_all = grads_in[section_index].astype(jnp.float32)
    return (jnp.stack(activations), jnp.stack(grads_in), jnp.stack(downs), jnp.stack(querys), jnp.stack(uppers))
```

```python
import functools

import jax
import jax.numpy as jnp
from jax import lax
from jax.experimental import pallas as pl
from jax.experimental.pallas import tpu as pltpu
from jax.sharding import PartitionSpec as P

epsilon = 1e-06
WIDTH = 3584
LAT = 256
FF = 256
SEQ = 64
EXPERTS = 32
DP = 4
CAP = 3
NZ = 8
NY = 4
PIECE = 512
PIECES = 7
BLOCK = (8, CAP * PIECE)
PACKED = PIECES * EXPERTS
ORDER = (0, 1, 7, 2, 6, 3, 5, 4)
MESH = pl.DeviceIdType.MESH
VMEM = pl.BlockSpec(memory_space=pltpu.VMEM)
ANY = pl.BlockSpec(memory_space=pl.ANY)
bf16 = jnp.bfloat16
f32 = jnp.float32


def dot(left, right):
    return jnp.dot(left, right, preferred_element_type=f32)


def times_t(left, right):
    return lax.dot_general(left, right, (((1,), (1,)), ((), ())), preferred_element_type=f32)


def t_times(left, right):
    return lax.dot_general(left, right, (((0,), (0,)), ((), ())), preferred_element_type=f32)


def rms_norm(values):
    inv_rms = lax.rsqrt(jnp.mean(values * values, axis=-1, keepdims=True) + epsilon)
    return (values * inv_rms, inv_rms)


def rms_back(normed, inv_rms, upstream):
    return inv_rms * (upstream - normed * jnp.mean(upstream * normed, axis=-1, keepdims=True))


def silu_parts(gate_pre):
    sigmoid = jax.nn.sigmoid(gate_pre)
    return (gate_pre * sigmoid, sigmoid * (1.0 + gate_pre * (1.0 - sigmoid)))


def spread_matrix():
    rows = lax.broadcasted_iota(jnp.int32, (EXPERTS * 8, PACKED), 0)
    cols = lax.broadcasted_iota(jnp.int32, (EXPERTS * 8, PACKED), 1)
    return ((rows % 8) * EXPERTS + rows // 8 == cols).astype(f32).astype(bf16)


def gather_matrix():
    rows = lax.broadcasted_iota(jnp.int32, (PACKED, EXPERTS * 8), 0)
    cols = lax.broadcasted_iota(jnp.int32, (PACKED, EXPERTS * 8), 1)
    return ((cols % 8) * EXPERTS + cols // 8 == rows).astype(f32).astype(bf16)


def slot_rows(route_row):
    experts = lax.broadcasted_iota(jnp.int32, (EXPERTS, SEQ), 0)
    hot = (experts == route_row).astype(f32)
    before = lax.broadcasted_iota(jnp.int32, (SEQ, SEQ), 0) < lax.broadcasted_iota(
        jnp.int32, (SEQ, SEQ), 1
    )
    rank = dot(hot.astype(bf16), before.astype(f32).astype(bf16))
    return jnp.concatenate(
        [(hot * (rank == float(s)).astype(f32)).astype(bf16) for s in range(CAP)], axis=0
    )


def slot_columns(route_col):
    experts = lax.broadcasted_iota(jnp.int32, (SEQ, EXPERTS), 1)
    hot = (experts == route_col).astype(f32)
    before = lax.broadcasted_iota(jnp.int32, (SEQ, SEQ), 0) > lax.broadcasted_iota(
        jnp.int32, (SEQ, SEQ), 1
    )
    rank = dot(before.astype(f32).astype(bf16), hot.astype(bf16))
    return jnp.concatenate(
        [(hot * (rank == float(s)).astype(f32)).astype(bf16) for s in range(CAP)], axis=1
    )


def pack_tokens(values_b, route_row, packed_ref, blocks_ref):
    picked = dot(slot_rows(route_row), values_b).astype(bf16)
    for s in range(CAP):
        for r in range(PIECES):
            packed_ref[r * EXPERTS : (r + 1) * EXPERTS, s * PIECE : (s + 1) * PIECE] = picked[
                s * EXPERTS : (s + 1) * EXPERTS, r * PIECE : (r + 1) * PIECE
            ]
    blocks_ref[...] = dot(spread_matrix(), packed_ref[...]).astype(bf16)


def unpack_tokens(blocks_ref, route_col, token_ref):
    packed = dot(gather_matrix(), blocks_ref[...]).astype(bf16)
    columns = slot_columns(route_col)
    for r in range(PIECES):
        stacked = jnp.concatenate(
            [
                packed[r * EXPERTS : (r + 1) * EXPERTS, s * PIECE : (s + 1) * PIECE]
                for s in range(CAP)
            ],
            axis=0,
        )
        token_ref[:, r * PIECE : (r + 1) * PIECE] = dot(columns, stacked)


def places():
    e = lax.axis_index("expert")
    d = lax.axis_index("dp")
    return e, d, e // NY, e % NY, (d + 1) % DP, (d + DP - 1) % DP, (d + 2) % DP


def meet(e, right, left):
    barrier = pltpu.get_barrier_semaphore()
    for k in range(1, EXPERTS):
        pl.semaphore_signal(
            barrier, inc=1, device_id={"expert": (e + k) % EXPERTS}, device_id_type=MESH
        )
    for side in (right, left):
        pl.semaphore_signal(barrier, inc=1, device_id={"dp": side}, device_id_type=MESH)
    pl.semaphore_wait(barrier, EXPERTS + 1)


def remote(src, dst, send, recv, where):
    return pltpu.make_async_remote_copy(
        src_ref=src, dst_ref=dst, send_sem=send, recv_sem=recv, device_id=where, device_id_type=MESH
    )


def dispatch_kernel(blk, rows, s1, sx, r1, rl, rr, ro):
    e, d, z, y, right, left, opp = places()
    meet(e, right, left)
    for j in ORDER:
        for dy in range(NY):
            if j == 0 and dy == 0:
                pltpu.make_async_copy(blk.at[e], rows.at[d * EXPERTS + e], r1.at[0]).start()
            else:
                peer = ((z + j) % NZ) * NY + (y + dy) % NY
                remote(
                    blk.at[peer],
                    rows.at[d * EXPERTS + e],
                    s1,
                    r1.at[(NZ - j) % NZ],
                    {"expert": peer},
                ).start()

    def group(owner, j):
        return rows.at[pl.ds(owner * EXPERTS + ((z + j) % NZ) * NY, NY)]

    def arrived(ref, sem):
        remote(ref, ref, s1, sem, {"dp": right}).wait_recv()

    def relay(i):
        j = ORDER[i]
        if i % 2 == 0:
            arrived(group(left, j), rl.at[j])
            remote(group(left, j), group(left, j), sx, ro.at[j], {"dp": right}).start()
        else:
            arrived(group(right, j), rr.at[j])
            remote(group(right, j), group(right, j), sx, ro.at[j], {"dp": left}).start()

    for i, j in enumerate(ORDER):
        arrived(group(d, j), r1.at[j])
        remote(group(d, j), group(d, j), sx, rl.at[j], {"dp": right}).start()
        remote(group(d, j), group(d, j), sx, rr.at[j], {"dp": left}).start()
        if i >= 2:
            relay(i - 2)
    relay(NZ - 2)
    relay(NZ - 1)
    for i, j in enumerate(ORDER):
        if i % 2 == 0:
            arrived(group(right, j), rr.at[j])
        else:
            arrived(group(left, j), rl.at[j])
        arrived(group(opp, j), ro.at[j])
    sent = blk.at[pl.ds(0, EXPERTS - 1)]
    remote(sent, sent, s1, r1.at[0], {"dp": right}).wait_send()
    sent = rows.at[pl.ds(0, 3 * EXPERTS)]
    remote(sent, sent, sx, r1.at[0], {"dp": right}).wait_send()


def dispatch(blocks):
    return pl.pallas_call(
        dispatch_kernel,
        name="dispatch",
        out_shape=jax.ShapeDtypeStruct((DP * EXPERTS, *BLOCK), bf16),
        in_specs=[VMEM],
        out_specs=VMEM,
        scratch_shapes=[
            pltpu.SemaphoreType.DMA,
            pltpu.SemaphoreType.DMA,
            pltpu.SemaphoreType.DMA((NZ,)),
            pltpu.SemaphoreType.DMA((NZ,)),
            pltpu.SemaphoreType.DMA((NZ,)),
            pltpu.SemaphoreType.DMA((NZ,)),
        ],
        compiler_params=pltpu.CompilerParams(collective_id=0, has_side_effects=True),
    )(blocks)


def combine_kernel(
    part, out, relayed, relay_sum, from_left, from_right, final, sx, s1, ra, rl, rr, rh
):
    e, d, z, y, right, left, opp = places()
    meet(e, right, left)

    def group(owner, j):
        return part.at[pl.ds(owner * EXPERTS + ((z + j) % NZ) * NY, NY)]

    def spot(ref, i):
        return ref.at[pl.ds(i * NY, NY)]

    def arrived(ref, sem):
        remote(ref, ref, s1, sem, {"dp": right}).wait_recv()

    for i, j in enumerate(ORDER):
        side = right if i % 2 == 0 else left
        remote(group(opp, j), spot(relayed, i), sx, ra.at[i], {"dp": side}).start()
    for i, j in enumerate(ORDER):
        if i % 2 == 0:
            remote(group(left, j), spot(from_right, i), sx, rr.at[i], {"dp": left}).start()
        else:
            remote(group(right, j), spot(from_left, i), sx, rl.at[i], {"dp": right}).start()

    def relay(i):
        j = ORDER[i]
        arrived(spot(relayed, i), ra.at[i])
        side = right if i % 2 == 0 else left
        spot(relay_sum, i)[...] = (
            spot(relayed, i)[...].astype(f32) + group(side, j)[...].astype(f32)
        ).astype(bf16)
        if i % 2 == 0:
            remote(spot(relay_sum, i), spot(from_left, i), sx, rl.at[i], {"dp": right}).start()
        else:
            remote(spot(relay_sum, i), spot(from_right, i), sx, rr.at[i], {"dp": left}).start()

    def finish(i):
        j = ORDER[i]
        arrived(spot(from_left, i), rl.at[i])
        arrived(spot(from_right, i), rr.at[i])
        spot(final, i)[...] = (
            group(d, j)[...].astype(f32)
            + spot(from_left, i)[...].astype(f32)
            + spot(from_right, i)[...].astype(f32)
        ).astype(bf16)
        for dy in range(NY):
            yy = (y + dy) % NY
            if j == 0 and dy == 0:
                pltpu.make_async_copy(final.at[i * NY + yy], out.at[e], rh).start()
            else:
                peer = ((z + j) % NZ) * NY + yy
                remote(final.at[i * NY + yy], out.at[e], s1, rh, {"expert": peer}).start()

    for i in range(NZ):
        relay(i)
    for i in range(NZ):
        finish(i)
    arrived(out, rh)
    sent = part.at[pl.ds(0, 3 * EXPERTS)]
    remote(sent, sent, sx, rh, {"dp": right}).wait_send()
    sent = part.at[pl.ds(0, EXPERTS - 1)]
    remote(sent, sent, s1, rh, {"dp": right}).wait_send()


def combine(partials):
    return pl.pallas_call(
        combine_kernel,
        name="combine",
        out_shape=jax.ShapeDtypeStruct((EXPERTS, *BLOCK), bf16),
        in_specs=[VMEM],
        out_specs=VMEM,
        scratch_shapes=[pltpu.VMEM((EXPERTS, *BLOCK), bf16)] * 5
        + [
            pltpu.SemaphoreType.DMA,
            pltpu.SemaphoreType.DMA,
            pltpu.SemaphoreType.DMA((NZ,)),
            pltpu.SemaphoreType.DMA((NZ,)),
            pltpu.SemaphoreType.DMA((NZ,)),
            pltpu.SemaphoreType.DMA,
        ],
        compiler_params=pltpu.CompilerParams(collective_id=1, has_side_effects=True),
    )(partials)


def fetch(layer, pairs, sems):
    mine = lax.axis_index("section") == layer
    for k, (own, other, dst) in enumerate(pairs):

        @pl.when(mine)
        def _():
            pltpu.make_async_copy(own, dst, sems.at[k]).start()

        @pl.when(jnp.logical_not(mine))
        def _():
            pltpu.make_async_copy(other, dst, sems.at[k]).start()

    def wait(k):
        own, _, dst = pairs[k]
        pltpu.make_async_copy(own, dst, sems.at[k]).wait()

    return wait


def attend(
    inputs, route_row, wd, wq, wu, wait, packed, blocks, residual, latent_o, queries_o, probs_o, mixed_o
):
    normed, _ = rms_norm(inputs.astype(f32))
    wait(0)
    latent = dot(normed.astype(bf16), wd[...]).astype(bf16)
    wait(1)
    queries = dot(latent, wq[...]).astype(bf16)
    scores = times_t(queries, latent) * (LAT ** (-0.5))
    causal = lax.broadcasted_iota(jnp.int32, (SEQ, SEQ), 0) >= lax.broadcasted_iota(
        jnp.int32, (SEQ, SEQ), 1
    )
    scores = jnp.where(causal, scores, -1e30)
    exponent = jnp.exp(scores - jnp.max(scores, axis=-1, keepdims=True))
    probs = exponent / jnp.sum(exponent, axis=-1, keepdims=True)
    mixed = dot(probs.astype(bf16), latent).astype(bf16)
    wait(2)
    resid = (inputs.astype(f32) + dot(mixed, wu[...])).astype(bf16)
    residual[...] = resid
    latent_o[...] = latent
    queries_o[...] = queries
    probs_o[...] = probs
    mixed_o[...] = mixed
    normed2, _ = rms_norm(resid.astype(f32))
    pack_tokens(normed2.astype(bf16), route_row, packed, blocks)


ATTN_SCRATCH = [
    pltpu.VMEM((WIDTH, LAT), bf16),
    pltpu.VMEM((LAT, LAT), bf16),
    pltpu.VMEM((LAT, WIDTH), bf16),
    pltpu.SemaphoreType.DMA((3,)),
]
ATTN_OUT = [
    jax.ShapeDtypeStruct((EXPERTS * 8, BLOCK[1]), bf16),
    jax.ShapeDtypeStruct((SEQ, WIDTH), bf16),
    jax.ShapeDtypeStruct((SEQ, LAT), bf16),
    jax.ShapeDtypeStruct((SEQ, LAT), bf16),
    jax.ShapeDtypeStruct((SEQ, SEQ), f32),
    jax.ShapeDtypeStruct((SEQ, LAT), bf16),
]
PACK_SCRATCH = [pltpu.VMEM((PACKED, BLOCK[1]), bf16)]
TOKEN_SCRATCH = [pltpu.VMEM((SEQ, WIDTH), f32)]


def first_kernel(
    x, route_row, wd0, wq0, wu0, wd1, wq1, wu1, blocks, residual, latent, queries, probs, mixed,
    packed, wd, wq, wu, sems,
):
    wait = fetch(0, ((wd0, wd1, wd), (wq0, wq1, wq), (wu0, wu1, wu)), sems)
    attend(
        x[...], route_row[...], wd, wq, wu, wait, packed, blocks, residual, latent, queries, probs,
        mixed,
    )


def first(x, route_row, attn):
    return pl.pallas_call(
        first_kernel,
        name="first",
        out_shape=ATTN_OUT,
        in_specs=[VMEM] * 2 + [ANY] * 6,
        out_specs=[VMEM] * 6,
        scratch_shapes=PACK_SCRATCH + ATTN_SCRATCH,
    )(x, route_row, *attn)


def second_kernel(
    back, resid_in, gate_col, route_col, route_row, wd0, wq0, wu0, wd1, wq1, wu1,
    act, blocks, residual, latent, queries, probs, mixed, tokens, packed, wd, wq, wu, sems,
):
    wait = fetch(1, ((wd0, wd1, wd), (wq0, wq1, wq), (wu0, wu1, wu)), sems)
    unpack_tokens(back, route_col[...], tokens)
    hidden = (resid_in[...].astype(f32) + gate_col[...] * tokens[...]).astype(bf16)
    act[...] = hidden
    attend(
        hidden, route_row[...], wd, wq, wu, wait, packed, blocks, residual, latent, queries, probs,
        mixed,
    )


def second(back, residual, gate_col, route_col, route_row, attn):
    return pl.pallas_call(
        second_kernel,
        name="second",
        out_shape=[jax.ShapeDtypeStruct((SEQ, WIDTH), bf16)] + ATTN_OUT,
        in_specs=[VMEM] * 5 + [ANY] * 6,
        out_specs=[VMEM] * 7,
        scratch_shapes=TOKEN_SCRATCH + PACK_SCRATCH + ATTN_SCRATCH,
    )(back, residual, gate_col, route_col, route_row, *attn)


def third_kernel(
    back, resid_in, gate_col, route_col, route_row, upstream, act, blocks, tokens, packed
):
    scaled = (gate_col[...] * upstream[...].astype(f32)).astype(bf16)
    pack_tokens(scaled, route_row[...], packed, blocks)
    unpack_tokens(back, route_col[...], tokens)
    act[...] = (resid_in[...].astype(f32) + gate_col[...] * tokens[...]).astype(bf16)


def third(back, residual, gate_col, route_col, route_row, upstream):
    return pl.pallas_call(
        third_kernel,
        name="third",
        out_shape=[jax.ShapeDtypeStruct((SEQ, WIDTH), bf16), ATTN_OUT[0]],
        in_specs=[VMEM] * 6,
        out_specs=[VMEM] * 2,
        scratch_shapes=TOKEN_SCRATCH + PACK_SCRATCH,
    )(back, residual, gate_col, route_col, route_row, upstream)


def back_kernel(
    layer, last, back, resid_in, inputs, upstream, route_col, gate_col, route_row, latent_i,
    queries_i, probs_i, mixed_i, wd0, wq0, wu0, wd1, wq1, wu1, *rest,
):
    if last:
        grad, normed_o, d_latent_o, d_queries_o, d_resid_o, tokens, wd, wq, wu, sems = rest
    else:
        grad, normed_o, d_latent_o, d_queries_o, d_resid_o, blocks, tokens, packed, wd, wq, wu, sems = rest
    wait = fetch(layer, ((wd0, wd1, wd), (wq0, wq1, wq), (wu0, wu1, wu)), sems)
    unpack_tokens(back, route_col[...], tokens)
    normed2, inv2 = rms_norm(resid_in[...].astype(f32))
    d_resid = upstream[...].astype(f32) + rms_back(normed2, inv2, tokens[...])
    d_resid_b = d_resid.astype(bf16)
    d_resid_o[...] = d_resid_b
    tokens[...] = d_resid
    latent, probs = latent_i[...], probs_i[...]
    wait(2)
    d_mixed = times_t(d_resid_b, wu[...]).astype(bf16)
    d_probs = times_t(d_mixed, latent)
    d_scores = (
        probs * (d_probs - jnp.sum(d_probs * probs, axis=-1, keepdims=True)) * (LAT ** (-0.5))
    ).astype(bf16)
    d_queries = dot(d_scores, latent).astype(bf16)
    wait(1)
    d_latent = (
        t_times(probs.astype(bf16), d_mixed)
        + t_times(d_scores, queries_i[...])
        + times_t(d_queries, wq[...])
    ).astype(bf16)
    wait(0)
    d_normed = times_t(d_latent, wd[...])
    normed, inv = rms_norm(inputs[...].astype(f32))
    normed_o[...] = normed.astype(bf16)
    d_latent_o[...] = d_latent
    d_queries_o[...] = d_queries
    d_input = (tokens[...] + rms_back(normed, inv, d_normed)).astype(bf16)
    grad[...] = d_input
    if not last:
        scaled = (gate_col[...] * d_input.astype(f32)).astype(bf16)
        pack_tokens(scaled, route_row[...], packed, blocks)


def backward(layer, back, residual, inputs, upstream, route_col, gate_col, route_row, kept, attn):
    last = layer == 0
    outs = [
        jax.ShapeDtypeStruct((SEQ, WIDTH), bf16),
        jax.ShapeDtypeStruct((SEQ, WIDTH), bf16),
        jax.ShapeDtypeStruct((SEQ, LAT), bf16),
        jax.ShapeDtypeStruct((SEQ, LAT), bf16),
        jax.ShapeDtypeStruct((SEQ, WIDTH), bf16),
    ] + ([] if last else [ATTN_OUT[0]])
    return pl.pallas_call(
        functools.partial(back_kernel, layer, last),
        name=f"backward{layer}",
        out_shape=outs,
        in_specs=[VMEM] * 11 + [ANY] * 6,
        out_specs=[VMEM] * len(outs),
        scratch_shapes=TOKEN_SCRATCH + ([] if last else PACK_SCRATCH) + ATTN_SCRATCH,
    )(back, residual, inputs, upstream, route_col, gate_col, route_row, *kept, *attn)


def unpack_rows(rows, wide):
    gather = gather_matrix()

    @pl.loop(0, DP)
    def _(g):
        start = pl.multiple_of(g * EXPERTS * 8, EXPERTS * 8)
        packed = dot(gather, rows[pl.ds(start, EXPERTS * 8), :]).astype(bf16)
        for s in range(CAP):
            at = pl.multiple_of(g * EXPERTS + s * DP * EXPERTS, EXPERTS)
            for r in range(PIECES):
                wide[pl.ds(at, EXPERTS), r * PIECE : (r + 1) * PIECE] = packed[
                    r * EXPERTS : (r + 1) * EXPERTS, s * PIECE : (s + 1) * PIECE
                ]


def pack_rows(wide, packed, out):
    spread = spread_matrix()

    @pl.loop(0, DP)
    def _(g):
        for s in range(CAP):
            at = pl.multiple_of(g * EXPERTS + s * DP * EXPERTS, EXPERTS)
            for r in range(PIECES):
                packed[r * EXPERTS : (r + 1) * EXPERTS, s * PIECE : (s + 1) * PIECE] = wide[
                    pl.ds(at, EXPERTS), r * PIECE : (r + 1) * PIECE
                ]
        start = pl.multiple_of(g * EXPERTS * 8, EXPERTS * 8)
        out[pl.ds(start, EXPERTS * 8), :] = dot(spread, packed[...]).astype(bf16)


def expert_forward_kernel(
    layer, rows, gw0, uw0, dw0, gw1, uw1, dw1, part, gate_o, up_o, wide, packed, gw, uw, dw, sems
):
    wait = fetch(layer, ((gw0, gw1, gw), (uw0, uw1, uw), (dw0, dw1, dw)), sems)
    unpack_rows(rows, wide)
    wait(0)
    gate_o[...] = dot(wide[...], gw[...])
    wait(1)
    up_o[...] = dot(wide[...], uw[...])
    hidden = (silu_parts(gate_o[...])[0] * up_o[...]).astype(bf16)
    wait(2)
    for c in range(PIECES):
        wide[:, c * PIECE : (c + 1) * PIECE] = dot(
            hidden, dw[:, c * PIECE : (c + 1) * PIECE]
        ).astype(bf16)
    pack_rows(wide, packed, part)


def expert_backward_kernel(
    layer, rows, gate_i, up_i, gw0, uw0, dw0, gw1, uw1, dw1, part, wide, packed, gw, uw, dw, sems
):
    wait = fetch(layer, ((gw0, gw1, gw), (uw0, uw1, uw), (dw0, dw1, dw)), sems)
    unpack_rows(rows, wide)
    wait(2)
    d_hidden = times_t(wide[...], dw[...])
    activated, slope = silu_parts(gate_i[...])
    d_gate = (d_hidden * up_i[...] * slope).astype(bf16)
    d_up = (d_hidden * activated).astype(bf16)
    wait(0)
    wait(1)
    for c in range(PIECES):
        wide[:, c * PIECE : (c + 1) * PIECE] = (
            times_t(d_gate, gw[c * PIECE : (c + 1) * PIECE, :])
            + times_t(d_up, uw[c * PIECE : (c + 1) * PIECE, :])
        ).astype(bf16)
    pack_rows(wide, packed, part)


EXPERT_SCRATCH = [
    pltpu.VMEM((CAP * DP * EXPERTS, WIDTH), bf16),
    pltpu.VMEM((PACKED, BLOCK[1]), bf16),
    pltpu.VMEM((WIDTH, FF), bf16),
    pltpu.VMEM((WIDTH, FF), bf16),
    pltpu.VMEM((FF, WIDTH), bf16),
    pltpu.SemaphoreType.DMA((3,)),
]
PARTS = jax.ShapeDtypeStruct((DP * EXPERTS * 8, BLOCK[1]), bf16)
PRE = jax.ShapeDtypeStruct((CAP * DP * EXPERTS, FF), f32)


def expert_forward(layer, rows, experts):
    return pl.pallas_call(
        functools.partial(expert_forward_kernel, layer),
        name=f"expert_forward{layer}",
        out_shape=[PARTS, PRE, PRE],
        in_specs=[VMEM] + [ANY] * 6,
        out_specs=[VMEM] * 3,
        scratch_shapes=EXPERT_SCRATCH,
    )(rows, *experts)


def expert_backward(layer, rows, gate_pre, up_pre, experts):
    return pl.pallas_call(
        functools.partial(expert_backward_kernel, layer),
        name=f"expert_backward{layer}",
        out_shape=PARTS,
        in_specs=[VMEM] * 3 + [ANY] * 6,
        out_specs=VMEM,
        scratch_shapes=EXPERT_SCRATCH,
    )(rows, gate_pre, up_pre, *experts)


def flat(blocks):
    return blocks.reshape(-1, BLOCK[1])


def blocked(rows):
    return rows.reshape(-1, *BLOCK)


def swap(value):
    return lax.ppermute(value, "section", [(0, 1), (1, 0)])


def spaced(values, per):
    rows, width = values.shape
    wide = (per + 7) // 8 * 8
    return jnp.pad(values.reshape(rows, width // per, per), ((0, 0), (0, 0), (0, wide - per))).reshape(
        rows, width // per * wide
    )


def body(x_in, dy_out, routes, gates, w_down, w_qk, w_up, e_gate, e_up, e_down):
    section = lax.axis_index("section")
    attn_own = (w_down[0], w_qk[0], w_up[0])
    experts_own = (e_gate[0, 0], e_up[0, 0], e_down[0, 0])
    attn = attn_own + tuple(swap(w) for w in attn_own)
    experts = experts_own + tuple(swap(w) for w in experts_own)
    x = lax.dynamic_index_in_dim(x_in[:, 0], section, 0, keepdims=False)
    dy = lax.dynamic_index_in_dim(dy_out[:, 0], section, 0, keepdims=False)

    def both_layers(table):
        other = swap(lax.dynamic_index_in_dim(table, 1 - section, 0, keepdims=False))
        own = lax.dynamic_index_in_dim(table, section, 0, keepdims=False)
        return (jnp.where(section == 0, own, other), jnp.where(section == 0, other, own))

    route_cols = both_layers(routes[0, :, 0])
    gate_cols = both_layers(gates[0, :, 0])
    route_rows = tuple(r.reshape(1, SEQ) for r in route_cols)

    blocks, resid0, *kept0 = first(x, route_rows[0], attn)
    rows = flat(dispatch(blocked(blocks)))
    parts, gate0, up0 = expert_forward(0, rows, experts)
    back = flat(combine(blocked(parts)))
    act0, blocks, resid1, *kept1 = second(
        back, resid0, gate_cols[0], route_cols[0], route_rows[1], attn
    )
    rows = flat(dispatch(blocked(blocks)))
    parts, gate1, up1 = expert_forward(1, rows, experts)
    back = flat(combine(blocked(parts)))
    act1, blocks = third(back, resid1, gate_cols[1], route_cols[1], route_rows[1], dy)
    rows = flat(dispatch(blocked(blocks)))
    parts = expert_backward(1, rows, gate1, up1, experts)
    back = flat(combine(blocked(parts)))
    grad1, n1, dl1, dq1, dr1, blocks = backward(
        1, back, resid1, act0, dy, route_cols[1], gate_cols[0], route_rows[0], kept1, attn
    )
    rows = flat(dispatch(blocked(blocks)))
    parts = expert_backward(0, rows, gate0, up0, experts)
    back = flat(combine(blocked(parts)))
    grad0, n0, dl0, dq0, dr0 = backward(
        0, back, resid0, x, grad1, route_cols[0], gate_cols[0], route_rows[0], kept0, attn
    )
    layer0 = (n0, dl0, kept0[0], dq0, dr0, kept0[3], act0, grad0)
    layer1 = (n1, dl1, kept1[0], dq1, dr1, kept1[3], act1, grad1)
    own = [jnp.where(section == 0, a, b) for a, b in zip(layer0, layer1)]
    other = [swap(jnp.where(section == 0, b, a)) for a, b in zip(layer0, layer1)]
    n1b, d_latent, latent, d_queries, d_resid, mixed = (
        jnp.concatenate([a, b], axis=0) for a, b in zip(own[:6], other[:6])
    )

    def in_order(a, b):
        return jnp.stack([jnp.where(section == 0, a, b), jnp.where(section == 0, b, a)])[
            None, :, None
        ]

    activations = in_order(own[6], other[6])
    grads_in = in_order(own[7], other[7])

    def scattered(left, right, per):
        total = t_times(spaced(left, per), right)
        mine = lax.psum_scatter(total, ("expert", "dp"), scatter_dimension=0, tiled=True)
        return mine[None, :per]

    g_down = scattered(n1b, d_latent, 28)
    g_qk = scattered(latent, d_queries, 2)
    g_up_t = scattered(d_resid, mixed, 28)
    return (activations, grads_in, g_down, g_qk, g_up_t)


def solution(mesh):
    placed = (
        P(None, ("expert", "dp"), None, None),
        P(None, ("expert", "dp"), None, None),
        P("section", None, ("expert", "dp"), None, None),
        P("section", None, ("expert", "dp"), None, None),
        P("section", None, None),
        P("section", None, None),
        P("section", None, None),
        P("section", "expert", None, "dp"),
        P("section", "expert", None, "dp"),
        P("section", "expert", "dp", None),
    )
    return jax.shard_map(
        body,
        mesh=mesh,
        in_specs=placed,
        out_specs=(
            P("section", None, ("expert", "dp"), None, None),
            P("section", None, ("expert", "dp"), None, None),
            P("section", ("expert", "dp"), None),
            P("section", ("expert", "dp"), None),
            P("section", ("expert", "dp"), None),
        ),
        check_vma=False,
    )
```

```python
import functools

import jax
import jax.numpy as jnp
from jax import lax
from jax.experimental import pallas as pl
from jax.experimental.pallas import tpu as pltpu
from jax.sharding import PartitionSpec as P

epsilon = 1e-06
WIDTH = 3584
LAT = 256
FF = 256
SEQ = 64
EXPERTS = 32
DP = 4
CAP = 3
NZ = 8
NY = 4
PIECE = 512
PIECES = 7
BLOCK = (8, CAP * PIECE)
PACKED = PIECES * EXPERTS
ORDER = (0, 1, 7, 2, 6, 3, 5, 4)
MESH = pl.DeviceIdType.MESH
VMEM = pl.BlockSpec(memory_space=pltpu.VMEM)
ANY = pl.BlockSpec(memory_space=pl.ANY)
bf16 = jnp.bfloat16
f32 = jnp.float32


def dot(left, right):
    return jnp.dot(left, right, preferred_element_type=f32)


def times_t(left, right):
    return lax.dot_general(left, right, (((1,), (1,)), ((), ())), preferred_element_type=f32)


def t_times(left, right):
    return lax.dot_general(left, right, (((0,), (0,)), ((), ())), preferred_element_type=f32)


def rms_norm(values):
    inv_rms = lax.rsqrt(jnp.mean(values * values, axis=-1, keepdims=True) + epsilon)
    return (values * inv_rms, inv_rms)


def rms_back(normed, inv_rms, upstream):
    return inv_rms * (upstream - normed * jnp.mean(upstream * normed, axis=-1, keepdims=True))


def silu_parts(gate_pre):
    sigmoid = jax.nn.sigmoid(gate_pre)
    return (gate_pre * sigmoid, sigmoid * (1.0 + gate_pre * (1.0 - sigmoid)))


def spread_matrix():
    rows = lax.broadcasted_iota(jnp.int32, (EXPERTS * 8, PACKED), 0)
    cols = lax.broadcasted_iota(jnp.int32, (EXPERTS * 8, PACKED), 1)
    return ((rows % 8) * EXPERTS + rows // 8 == cols).astype(f32).astype(bf16)


def gather_matrix():
    rows = lax.broadcasted_iota(jnp.int32, (PACKED, EXPERTS * 8), 0)
    cols = lax.broadcasted_iota(jnp.int32, (PACKED, EXPERTS * 8), 1)
    return ((cols % 8) * EXPERTS + cols // 8 == rows).astype(f32).astype(bf16)


def slot_rows(route_row):
    experts = lax.broadcasted_iota(jnp.int32, (EXPERTS, SEQ), 0)
    hot = (experts == route_row).astype(f32)
    before = lax.broadcasted_iota(jnp.int32, (SEQ, SEQ), 0) < lax.broadcasted_iota(
        jnp.int32, (SEQ, SEQ), 1
    )
    rank = dot(hot.astype(bf16), before.astype(f32).astype(bf16))
    return jnp.concatenate(
        [(hot * (rank == float(s)).astype(f32)).astype(bf16) for s in range(CAP)], axis=0
    )


def slot_columns(route_col):
    experts = lax.broadcasted_iota(jnp.int32, (SEQ, EXPERTS), 1)
    hot = (experts == route_col).astype(f32)
    before = lax.broadcasted_iota(jnp.int32, (SEQ, SEQ), 0) > lax.broadcasted_iota(
        jnp.int32, (SEQ, SEQ), 1
    )
    rank = dot(before.astype(f32).astype(bf16), hot.astype(bf16))
    return jnp.concatenate(
        [(hot * (rank == float(s)).astype(f32)).astype(bf16) for s in range(CAP)], axis=1
    )


def pack_tokens(values_b, route_row, packed_ref, blocks_ref):
    picked = dot(slot_rows(route_row), values_b).astype(bf16)
    for s in range(CAP):
        for r in range(PIECES):
            packed_ref[r * EXPERTS : (r + 1) * EXPERTS, s * PIECE : (s + 1) * PIECE] = picked[
                s * EXPERTS : (s + 1) * EXPERTS, r * PIECE : (r + 1) * PIECE
            ]
    blocks_ref[...] = dot(spread_matrix(), packed_ref[...]).astype(bf16)


def unpack_tokens(blocks_ref, route_col, token_ref):
    packed = dot(gather_matrix(), blocks_ref[...]).astype(bf16)
    columns = slot_columns(route_col)
    for r in range(PIECES):
        stacked = jnp.concatenate(
            [
                packed[r * EXPERTS : (r + 1) * EXPERTS, s * PIECE : (s + 1) * PIECE]
                for s in range(CAP)
            ],
            axis=0,
        )
        token_ref[:, r * PIECE : (r + 1) * PIECE] = dot(columns, stacked)


def places():
    e = lax.axis_index("expert")
    d = lax.axis_index("dp")
    return e, d, e // NY, e % NY, (d + 1) % DP, (d + DP - 1) % DP, (d + 2) % DP


def meet(e, right, left):
    barrier = pltpu.get_barrier_semaphore()
    for k in range(1, EXPERTS):
        pl.semaphore_signal(
            barrier, inc=1, device_id={"expert": (e + k) % EXPERTS}, device_id_type=MESH
        )
    for side in (right, left):
        pl.semaphore_signal(barrier, inc=1, device_id={"dp": side}, device_id_type=MESH)
    pl.semaphore_wait(barrier, EXPERTS + 1)


def remote(src, dst, send, recv, where):
    return pltpu.make_async_remote_copy(
        src_ref=src, dst_ref=dst, send_sem=send, recv_sem=recv, device_id=where, device_id_type=MESH
    )


def dispatch_kernel(blk, rows, s1, sx, r1, rl, rr, ro):
    e, d, z, y, right, left, opp = places()
    meet(e, right, left)
    for j in ORDER:
        for dy in range(NY):
            if j == 0 and dy == 0:
                pltpu.make_async_copy(blk.at[e], rows.at[d * EXPERTS + e], r1.at[0]).start()
            else:
                peer = ((z + j) % NZ) * NY + (y + dy) % NY
                remote(
                    blk.at[peer],
                    rows.at[d * EXPERTS + e],
                    s1,
                    r1.at[(NZ - j) % NZ],
                    {"expert": peer},
                ).start()

    def group(owner, j):
        return rows.at[pl.ds(owner * EXPERTS + ((z + j) % NZ) * NY, NY)]

    def arrived(ref, sem):
        remote(ref, ref, s1, sem, {"dp": right}).wait_recv()

    def relay(i):
        j = ORDER[i]
        if i % 2 == 0:
            arrived(group(left, j), rl.at[j])
            remote(group(left, j), group(left, j), sx, ro.at[j], {"dp": right}).start()
        else:
            arrived(group(right, j), rr.at[j])
            remote(group(right, j), group(right, j), sx, ro.at[j], {"dp": left}).start()

    for i, j in enumerate(ORDER):
        arrived(group(d, j), r1.at[j])
        remote(group(d, j), group(d, j), sx, rl.at[j], {"dp": right}).start()
        remote(group(d, j), group(d, j), sx, rr.at[j], {"dp": left}).start()
        if i >= 2:
            relay(i - 2)
    relay(NZ - 2)
    relay(NZ - 1)
    for i, j in enumerate(ORDER):
        if i % 2 == 0:
            arrived(group(right, j), rr.at[j])
        else:
            arrived(group(left, j), rl.at[j])
        arrived(group(opp, j), ro.at[j])
    sent = blk.at[pl.ds(0, EXPERTS - 1)]
    remote(sent, sent, s1, r1.at[0], {"dp": right}).wait_send()
    sent = rows.at[pl.ds(0, 3 * EXPERTS)]
    remote(sent, sent, sx, r1.at[0], {"dp": right}).wait_send()


def dispatch(blocks):
    return pl.pallas_call(
        dispatch_kernel,
        name="dispatch",
        out_shape=jax.ShapeDtypeStruct((DP * EXPERTS, *BLOCK), bf16),
        in_specs=[VMEM],
        out_specs=VMEM,
        scratch_shapes=[
            pltpu.SemaphoreType.DMA,
            pltpu.SemaphoreType.DMA,
            pltpu.SemaphoreType.DMA((NZ,)),
            pltpu.SemaphoreType.DMA((NZ,)),
            pltpu.SemaphoreType.DMA((NZ,)),
            pltpu.SemaphoreType.DMA((NZ,)),
        ],
        compiler_params=pltpu.CompilerParams(collective_id=0, has_side_effects=True),
    )(blocks)


def combine_kernel(
    part, out, relayed, relay_sum, from_left, from_right, final, sx, s1, ra, rl, rr, rh
):
    e, d, z, y, right, left, opp = places()
    meet(e, right, left)

    def group(owner, j):
        return part.at[pl.ds(owner * EXPERTS + ((z + j) % NZ) * NY, NY)]

    def spot(ref, i):
        return ref.at[pl.ds(i * NY, NY)]

    def arrived(ref, sem):
        remote(ref, ref, s1, sem, {"dp": right}).wait_recv()

    for i, j in enumerate(ORDER):
        side = right if i % 2 == 0 else left
        remote(group(opp, j), spot(relayed, i), sx, ra.at[i], {"dp": side}).start()
    for i, j in enumerate(ORDER):
        if i % 2 == 0:
            remote(group(left, j), spot(from_right, i), sx, rr.at[i], {"dp": left}).start()
        else:
            remote(group(right, j), spot(from_left, i), sx, rl.at[i], {"dp": right}).start()

    def relay(i):
        j = ORDER[i]
        arrived(spot(relayed, i), ra.at[i])
        side = right if i % 2 == 0 else left
        spot(relay_sum, i)[...] = (
            spot(relayed, i)[...].astype(f32) + group(side, j)[...].astype(f32)
        ).astype(bf16)
        if i % 2 == 0:
            remote(spot(relay_sum, i), spot(from_left, i), sx, rl.at[i], {"dp": right}).start()
        else:
            remote(spot(relay_sum, i), spot(from_right, i), sx, rr.at[i], {"dp": left}).start()

    def finish(i):
        j = ORDER[i]
        arrived(spot(from_left, i), rl.at[i])
        arrived(spot(from_right, i), rr.at[i])
        spot(final, i)[...] = (
            group(d, j)[...].astype(f32)
            + spot(from_left, i)[...].astype(f32)
            + spot(from_right, i)[...].astype(f32)
        ).astype(bf16)
        for dy in range(NY):
            yy = (y + dy) % NY
            if j == 0 and dy == 0:
                pltpu.make_async_copy(final.at[i * NY + yy], out.at[e], rh).start()
            else:
                peer = ((z + j) % NZ) * NY + yy
                remote(final.at[i * NY + yy], out.at[e], s1, rh, {"expert": peer}).start()

    for i in range(NZ):
        relay(i)
    for i in range(NZ):
        finish(i)
    arrived(out, rh)
    sent = part.at[pl.ds(0, 3 * EXPERTS)]
    remote(sent, sent, sx, rh, {"dp": right}).wait_send()
    sent = part.at[pl.ds(0, EXPERTS - 1)]
    remote(sent, sent, s1, rh, {"dp": right}).wait_send()


def combine(partials):
    return pl.pallas_call(
        combine_kernel,
        name="combine",
        out_shape=jax.ShapeDtypeStruct((EXPERTS, *BLOCK), bf16),
        in_specs=[VMEM],
        out_specs=VMEM,
        scratch_shapes=[pltpu.VMEM((EXPERTS, *BLOCK), bf16)] * 5
        + [
            pltpu.SemaphoreType.DMA,
            pltpu.SemaphoreType.DMA,
            pltpu.SemaphoreType.DMA((NZ,)),
            pltpu.SemaphoreType.DMA((NZ,)),
            pltpu.SemaphoreType.DMA((NZ,)),
            pltpu.SemaphoreType.DMA,
        ],
        compiler_params=pltpu.CompilerParams(collective_id=1, has_side_effects=True),
    )(partials)


def fetch(layer, pairs, sems):
    mine = lax.axis_index("section") == layer
    for k, (own, other, dst) in enumerate(pairs):

        @pl.when(mine)
        def _():
            pltpu.make_async_copy(own, dst, sems.at[k]).start()

        @pl.when(jnp.logical_not(mine))
        def _():
            pltpu.make_async_copy(other, dst, sems.at[k]).start()

    def wait(k):
        own, _, dst = pairs[k]
        pltpu.make_async_copy(own, dst, sems.at[k]).wait()

    return wait


def attend(
    inputs, route_row, wd, wq, wu, wait, packed, blocks, residual, latent_o, queries_o, probs_o, mixed_o
):
    normed, _ = rms_norm(inputs.astype(f32))
    wait(0)
    latent = dot(normed.astype(bf16), wd[...]).astype(bf16)
    wait(1)
    queries = dot(latent, wq[...]).astype(bf16)
    scores = times_t(queries, latent) * (LAT ** (-0.5))
    causal = lax.broadcasted_iota(jnp.int32, (SEQ, SEQ), 0) >= lax.broadcasted_iota(
        jnp.int32, (SEQ, SEQ), 1
    )
    scores = jnp.where(causal, scores, -1e30)
    exponent = jnp.exp(scores - jnp.max(scores, axis=-1, keepdims=True))
    probs = exponent / jnp.sum(exponent, axis=-1, keepdims=True)
    mixed = dot(probs.astype(bf16), latent).astype(bf16)
    wait(2)
    resid = (inputs.astype(f32) + dot(mixed, wu[...])).astype(bf16)
    residual[...] = resid
    latent_o[...] = latent
    queries_o[...] = queries
    probs_o[...] = probs
    mixed_o[...] = mixed
    normed2, _ = rms_norm(resid.astype(f32))
    pack_tokens(normed2.astype(bf16), route_row, packed, blocks)


ATTN_SCRATCH = [
    pltpu.VMEM((WIDTH, LAT), bf16),
    pltpu.VMEM((LAT, LAT), bf16),
    pltpu.VMEM((LAT, WIDTH), bf16),
    pltpu.SemaphoreType.DMA((3,)),
]
ATTN_OUT = [
    jax.ShapeDtypeStruct((EXPERTS * 8, BLOCK[1]), bf16),
    jax.ShapeDtypeStruct((SEQ, WIDTH), bf16),
    jax.ShapeDtypeStruct((SEQ, LAT), bf16),
    jax.ShapeDtypeStruct((SEQ, LAT), bf16),
    jax.ShapeDtypeStruct((SEQ, SEQ), f32),
    jax.ShapeDtypeStruct((SEQ, LAT), bf16),
]
PACK_SCRATCH = [pltpu.VMEM((PACKED, BLOCK[1]), bf16)]
TOKEN_SCRATCH = [pltpu.VMEM((SEQ, WIDTH), f32)]


def first_kernel(
    x, route_row, wd0, wq0, wu0, wd1, wq1, wu1, blocks, residual, latent, queries, probs, mixed,
    packed, wd, wq, wu, sems,
):
    wait = fetch(0, ((wd0, wd1, wd), (wq0, wq1, wq), (wu0, wu1, wu)), sems)
    attend(
        x[...], route_row[...], wd, wq, wu, wait, packed, blocks, residual, latent, queries, probs,
        mixed,
    )


def first(x, route_row, attn):
    return pl.pallas_call(
        first_kernel,
        name="first",
        out_shape=ATTN_OUT,
        in_specs=[VMEM] * 2 + [ANY] * 6,
        out_specs=[VMEM] * 6,
        scratch_shapes=PACK_SCRATCH + ATTN_SCRATCH,
    )(x, route_row, *attn)


def second_kernel(
    back, resid_in, gate_col, route_col, route_row, wd0, wq0, wu0, wd1, wq1, wu1,
    act, blocks, residual, latent, queries, probs, mixed, tokens, packed, wd, wq, wu, sems,
):
    wait = fetch(1, ((wd0, wd1, wd), (wq0, wq1, wq), (wu0, wu1, wu)), sems)
    unpack_tokens(back, route_col[...], tokens)
    hidden = (resid_in[...].astype(f32) + gate_col[...] * tokens[...]).astype(bf16)
    act[...] = hidden
    attend(
        hidden, route_row[...], wd, wq, wu, wait, packed, blocks, residual, latent, queries, probs,
        mixed,
    )


def second(back, residual, gate_col, route_col, route_row, attn):
    return pl.pallas_call(
        second_kernel,
        name="second",
        out_shape=[jax.ShapeDtypeStruct((SEQ, WIDTH), bf16)] + ATTN_OUT,
        in_specs=[VMEM] * 5 + [ANY] * 6,
        out_specs=[VMEM] * 7,
        scratch_shapes=TOKEN_SCRATCH + PACK_SCRATCH + ATTN_SCRATCH,
    )(back, residual, gate_col, route_col, route_row, *attn)


def third_kernel(
    back, resid_in, gate_col, route_col, route_row, upstream, act, blocks, tokens, packed
):
    scaled = (gate_col[...] * upstream[...].astype(f32)).astype(bf16)
    pack_tokens(scaled, route_row[...], packed, blocks)
    unpack_tokens(back, route_col[...], tokens)
    act[...] = (resid_in[...].astype(f32) + gate_col[...] * tokens[...]).astype(bf16)


def third(back, residual, gate_col, route_col, route_row, upstream):
    return pl.pallas_call(
        third_kernel,
        name="third",
        out_shape=[jax.ShapeDtypeStruct((SEQ, WIDTH), bf16), ATTN_OUT[0]],
        in_specs=[VMEM] * 6,
        out_specs=[VMEM] * 2,
        scratch_shapes=TOKEN_SCRATCH + PACK_SCRATCH,
    )(back, residual, gate_col, route_col, route_row, upstream)


def back_kernel(
    layer, last, back, resid_in, inputs, upstream, route_col, gate_col, route_row, latent_i,
    queries_i, probs_i, mixed_i, wd0, wq0, wu0, wd1, wq1, wu1, *rest,
):
    if last:
        grad, normed_o, d_latent_o, d_queries_o, d_resid_o, tokens, wd, wq, wu, sems = rest
    else:
        grad, normed_o, d_latent_o, d_queries_o, d_resid_o, blocks, tokens, packed, wd, wq, wu, sems = rest
    wait = fetch(layer, ((wd0, wd1, wd), (wq0, wq1, wq), (wu0, wu1, wu)), sems)
    unpack_tokens(back, route_col[...], tokens)
    normed2, inv2 = rms_norm(resid_in[...].astype(f32))
    d_resid = upstream[...].astype(f32) + rms_back(normed2, inv2, tokens[...])
    d_resid_b = d_resid.astype(bf16)
    d_resid_o[...] = d_resid_b
    tokens[...] = d_resid
    latent, probs = latent_i[...], probs_i[...]
    wait(2)
    d_mixed = times_t(d_resid_b, wu[...]).astype(bf16)
    d_probs = times_t(d_mixed, latent)
    d_scores = (
        probs * (d_probs - jnp.sum(d_probs * probs, axis=-1, keepdims=True)) * (LAT ** (-0.5))
    ).astype(bf16)
    d_queries = dot(d_scores, latent).astype(bf16)
    wait(1)
    d_latent = (
        t_times(probs.astype(bf16), d_mixed)
        + t_times(d_scores, queries_i[...])
        + times_t(d_queries, wq[...])
    ).astype(bf16)
    wait(0)
    d_normed = times_t(d_latent, wd[...])
    normed, inv = rms_norm(inputs[...].astype(f32))
    normed_o[...] = normed.astype(bf16)
    d_latent_o[...] = d_latent
    d_queries_o[...] = d_queries
    d_input = (tokens[...] + rms_back(normed, inv, d_normed)).astype(bf16)
    grad[...] = d_input
    if not last:
        scaled = (gate_col[...] * d_input.astype(f32)).astype(bf16)
        pack_tokens(scaled, route_row[...], packed, blocks)


def backward(layer, back, residual, inputs, upstream, route_col, gate_col, route_row, kept, attn):
    last = layer == 0
    outs = [
        jax.ShapeDtypeStruct((SEQ, WIDTH), bf16),
        jax.ShapeDtypeStruct((SEQ, WIDTH), bf16),
        jax.ShapeDtypeStruct((SEQ, LAT), bf16),
        jax.ShapeDtypeStruct((SEQ, LAT), bf16),
        jax.ShapeDtypeStruct((SEQ, WIDTH), bf16),
    ] + ([] if last else [ATTN_OUT[0]])
    return pl.pallas_call(
        functools.partial(back_kernel, layer, last),
        name=f"backward{layer}",
        out_shape=outs,
        in_specs=[VMEM] * 11 + [ANY] * 6,
        out_specs=[VMEM] * len(outs),
        scratch_shapes=TOKEN_SCRATCH + ([] if last else PACK_SCRATCH) + ATTN_SCRATCH,
    )(back, residual, inputs, upstream, route_col, gate_col, route_row, *kept, *attn)


def unpack_rows(rows, wide):
    gather = gather_matrix()

    @pl.loop(0, DP)
    def _(g):
        start = pl.multiple_of(g * EXPERTS * 8, EXPERTS * 8)
        packed = dot(gather, rows[pl.ds(start, EXPERTS * 8), :]).astype(bf16)
        for s in range(CAP):
            at = pl.multiple_of(g * EXPERTS + s * DP * EXPERTS, EXPERTS)
            for r in range(PIECES):
                wide[pl.ds(at, EXPERTS), r * PIECE : (r + 1) * PIECE] = packed[
                    r * EXPERTS : (r + 1) * EXPERTS, s * PIECE : (s + 1) * PIECE
                ]


def pack_rows(wide, packed, out):
    spread = spread_matrix()

    @pl.loop(0, DP)
    def _(g):
        for s in range(CAP):
            at = pl.multiple_of(g * EXPERTS + s * DP * EXPERTS, EXPERTS)
            for r in range(PIECES):
                packed[r * EXPERTS : (r + 1) * EXPERTS, s * PIECE : (s + 1) * PIECE] = wide[
                    pl.ds(at, EXPERTS), r * PIECE : (r + 1) * PIECE
                ]
        start = pl.multiple_of(g * EXPERTS * 8, EXPERTS * 8)
        out[pl.ds(start, EXPERTS * 8), :] = dot(spread, packed[...]).astype(bf16)


def expert_forward_kernel(
    layer, rows, gw0, uw0, dw0, gw1, uw1, dw1, part, gate_o, up_o, wide, packed, gw, uw, dw, sems
):
    wait = fetch(layer, ((gw0, gw1, gw), (uw0, uw1, uw), (dw0, dw1, dw)), sems)
    unpack_rows(rows, wide)
    wait(0)
    gate_o[...] = dot(wide[...], gw[...])
    wait(1)
    up_o[...] = dot(wide[...], uw[...])
    hidden = (silu_parts(gate_o[...])[0] * up_o[...]).astype(bf16)
    wait(2)
    for c in range(PIECES):
        wide[:, c * PIECE : (c + 1) * PIECE] = dot(
            hidden, dw[:, c * PIECE : (c + 1) * PIECE]
        ).astype(bf16)
    pack_rows(wide, packed, part)


def expert_backward_kernel(
    layer, rows, gate_i, up_i, gw0, uw0, dw0, gw1, uw1, dw1, part, wide, packed, gw, uw, dw, sems
):
    wait = fetch(layer, ((gw0, gw1, gw), (uw0, uw1, uw), (dw0, dw1, dw)), sems)
    unpack_rows(rows, wide)
    wait(2)
    d_hidden = times_t(wide[...], dw[...])
    activated, slope = silu_parts(gate_i[...])
    d_gate = (d_hidden * up_i[...] * slope).astype(bf16)
    d_up = (d_hidden * activated).astype(bf16)
    wait(0)
    wait(1)
    for c in range(PIECES):
        wide[:, c * PIECE : (c + 1) * PIECE] = (
            times_t(d_gate, gw[c * PIECE : (c + 1) * PIECE, :])
            + times_t(d_up, uw[c * PIECE : (c + 1) * PIECE, :])
        ).astype(bf16)
    pack_rows(wide, packed, part)


EXPERT_SCRATCH = [
    pltpu.VMEM((CAP * DP * EXPERTS, WIDTH), bf16),
    pltpu.VMEM((PACKED, BLOCK[1]), bf16),
    pltpu.VMEM((WIDTH, FF), bf16),
    pltpu.VMEM((WIDTH, FF), bf16),
    pltpu.VMEM((FF, WIDTH), bf16),
    pltpu.SemaphoreType.DMA((3,)),
]
PARTS = jax.ShapeDtypeStruct((DP * EXPERTS * 8, BLOCK[1]), bf16)
PRE = jax.ShapeDtypeStruct((CAP * DP * EXPERTS, FF), f32)


def expert_forward(layer, rows, experts):
    return pl.pallas_call(
        functools.partial(expert_forward_kernel, layer),
        name=f"expert_forward{layer}",
        out_shape=[PARTS, PRE, PRE],
        in_specs=[VMEM] + [ANY] * 6,
        out_specs=[VMEM] * 3,
        scratch_shapes=EXPERT_SCRATCH,
    )(rows, *experts)


def expert_backward(layer, rows, gate_pre, up_pre, experts):
    return pl.pallas_call(
        functools.partial(expert_backward_kernel, layer),
        name=f"expert_backward{layer}",
        out_shape=PARTS,
        in_specs=[VMEM] * 3 + [ANY] * 6,
        out_specs=VMEM,
        scratch_shapes=EXPERT_SCRATCH,
    )(rows, gate_pre, up_pre, *experts)


def flat(blocks):
    return blocks.reshape(-1, BLOCK[1])


def blocked(rows):
    return rows.reshape(-1, *BLOCK)


def swap(value):
    return lax.ppermute(value, "section", [(0, 1), (1, 0)])


ROUND = 1792
SIDE = 1280


def quarter_matrix(first_is_dp):
    out = lax.broadcasted_iota(jnp.int32, (1, 1024), 1)
    one, two, zz, i = out // 256, (out // 64) % 4, (out // 32) % 2, out % 32
    y, x = (two, one) if first_is_dp else (one, two)
    source = jnp.where(i < 28, zz * 448 + y * 112 + x * 28 + i, -1)
    return (lax.broadcasted_iota(jnp.int32, (896, 1024), 0) == source).astype(f32).astype(bf16)


def small_matrix():
    out = lax.broadcasted_iota(jnp.int32, (1, 1024), 1)
    x, y, z, i = out // 256, (out // 64) % 4, (out // 8) % 8, out % 8
    source = jnp.where(i < 2, z * 32 + y * 8 + x * 2 + i, -1)
    return (lax.broadcasted_iota(jnp.int32, (LAT, 1024), 0) == source).astype(f32).astype(bf16)


def lay_out(factor, matrix, sent, layer):
    stacked = jnp.concatenate([factor[:, c * 896 : (c + 1) * 896] for c in range(4)], axis=0)
    moved = dot(stacked, matrix).astype(bf16)
    for q in range(4):
        for c in range(4):
            sent[layer, q, :, c * 256 : (c + 1) * 256] = moved[
                c * SEQ : (c + 1) * SEQ, q * 256 : (q + 1) * 256
            ]


class Ring:
    def __init__(self, section, position, near, sent, got, relay, ssem, fsem, rsem):
        self.section, self.position, self.near = section, position, near
        self.sent, self.got, self.relay_buf = sent, got, relay
        self.ssem, self.fsem, self.rsem = ssem, fsem, rsem

    def start(self, layer):
        pos, s = self.position, self.section
        way = 1 if layer == 0 else 3
        remote(
            self.sent.at[layer, (pos + 2) % 4],
            self.relay_buf.at[layer],
            self.ssem,
            self.rsem.at[layer],
            self.near(way),
        ).start()
        for step, back in ((1, 1), (3, 0)):
            remote(
                self.sent.at[layer, (pos + step) % 4],
                self.got.at[s, pos],
                self.ssem,
                self.fsem.at[s, back],
                {**self.near(step), "section": layer},
            ).start()

    def own(self):
        pos, s = self.position, self.section
        pltpu.make_async_copy(self.sent.at[s, pos], self.got.at[s, pos], self.fsem.at[s, 3]).start()
        remote(
            self.sent.at[1 - s, pos],
            self.got.at[s, pos],
            self.ssem,
            self.fsem.at[s, 3],
            {"section": 1 - s},
        ).start()

    def relay(self):
        for layer, way in ((0, 1), (1, 3)):
            buf = self.relay_buf.at[layer]
            remote(buf, buf, self.ssem, self.rsem.at[layer], self.near(1)).wait_recv()
            origin = (self.position + 4 - way) % 4
            remote(
                buf,
                self.got.at[self.section, origin],
                self.ssem,
                self.fsem.at[self.section, 2],
                {**self.near(way), "section": layer},
            ).start()

    def arrive(self):
        for m in range(2):
            for k, step in enumerate((1, 3, 2, 0)):
                ref = self.got.at[m, (self.position + step) % 4]
                remote(ref, ref, self.ssem, self.fsem.at[m, k], self.near(1)).wait_recv()

    def drain(self):
        for layer in range(2):
            ref = self.sent.at[layer]
            remote(ref, ref, self.ssem, self.rsem.at[0], self.near(1)).wait_send()
        ref = self.sent.at[0, 0]
        remote(ref, ref, self.ssem, self.rsem.at[0], self.near(1)).wait_send()


def fold(pieces):
    total = pieces[0].astype(f32)
    for piece in pieces[1:]:
        total = total + piece.astype(f32)
    return total


def grads_kernel(
    n0, dl0, la0, dq0, dr0, mx0, act0, grad0, n1, dl1, la1, dq1, dr1, mx1, act1, grad1,
    act_o, grad_o, down_o, qk_o, up_o,
    xs, xg, xr, ys, yg, yr, td, sd, zd, zr, tu, su, zu, zv,
    xssem, xfsem, xrsem, yssem, yfsem, yrsem, psem, qsem, asem, dsem, dr, usem, ur, zsem, zrecv,
):
    s = lax.axis_index("section")
    e, d, z, y, right, left, opp = places()

    def near_x(k):
        return {"dp": (d + k) % 4}

    def near_y(k):
        return {"expert": z * NY + (y + k) % 4}

    def near_z(k):
        return {"expert": ((z + k) % NZ) * NY + y}

    barrier = pltpu.get_barrier_semaphore()
    peers = [{"section": 1 - s}]
    for near in (near_x, near_y):
        for k in (1, 3):
            peers += [{**near(k), "section": 0}, {**near(k), "section": 1}]
        peers.append(near(2))
    peers += [near_z(k) for k in range(1, NZ)]
    for peer in peers:
        pl.semaphore_signal(barrier, inc=1, device_id=peer, device_id_type=MESH)
    x_ring = Ring(s, d, near_x, xs, xg, xr, xssem, xfsem, xrsem)
    y_ring = Ring(s, y, near_y, ys, yg, yr, yssem, yfsem, yrsem)
    factors = ((n0, dl0, la0, dq0, dr0, mx0), (n1, dl1, la1, dq1, dr1, mx1))
    by_x, by_y, small = quarter_matrix(True), quarter_matrix(False), small_matrix()
    for layer, (n, dl, la, dq, _, _) in enumerate(factors):
        lay_out(n[...], by_x, xs, layer)
        moved = dot(la[...], small).astype(bf16)
        for q in range(4):
            xs[layer, q, :, 1024:1280] = dl[...]
            xs[layer, q, :, 1280:1536] = moved[:, q * 256 : (q + 1) * 256]
            xs[layer, q, :, 1536:1792] = dq[...]
    pl.semaphore_wait(barrier, len(peers))
    x_ring.start(0)
    x_ring.start(1)
    for layer, (_, _, _, _, dres, mx) in enumerate(factors):
        lay_out(dres[...], by_y, ys, layer)
        for q in range(4):
            ys[layer, q, :, 1024:1280] = mx[...]
    y_ring.start(0)
    y_ring.start(1)
    x_ring.own()
    y_ring.own()

    for k, (out, first_layer, second_layer) in enumerate(((act_o, act0, act1), (grad_o, grad0, grad1))):
        for here, keep, give in ((0, first_layer, second_layer), (1, second_layer, first_layer)):

            @pl.when(s == here)
            def _():
                pltpu.make_async_copy(keep, out.at[s], asem.at[k]).start()
                remote(give, out.at[s], psem, qsem.at[k], {"section": 1 - s}).start()

    x_ring.relay()
    y_ring.relay()

    def rows(ring, start, width):
        got = ring.got
        return jnp.concatenate(
            [got[m, q, :, start : start + width] for m in range(2) for q in range(4)], axis=0
        )

    x_ring.arrive()
    total = t_times(rows(x_ring, 0, 1024), rows(x_ring, 1024, 256)).astype(bf16)
    total_qk = t_times(rows(x_ring, 1280, 256), rows(x_ring, 1536, 256)).astype(bf16)
    for q in range(4):
        for c in range(4):
            td[q, c * 64 : (c + 1) * 64, :] = total[c * 256 + q * 64 : c * 256 + (q + 1) * 64]
        td[q, 256:320, :] = total_qk[q * 64 : (q + 1) * 64]
    for k in (2, 1, 3):
        remote(td.at[(y + k) % 4], sd.at[y], dsem, dr.at[4 - k - 1], near_y(k)).start()
    y_ring.arrive()
    total = t_times(rows(y_ring, 0, 1024), rows(y_ring, 1024, 256)).astype(bf16)
    for q in range(4):
        for c in range(4):
            tu[q, c * 64 : (c + 1) * 64, :] = total[c * 256 + q * 64 : c * 256 + (q + 1) * 64]
    for k in (2, 1, 3):
        remote(tu.at[(d + k) % 4], su.at[d], usem, ur.at[4 - k - 1], near_x(k)).start()

    def gathered(buf, recv, position):
        for k in (1, 2, 3):
            ref = buf.at[(position + k) % 4]
            remote(ref, ref, dsem, recv.at[k - 1], near_x(1)).wait_recv()
        return [buf[(position + k) % 4] for k in (1, 2, 3)]

    summed = fold([td[y]] + gathered(sd, dr, y)).astype(bf16)
    for k in range(NZ):
        zd[k, 0:32, :] = summed[k * 32 : (k + 1) * 32]
        zd[k, 32:40, :] = summed[256 + k * 8 : 264 + k * 8]
    for k in range(1, NZ):
        remote(zd.at[(z + k) % NZ], zr.at[z], zsem.at[0], zrecv.at[0, NZ - k - 1], near_z(k)).start()
    summed = fold([tu[d]] + gathered(su, ur, d)).astype(bf16)
    for k in range(NZ):
        zu[k] = summed[k * 32 : (k + 1) * 32]
    for k in range(1, NZ):
        remote(zu.at[(z + k) % NZ], zv.at[z], zsem.at[1], zrecv.at[1, NZ - k - 1], near_z(k)).start()

    def last(own, buf, which):
        for k in range(1, NZ):
            ref = buf.at[(z + k) % NZ]
            remote(ref, ref, zsem.at[0], zrecv.at[which, k - 1], near_z(1)).wait_recv()
        return fold([own[z]] + [buf[(z + k) % NZ] for k in range(1, NZ)])

    mine = last(zd, zr, 0)
    down_o[...] = mine[0:28]
    qk_o[...] = mine[32:34]
    mine = last(zu, zv, 1)
    up_o[...] = mine[0:28]

    x_ring.drain()
    y_ring.drain()
    for k, (out, some) in enumerate(((act_o, act0), (grad_o, grad0))):
        pltpu.make_async_copy(some, out.at[s], asem.at[k]).wait()
        remote(some, out.at[1 - s], psem, qsem.at[k], {"section": 1 - s}).wait_recv()
    whole = act_o
    remote(whole, whole, psem, qsem.at[0], {"section": 1 - s}).wait_send()
    ref = td.at[pl.ds(0, 3)]
    remote(ref, ref, dsem, dr.at[0], near_x(1)).wait_send()
    ref = tu.at[pl.ds(0, 3)]
    remote(ref, ref, usem, ur.at[0], near_x(1)).wait_send()
    ref = zd.at[pl.ds(0, NZ - 1)]
    remote(ref, ref, zsem.at[0], dr.at[0], near_x(1)).wait_send()
    ref = zu.at[pl.ds(0, NZ - 1)]
    remote(ref, ref, zsem.at[1], dr.at[0], near_x(1)).wait_send()


def weight_grads(layer0, layer1):
    dma = pltpu.SemaphoreType.DMA
    ring_sems = [dma, dma((2, 4)), dma((2,))]
    return pl.pallas_call(
        grads_kernel,
        name="weight_grads",
        out_shape=[
            jax.ShapeDtypeStruct((2, SEQ, WIDTH), bf16),
            jax.ShapeDtypeStruct((2, SEQ, WIDTH), bf16),
            jax.ShapeDtypeStruct((28, LAT), f32),
            jax.ShapeDtypeStruct((2, LAT), f32),
            jax.ShapeDtypeStruct((28, LAT), f32),
        ],
        in_specs=[VMEM] * 16,
        out_specs=[VMEM] * 5,
        scratch_shapes=[
            pltpu.VMEM((2, 4, SEQ, ROUND), bf16),
            pltpu.VMEM((2, 4, SEQ, ROUND), bf16),
            pltpu.VMEM((2, SEQ, ROUND), bf16),
            pltpu.VMEM((2, 4, SEQ, SIDE), bf16),
            pltpu.VMEM((2, 4, SEQ, SIDE), bf16),
            pltpu.VMEM((2, SEQ, SIDE), bf16),
            pltpu.VMEM((4, 320, LAT), bf16),
            pltpu.VMEM((4, 320, LAT), bf16),
            pltpu.VMEM((NZ, 40, LAT), bf16),
            pltpu.VMEM((NZ, 40, LAT), bf16),
            pltpu.VMEM((4, 256, LAT), bf16),
            pltpu.VMEM((4, 256, LAT), bf16),
            pltpu.VMEM((NZ, 32, LAT), bf16),
            pltpu.VMEM((NZ, 32, LAT), bf16),
        ]
        + ring_sems * 2
        + [dma, dma((2,)), dma((2,)), dma, dma((3,)), dma, dma((3,)), dma((2,)), dma((2, NZ - 1))],
        compiler_params=pltpu.CompilerParams(collective_id=2, has_side_effects=True),
    )(*layer0, *layer1)


def body(x_in, dy_out, routes, gates, w_down, w_qk, w_up, e_gate, e_up, e_down):
    section = lax.axis_index("section")
    attn_own = (w_down[0], w_qk[0], w_up[0])
    experts_own = (e_gate[0, 0], e_up[0, 0], e_down[0, 0])
    attn = attn_own + tuple(swap(w) for w in attn_own)
    experts = experts_own + tuple(swap(w) for w in experts_own)
    x = lax.dynamic_index_in_dim(x_in[:, 0], section, 0, keepdims=False)
    dy = lax.dynamic_index_in_dim(dy_out[:, 0], section, 0, keepdims=False)

    def both_layers(table):
        other = swap(lax.dynamic_index_in_dim(table, 1 - section, 0, keepdims=False))
        own = lax.dynamic_index_in_dim(table, section, 0, keepdims=False)
        return (jnp.where(section == 0, own, other), jnp.where(section == 0, other, own))

    route_cols = both_layers(routes[0, :, 0])
    gate_cols = both_layers(gates[0, :, 0])
    route_rows = tuple(r.reshape(1, SEQ) for r in route_cols)

    blocks, resid0, *kept0 = first(x, route_rows[0], attn)
    rows = flat(dispatch(blocked(blocks)))
    parts, gate0, up0 = expert_forward(0, rows, experts)
    back = flat(combine(blocked(parts)))
    act0, blocks, resid1, *kept1 = second(
        back, resid0, gate_cols[0], route_cols[0], route_rows[1], attn
    )
    rows = flat(dispatch(blocked(blocks)))
    parts, gate1, up1 = expert_forward(1, rows, experts)
    back = flat(combine(blocked(parts)))
    act1, blocks = third(back, resid1, gate_cols[1], route_cols[1], route_rows[1], dy)
    rows = flat(dispatch(blocked(blocks)))
    parts = expert_backward(1, rows, gate1, up1, experts)
    back = flat(combine(blocked(parts)))
    grad1, n1, dl1, dq1, dr1, blocks = backward(
        1, back, resid1, act0, dy, route_cols[1], gate_cols[0], route_rows[0], kept1, attn
    )
    rows = flat(dispatch(blocked(blocks)))
    parts = expert_backward(0, rows, gate0, up0, experts)
    back = flat(combine(blocked(parts)))
    grad0, n0, dl0, dq0, dr0 = backward(
        0, back, resid0, x, grad1, route_cols[0], gate_cols[0], route_rows[0], kept0, attn
    )
    layer0 = (n0, dl0, kept0[0], dq0, dr0, kept0[3], act0, grad0)
    layer1 = (n1, dl1, kept1[0], dq1, dr1, kept1[3], act1, grad1)
    activations, grads_in, g_down, g_qk, g_up_t = weight_grads(layer0, layer1)
    return (
        activations[None, :, None],
        grads_in[None, :, None],
        g_down[None],
        g_qk[None],
        g_up_t[None],
    )


def solution(mesh):
    placed = (
        P(None, ("expert", "dp"), None, None),
        P(None, ("expert", "dp"), None, None),
        P("section", None, ("expert", "dp"), None, None),
        P("section", None, ("expert", "dp"), None, None),
        P("section", None, None),
        P("section", None, None),
        P("section", None, None),
        P("section", "expert", None, "dp"),
        P("section", "expert", None, "dp"),
        P("section", "expert", "dp", None),
    )
    return jax.shard_map(
        body,
        mesh=mesh,
        in_specs=placed,
        out_specs=(
            P("section", None, ("expert", "dp"), None, None),
            P("section", None, ("expert", "dp"), None, None),
            P("section", ("expert", "dp"), None),
            P("section", ("expert", "dp"), None),
            P("section", ("expert", "dp"), None),
        ),
        check_vma=False,
    )
```

```python
import functools

import jax
import jax.numpy as jnp
from jax import lax
from jax.experimental import pallas as pl
from jax.experimental.pallas import tpu as pltpu
from jax.sharding import PartitionSpec as P

epsilon = 1e-06
WIDTH = 3584
LAT = 256
FF = 256
SEQ = 64
EXPERTS = 32
DP = 4
CAP = 3
NZ = 8
NY = 4
PIECE = 512
PIECES = 7
BLOCK = (8, CAP * PIECE)
PACKED = PIECES * EXPERTS
ORDER = (0, 1, 7, 2, 6, 3, 5, 4)
MESH = pl.DeviceIdType.MESH
VMEM = pl.BlockSpec(memory_space=pltpu.VMEM)
ANY = pl.BlockSpec(memory_space=pl.ANY)
bf16 = jnp.bfloat16
f32 = jnp.float32


def dot(left, right):
    return jnp.dot(left, right, preferred_element_type=f32)


def times_t(left, right):
    return lax.dot_general(left, right, (((1,), (1,)), ((), ())), preferred_element_type=f32)


def t_times(left, right):
    return lax.dot_general(left, right, (((0,), (0,)), ((), ())), preferred_element_type=f32)


def rms_norm(values):
    inv_rms = lax.rsqrt(jnp.mean(values * values, axis=-1, keepdims=True) + epsilon)
    return (values * inv_rms, inv_rms)


def rms_back(normed, inv_rms, upstream):
    return inv_rms * (upstream - normed * jnp.mean(upstream * normed, axis=-1, keepdims=True))


def silu_parts(gate_pre):
    sigmoid = jax.nn.sigmoid(gate_pre)
    return (gate_pre * sigmoid, sigmoid * (1.0 + gate_pre * (1.0 - sigmoid)))


def spread_matrix():
    rows = lax.broadcasted_iota(jnp.int32, (EXPERTS * 8, PACKED), 0)
    cols = lax.broadcasted_iota(jnp.int32, (EXPERTS * 8, PACKED), 1)
    return ((rows % 8) * EXPERTS + rows // 8 == cols).astype(f32).astype(bf16)


def gather_matrix():
    rows = lax.broadcasted_iota(jnp.int32, (PACKED, EXPERTS * 8), 0)
    cols = lax.broadcasted_iota(jnp.int32, (PACKED, EXPERTS * 8), 1)
    return ((cols % 8) * EXPERTS + cols // 8 == rows).astype(f32).astype(bf16)


def slot_rows(route_row):
    experts = lax.broadcasted_iota(jnp.int32, (EXPERTS, SEQ), 0)
    hot = (experts == route_row).astype(f32)
    before = lax.broadcasted_iota(jnp.int32, (SEQ, SEQ), 0) < lax.broadcasted_iota(
        jnp.int32, (SEQ, SEQ), 1
    )
    rank = dot(hot.astype(bf16), before.astype(f32).astype(bf16))
    return jnp.concatenate(
        [(hot * (rank == float(s)).astype(f32)).astype(bf16) for s in range(CAP)], axis=0
    )


def slot_columns(route_col):
    experts = lax.broadcasted_iota(jnp.int32, (SEQ, EXPERTS), 1)
    hot = (experts == route_col).astype(f32)
    before = lax.broadcasted_iota(jnp.int32, (SEQ, SEQ), 0) > lax.broadcasted_iota(
        jnp.int32, (SEQ, SEQ), 1
    )
    rank = dot(before.astype(f32).astype(bf16), hot.astype(bf16))
    return jnp.concatenate(
        [(hot * (rank == float(s)).astype(f32)).astype(bf16) for s in range(CAP)], axis=1
    )


def pack_tokens(values_b, route_row, packed_ref, blocks_ref):
    picked = dot(slot_rows(route_row), values_b).astype(bf16)
    for s in range(CAP):
        for r in range(PIECES):
            packed_ref[r * EXPERTS : (r + 1) * EXPERTS, s * PIECE : (s + 1) * PIECE] = picked[
                s * EXPERTS : (s + 1) * EXPERTS, r * PIECE : (r + 1) * PIECE
            ]
    blocks_ref[...] = dot(spread_matrix(), packed_ref[...]).astype(bf16).reshape(HOME)


def unpack_tokens(blocks_ref, route_col, token_ref):
    packed = dot(gather_matrix(), blocks_ref[...].reshape(EXPERTS * 8, BLOCK[1])).astype(bf16)
    columns = slot_columns(route_col)
    for r in range(PIECES):
        stacked = jnp.concatenate(
            [
                packed[r * EXPERTS : (r + 1) * EXPERTS, s * PIECE : (s + 1) * PIECE]
                for s in range(CAP)
            ],
            axis=0,
        )
        token_ref[:, r * PIECE : (r + 1) * PIECE] = dot(columns, stacked)


def places():
    e = lax.axis_index("expert")
    d = lax.axis_index("dp")
    return e, d, e // NY, e % NY, (d + 1) % DP, (d + DP - 1) % DP, (d + 2) % DP


def greet(e, right, left):
    barrier = pltpu.get_barrier_semaphore()
    for k in range(1, EXPERTS):
        pl.semaphore_signal(
            barrier, inc=1, device_id={"expert": (e + k) % EXPERTS}, device_id_type=MESH
        )
    for side in (right, left):
        pl.semaphore_signal(barrier, inc=1, device_id={"dp": side}, device_id_type=MESH)


def greeted():
    pl.semaphore_wait(pltpu.get_barrier_semaphore(), EXPERTS + 1)


def remote(src, dst, send, recv, where):
    return pltpu.make_async_remote_copy(
        src_ref=src, dst_ref=dst, send_sem=send, recv_sem=recv, device_id=where, device_id_type=MESH
    )


class Dispatch:
    sems = (
        pltpu.SemaphoreType.DMA,
        pltpu.SemaphoreType.DMA,
        pltpu.SemaphoreType.DMA((NZ,)),
        pltpu.SemaphoreType.DMA((NZ,)),
        pltpu.SemaphoreType.DMA((NZ,)),
        pltpu.SemaphoreType.DMA((NZ,)),
    )

    def __init__(self, blk, rows, sems):
        self.blk, self.rows = blk, rows
        self.s1, self.sx, self.r1, self.rl, self.rr, self.ro = sems
        self.e, self.d, self.z, self.y, self.right, self.left, self.opp = places()

    def start(self):
        for j in ORDER:
            for dy in range(NY):
                spot = self.rows.at[self.d * EXPERTS + self.e]
                if j == 0 and dy == 0:
                    pltpu.make_async_copy(self.blk.at[self.e], spot, self.r1.at[0]).start()
                else:
                    peer = ((self.z + j) % NZ) * NY + (self.y + dy) % NY
                    remote(
                        self.blk.at[peer], spot, self.s1, self.r1.at[(NZ - j) % NZ], {"expert": peer}
                    ).start()

    def group(self, owner, j):
        return self.rows.at[pl.ds(owner * EXPERTS + ((self.z + j) % NZ) * NY, NY)]

    def arrived(self, ref, sem):
        remote(ref, ref, self.s1, sem, {"dp": self.right}).wait_recv()

    def forward(self, i):
        j = ORDER[i]
        mine = self.group(self.d, j)
        self.arrived(mine, self.r1.at[j])
        remote(mine, mine, self.sx, self.rl.at[j], {"dp": self.right}).start()
        remote(mine, mine, self.sx, self.rr.at[j], {"dp": self.left}).start()

    def relay(self, i):
        j = ORDER[i]
        owner, sem, to = (
            (self.left, self.rl, self.right) if i % 2 == 0 else (self.right, self.rr, self.left)
        )
        ref = self.group(owner, j)
        self.arrived(ref, sem.at[j])
        remote(ref, ref, self.sx, self.ro.at[j], {"dp": to}).start()

    def rest(self, use):
        use(self.d)
        for i, j in enumerate(ORDER):
            if i % 2 == 0:
                self.arrived(self.group(self.right, j), self.rr.at[j])
        use(self.right)
        for i, j in enumerate(ORDER):
            if i % 2 == 1:
                self.arrived(self.group(self.left, j), self.rl.at[j])
        use(self.left)
        for j in ORDER:
            self.arrived(self.group(self.opp, j), self.ro.at[j])
        use(self.opp)

    def drain(self):
        sent = self.blk.at[pl.ds(0, EXPERTS - 1)]
        remote(sent, sent, self.s1, self.r1.at[0], {"dp": self.right}).wait_send()
        sent = self.rows.at[pl.ds(0, 3 * EXPERTS)]
        remote(sent, sent, self.sx, self.r1.at[0], {"dp": self.right}).wait_send()


class Combine:
    sems = (
        pltpu.SemaphoreType.DMA,
        pltpu.SemaphoreType.DMA,
        pltpu.SemaphoreType.DMA((NZ,)),
        pltpu.SemaphoreType.DMA((NZ,)),
        pltpu.SemaphoreType.DMA((NZ,)),
        pltpu.SemaphoreType.DMA,
    )
    buffers = (pltpu.VMEM((EXPERTS, *BLOCK), bf16),) * 5

    def __init__(self, part, out, buffers, sems):
        self.part, self.out = part, out
        self.relayed, self.relay_sum, self.from_left, self.from_right, self.final = buffers
        self.sx, self.s1, self.ra, self.rl, self.rr, self.rh = sems
        self.e, self.d, self.z, self.y, self.right, self.left, self.opp = places()

    def group(self, owner, j):
        return self.part.at[pl.ds(owner * EXPERTS + ((self.z + j) % NZ) * NY, NY)]

    def spot(self, ref, i):
        return ref.at[pl.ds(i * NY, NY)]

    def arrived(self, ref, sem):
        remote(ref, ref, self.s1, sem, {"dp": self.right}).wait_recv()

    def start_far(self):
        for i, j in enumerate(ORDER):
            side = self.right if i % 2 == 0 else self.left
            remote(
                self.group(self.opp, j), self.spot(self.relayed, i), self.sx, self.ra.at[i], {"dp": side}
            ).start()

    def start_near(self):
        for i, j in enumerate(ORDER):
            if i % 2 == 0:
                ref, to, sem, side = self.left, self.from_right, self.rr, self.left
            else:
                ref, to, sem, side = self.right, self.from_left, self.rl, self.right
            remote(self.group(ref, j), self.spot(to, i), self.sx, sem.at[i], {"dp": side}).start()

    def relay(self, i):
        j = ORDER[i]
        self.arrived(self.spot(self.relayed, i), self.ra.at[i])
        side, to, sem = (
            (self.right, self.from_left, self.rl)
            if i % 2 == 0
            else (self.left, self.from_right, self.rr)
        )
        self.spot(self.relay_sum, i)[...] = (
            self.spot(self.relayed, i)[...].astype(f32) + self.group(side, j)[...].astype(f32)
        ).astype(bf16)
        remote(
            self.spot(self.relay_sum, i), self.spot(to, i), self.sx, sem.at[i], {"dp": side}
        ).start()

    def finish(self, i):
        j = ORDER[i]
        self.arrived(self.spot(self.from_left, i), self.rl.at[i])
        self.arrived(self.spot(self.from_right, i), self.rr.at[i])
        self.spot(self.final, i)[...] = (
            self.group(self.d, j)[...].astype(f32)
            + self.spot(self.from_left, i)[...].astype(f32)
            + self.spot(self.from_right, i)[...].astype(f32)
        ).astype(bf16)
        for dy in range(NY):
            yy = (self.y + dy) % NY
            spot = self.out.at[self.e]
            if j == 0 and dy == 0:
                pltpu.make_async_copy(self.final.at[i * NY + yy], spot, self.rh).start()
            else:
                peer = ((self.z + j) % NZ) * NY + yy
                remote(
                    self.final.at[i * NY + yy], spot, self.s1, self.rh, {"expert": peer}
                ).start()

    def arrive(self):
        self.arrived(self.out, self.rh)

    def drain(self):
        sent = self.part.at[pl.ds(0, 3 * EXPERTS)]
        remote(sent, sent, self.sx, self.rh, {"dp": self.right}).wait_send()
        sent = self.part.at[pl.ds(0, EXPERTS - 1)]
        remote(sent, sent, self.s1, self.rh, {"dp": self.right}).wait_send()


def fetch(layer, pairs, sems):
    mine = lax.axis_index("section") == layer
    for k, (own, other, dst) in enumerate(pairs):

        @pl.when(mine)
        def _():
            pltpu.make_async_copy(own, dst, sems.at[k]).start()

        @pl.when(jnp.logical_not(mine))
        def _():
            pltpu.make_async_copy(other, dst, sems.at[k]).start()

    def wait(k):
        own, _, dst = pairs[k]
        pltpu.make_async_copy(own, dst, sems.at[k]).wait()

    return wait


def attend(
    inputs, route_row, wd, wq, wu, wait, packed, blocks, residual, latent_o, queries_o, probs_o, mixed_o
):
    normed, _ = rms_norm(inputs.astype(f32))
    wait(0)
    latent = dot(normed.astype(bf16), wd[...]).astype(bf16)
    wait(1)
    queries = dot(latent, wq[...]).astype(bf16)
    scores = times_t(queries, latent) * (LAT ** (-0.5))
    causal = lax.broadcasted_iota(jnp.int32, (SEQ, SEQ), 0) >= lax.broadcasted_iota(
        jnp.int32, (SEQ, SEQ), 1
    )
    scores = jnp.where(causal, scores, -1e30)
    exponent = jnp.exp(scores - jnp.max(scores, axis=-1, keepdims=True))
    probs = exponent / jnp.sum(exponent, axis=-1, keepdims=True)
    mixed = dot(probs.astype(bf16), latent).astype(bf16)
    wait(2)
    resid = (inputs.astype(f32) + dot(mixed, wu[...])).astype(bf16)
    residual[...] = resid
    latent_o[...] = latent
    queries_o[...] = queries
    probs_o[...] = probs
    mixed_o[...] = mixed
    normed2, _ = rms_norm(resid.astype(f32))
    pack_tokens(normed2.astype(bf16), route_row, packed, blocks)


def attend_back(
    upstream, inputs, resid, latent, queries, probs, mixed, w, wait, tokens, normed_o, d_latent_o,
    d_queries_o, d_resid_o, grad,
):
    normed2, inv2 = rms_norm(resid.astype(f32))
    d_resid = upstream.astype(f32) + rms_back(normed2, inv2, tokens[...])
    d_resid_b = d_resid.astype(bf16)
    d_resid_o[...] = d_resid_b
    tokens[...] = d_resid
    wd, wq, wu = w
    wait(2)
    d_mixed = times_t(d_resid_b, wu[...]).astype(bf16)
    d_probs = times_t(d_mixed, latent)
    d_scores = (
        probs * (d_probs - jnp.sum(d_probs * probs, axis=-1, keepdims=True)) * (LAT ** (-0.5))
    ).astype(bf16)
    d_queries = dot(d_scores, latent).astype(bf16)
    wait(1)
    d_latent = (
        t_times(probs.astype(bf16), d_mixed)
        + t_times(d_scores, queries)
        + times_t(d_queries, wq[...])
    ).astype(bf16)
    wait(0)
    d_normed = times_t(d_latent, wd[...])
    normed, inv = rms_norm(inputs.astype(f32))
    normed_o[...] = normed.astype(bf16)
    d_latent_o[...] = d_latent
    d_queries_o[...] = d_queries
    grad[...] = (tokens[...] + rms_back(normed, inv, d_normed)).astype(bf16)


def unpack_rows(rows, wide, g):
    packed = dot(
        gather_matrix(), rows[pl.ds(g * EXPERTS, EXPERTS)].reshape(EXPERTS * 8, BLOCK[1])
    ).astype(bf16)
    for s in range(CAP):
        at = pl.multiple_of(g * EXPERTS + s * DP * EXPERTS, EXPERTS)
        for r in range(PIECES):
            wide[pl.ds(at, EXPERTS), r * PIECE : (r + 1) * PIECE] = packed[
                r * EXPERTS : (r + 1) * EXPERTS, s * PIECE : (s + 1) * PIECE
            ]


def pack_rows(wide, packed, out, g):
    for s in range(CAP):
        at = pl.multiple_of(g * EXPERTS + s * DP * EXPERTS, EXPERTS)
        for r in range(PIECES):
            packed[r * EXPERTS : (r + 1) * EXPERTS, s * PIECE : (s + 1) * PIECE] = wide[
                pl.ds(at, EXPERTS), r * PIECE : (r + 1) * PIECE
            ]
    out[pl.ds(g * EXPERTS, EXPERTS)] = (
        dot(spread_matrix(), packed[...]).astype(bf16).reshape(EXPERTS, *BLOCK)
    )


def send_back(combine, wide, packed):
    pack_rows(wide, packed, combine.part, combine.opp)
    combine.start_far()
    pack_rows(wide, packed, combine.part, combine.left)
    pack_rows(wide, packed, combine.part, combine.right)
    combine.start_near()
    pack_rows(wide, packed, combine.part, combine.d)


def expert_out(hidden, dw, wide):
    for c in range(PIECES):
        cols = slice(c * PIECE, (c + 1) * PIECE)
        wide[:, cols] = dot(hidden, dw[:, cols]).astype(bf16)


def expert_back(wide, gate_pre, up_pre, gw, uw, dw):
    d_hidden = times_t(wide[...], dw[...])
    activated, slope = silu_parts(gate_pre)
    d_gate = (d_hidden * up_pre * slope).astype(bf16)
    d_up = (d_hidden * activated).astype(bf16)
    for c in range(PIECES):
        cols = slice(c * PIECE, (c + 1) * PIECE)
        wide[:, cols] = (times_t(d_gate, gw[cols, :]) + times_t(d_up, uw[cols, :])).astype(bf16)


class Refs:
    def __init__(self, names, refs):
        for name, ref in zip(names, refs, strict=True):
            setattr(self, name, ref)

    def some(self, prefix, count):
        return tuple(getattr(self, f"{prefix}{k}") for k in range(count))


def named(prefix, items):
    return {f"{prefix}{k}": item for k, item in enumerate(items)}


def fused(run, name, ins, outs, scratch, number):
    names = [*ins, *outs, *scratch]

    def kernel(*refs):
        run(Refs(names, refs))

    results = pl.pallas_call(
        kernel,
        name=name,
        out_shape=list(outs.values()),
        in_specs=[spec for _, spec in ins.values()],
        out_specs=[VMEM] * len(outs),
        scratch_shapes=list(scratch.values()),
        compiler_params=pltpu.CompilerParams(
            collective_id=number, has_side_effects=True, vmem_limit_bytes=60 * 1024 * 1024
        ),
    )(*[array for array, _ in ins.values()])
    return dict(zip(outs, results))


def shaped(*shape, dtype=bf16):
    return jax.ShapeDtypeStruct(shape, dtype)


TOKENS = (SEQ, WIDTH)
ROWS = (DP * EXPERTS, *BLOCK)
HOME = (EXPERTS, *BLOCK)
PRE = (CAP * DP * EXPERTS, FF)
COMMON = {
    "tokens": pltpu.VMEM(TOKENS, f32),
    "wide": pltpu.VMEM((CAP * DP * EXPERTS, WIDTH), bf16),
    "packed": pltpu.VMEM((PACKED, BLOCK[1]), bf16),
    "w0": pltpu.VMEM((WIDTH, LAT), bf16),
    "w1": pltpu.VMEM((LAT, LAT), bf16),
    "w2": pltpu.VMEM((LAT, WIDTH), bf16),
    "wsem": pltpu.SemaphoreType.DMA((3,)),
    "v0": pltpu.VMEM((WIDTH, FF), bf16),
    "v1": pltpu.VMEM((WIDTH, FF), bf16),
    "v2": pltpu.VMEM((FF, WIDTH), bf16),
    "vsem": pltpu.SemaphoreType.DMA((3,)),
}


def fetch_attn(refs, layer):
    attn = refs.some("attn", 6)
    return fetch(layer, [(attn[k], attn[3 + k], getattr(refs, f"w{k}")) for k in range(3)], refs.wsem)


def fetch_expert(refs, layer):
    expert = refs.some("expert", 6)
    return fetch(
        layer, [(expert[k], expert[3 + k], getattr(refs, f"v{k}")) for k in range(3)], refs.vsem
    )


def dispatch_of(refs, tag):
    return Dispatch(
        getattr(refs, "blk" + tag), getattr(refs, "rows" + tag), refs.some("ds" + tag + "_", 6)
    )


def dispatch_scratch(tag):
    return {
        "blk" + tag: pltpu.VMEM(HOME, bf16),
        "rows" + tag: pltpu.VMEM(ROWS, bf16),
        **named("ds" + tag + "_", Dispatch.sems),
    }


def combine_of(refs, tag):
    return Combine(
        getattr(refs, "part" + tag),
        getattr(refs, "home" + tag),
        refs.some("cb" + tag + "_", 5),
        refs.some("cs" + tag + "_", 6),
    )


def combine_scratch(tag, skip=()):
    whole = {
        "part" + tag: pltpu.VMEM(ROWS, bf16),
        "home" + tag: pltpu.VMEM(HOME, bf16),
        **named("cb" + tag + "_", Combine.buffers),
        **named("cs" + tag + "_", Combine.sems),
    }
    return {k: v for k, v in whole.items() if k not in skip}


def kept_shapes(layer):
    return {
        f"resid{layer}": shaped(*TOKENS),
        f"latent{layer}": shaped(SEQ, LAT),
        f"queries{layer}": shaped(SEQ, LAT),
        f"probs{layer}": shaped(SEQ, SEQ, dtype=f32),
        f"mixed{layer}": shaped(SEQ, LAT),
    }


def kept_refs(refs, layer):
    return [getattr(refs, f"{k}{layer}") for k in ("resid", "latent", "queries", "probs", "mixed")]


def forward_run(refs):
    e, _, _, _, right, left, _ = places()
    greet(e, right, left)
    wait_w = fetch_attn(refs, 0)
    wait_v = fetch_expert(refs, 0)
    first, early, second = (dispatch_of(refs, tag) for tag in ("a", "b", "c"))
    out0, back1 = combine_of(refs, "a"), combine_of(refs, "b")
    w = refs.some("w", 3)

    attend(
        refs.x[...], refs.route_row0[...], *w, wait_w, refs.packed, refs.blka, *kept_refs(refs, 0)
    )
    wait_w = fetch_attn(refs, 1)
    greeted()
    first.start()
    scaled = (refs.gate_col1[...] * refs.dy[...].astype(f32)).astype(bf16)
    pack_tokens(scaled, refs.route_row1[...], refs.packed, refs.blkb)
    for i in range(NZ):
        first.forward(i)
        if i >= 2:
            first.relay(i - 2)
        if i == 5:
            early.start()
    first.relay(6)
    first.relay(7)
    first.rest(lambda g: unpack_rows(refs.rowsa, refs.wide, g))

    wait_v(0)
    refs.gate0[...] = dot(refs.wide[...], refs.v0[...])
    wait_v(1)
    refs.up0[...] = dot(refs.wide[...], refs.v1[...])
    hidden = (silu_parts(refs.gate0[...])[0] * refs.up0[...]).astype(bf16)
    wait_v(2)
    expert_out(hidden, refs.v2, refs.wide)
    wait_v = fetch_expert(refs, 1)
    send_back(out0, refs.wide, refs.packed)
    for i in range(NZ):
        out0.relay(i)
    for i in range(NZ):
        early.forward(i)
    for i in range(NZ):
        out0.finish(i)
    out0.arrive()

    unpack_tokens(refs.homea, refs.route_col0[...], refs.tokens)
    act0 = (refs.resid0[...].astype(f32) + refs.gate_col0[...] * refs.tokens[...]).astype(bf16)
    refs.act0[...] = act0
    attend(act0, refs.route_row1[...], *w, wait_w, refs.packed, refs.blkc, *kept_refs(refs, 1))
    second.start()
    for i in range(NZ):
        early.relay(i)
    for i in range(NZ):
        second.forward(i)
        if i >= 2:
            second.relay(i - 2)
    second.relay(6)
    second.relay(7)
    second.rest(lambda g: unpack_rows(refs.rowsc, refs.wide, g))

    wait_v(0)
    refs.gate1[...] = dot(refs.wide[...], refs.v0[...])
    wait_v(1)
    refs.up1[...] = dot(refs.wide[...], refs.v1[...])
    early.rest(lambda g: unpack_rows(refs.rowsb, refs.wide, g))
    wait_v(2)
    expert_back(refs.wide, refs.gate1[...], refs.up1[...], refs.v0, refs.v1, refs.v2)
    send_back(back1, refs.wide, refs.packed)
    hidden = (silu_parts(refs.gate1[...])[0] * refs.up1[...]).astype(bf16)
    expert_out(hidden, refs.v2, refs.wide)
    for i in range(NZ):
        back1.relay(i)
    for g in range(DP):
        pack_rows(refs.wide, refs.packed, refs.part1, g)
    for i in range(NZ):
        back1.finish(i)
    back1.arrive()
    for each in (first, early, second, out0, back1):
        each.drain()


def backward_run(refs):
    e, _, _, _, right, left, _ = places()
    greet(e, right, left)
    wait_w = fetch_attn(refs, 1)
    wait_v = fetch_expert(refs, 0)
    again = dispatch_of(refs, "a")
    out1, back0 = combine_of(refs, "a"), combine_of(refs, "b")
    w = refs.some("w", 3)

    unpack_tokens(refs.back1, refs.route_col1[...], refs.tokens)
    greeted()
    out1.start_far()
    out1.start_near()
    attend_back(
        refs.dy[...], refs.act0[...], *[ref[...] for ref in kept_refs(refs, 1)], w, wait_w,
        refs.tokens, refs.n1, refs.dl1, refs.dq1, refs.dr1, refs.grad1,
    )
    wait_w = fetch_attn(refs, 0)
    scaled = (refs.gate_col0[...] * refs.grad1[...].astype(f32)).astype(bf16)
    pack_tokens(scaled, refs.route_row0[...], refs.packed, refs.blka)
    again.start()
    for i in range(NZ):
        out1.relay(i)
    for i in range(NZ):
        again.forward(i)
        if i >= 2:
            again.relay(i - 2)
    again.relay(6)
    again.relay(7)
    for i in range(NZ):
        out1.finish(i)
    again.rest(lambda g: unpack_rows(refs.rowsa, refs.wide, g))
    for k in range(3):
        wait_v(k)
    expert_back(refs.wide, refs.gate0[...], refs.up0[...], refs.v0, refs.v1, refs.v2)
    send_back(back0, refs.wide, refs.packed)
    for i in range(NZ):
        back0.relay(i)
    out1.arrive()
    unpack_tokens(refs.homea, refs.route_col1[...], refs.tokens)
    refs.act1[...] = (
        refs.resid1[...].astype(f32) + refs.gate_col1[...] * refs.tokens[...]
    ).astype(bf16)
    for i in range(NZ):
        back0.finish(i)
    back0.arrive()
    unpack_tokens(refs.homeb, refs.route_col0[...], refs.tokens)
    attend_back(
        refs.grad1[...], refs.x[...], *[ref[...] for ref in kept_refs(refs, 0)], w, wait_w,
        refs.tokens, refs.n0, refs.dl0, refs.dq0, refs.dr0, refs.grad0,
    )
    for each in (again, out1, back0):
        each.drain()


def factor_shapes(layer):
    return {
        f"n{layer}": shaped(*TOKENS),
        f"dl{layer}": shaped(SEQ, LAT),
        f"dq{layer}": shaped(SEQ, LAT),
        f"dr{layer}": shaped(*TOKENS),
        f"grad{layer}": shaped(*TOKENS),
    }


ROUND = 1792
SIDE = 1280


def quarter_matrix(first_is_dp):
    out = lax.broadcasted_iota(jnp.int32, (1, 1024), 1)
    one, two, zz, i = out // 256, (out // 64) % 4, (out // 32) % 2, out % 32
    y, x = (two, one) if first_is_dp else (one, two)
    source = jnp.where(i < 28, zz * 448 + y * 112 + x * 28 + i, -1)
    return (lax.broadcasted_iota(jnp.int32, (896, 1024), 0) == source).astype(f32).astype(bf16)


def small_matrix():
    out = lax.broadcasted_iota(jnp.int32, (1, 1024), 1)
    x, y, z, i = out // 256, (out // 64) % 4, (out // 8) % 8, out % 8
    source = jnp.where(i < 2, z * 32 + y * 8 + x * 2 + i, -1)
    return (lax.broadcasted_iota(jnp.int32, (LAT, 1024), 0) == source).astype(f32).astype(bf16)


def lay_out(factor, matrix, sent, layer):
    stacked = jnp.concatenate([factor[:, c * 896 : (c + 1) * 896] for c in range(4)], axis=0)
    moved = dot(stacked, matrix).astype(bf16)
    for q in range(4):
        for c in range(4):
            sent[layer, q, :, c * 256 : (c + 1) * 256] = moved[
                c * SEQ : (c + 1) * SEQ, q * 256 : (q + 1) * 256
            ]


class Ring:
    def __init__(self, section, position, near, sent, got, relay, ssem, fsem, rsem):
        self.section, self.position, self.near = section, position, near
        self.sent, self.got, self.relay_buf = sent, got, relay
        self.ssem, self.fsem, self.rsem = ssem, fsem, rsem

    def start(self, layer):
        pos, s = self.position, self.section
        way = 1 if layer == 0 else 3
        remote(
            self.sent.at[layer, (pos + 2) % 4],
            self.relay_buf.at[layer],
            self.ssem,
            self.rsem.at[layer],
            self.near(way),
        ).start()
        for step, back in ((1, 1), (3, 0)):
            remote(
                self.sent.at[layer, (pos + step) % 4],
                self.got.at[s, pos],
                self.ssem,
                self.fsem.at[s, back],
                {**self.near(step), "section": layer},
            ).start()

    def own(self):
        pos, s = self.position, self.section
        pltpu.make_async_copy(self.sent.at[s, pos], self.got.at[s, pos], self.fsem.at[s, 3]).start()
        remote(
            self.sent.at[1 - s, pos],
            self.got.at[s, pos],
            self.ssem,
            self.fsem.at[s, 3],
            {"section": 1 - s},
        ).start()

    def relay(self):
        for layer, way in ((0, 1), (1, 3)):
            buf = self.relay_buf.at[layer]
            remote(buf, buf, self.ssem, self.rsem.at[layer], self.near(1)).wait_recv()
            origin = (self.position + 4 - way) % 4
            remote(
                buf,
                self.got.at[self.section, origin],
                self.ssem,
                self.fsem.at[self.section, 2],
                {**self.near(way), "section": layer},
            ).start()

    def arrive(self):
        for m in range(2):
            for k, step in enumerate((1, 3, 2, 0)):
                ref = self.got.at[m, (self.position + step) % 4]
                remote(ref, ref, self.ssem, self.fsem.at[m, k], self.near(1)).wait_recv()

    def drain(self):
        for layer in range(2):
            ref = self.sent.at[layer]
            remote(ref, ref, self.ssem, self.rsem.at[0], self.near(1)).wait_send()
        ref = self.sent.at[0, 0]
        remote(ref, ref, self.ssem, self.rsem.at[0], self.near(1)).wait_send()


def fold(pieces):
    total = pieces[0].astype(f32)
    for piece in pieces[1:]:
        total = total + piece.astype(f32)
    return total


def grads_kernel(
    n0, dl0, la0, dq0, dr0, mx0, act0, grad0, n1, dl1, la1, dq1, dr1, mx1, act1, grad1,
    act_o, grad_o, down_o, qk_o, up_o,
    xs, xg, xr, ys, yg, yr, td, sd, zd, zr, tu, su, zu, zv,
    xssem, xfsem, xrsem, yssem, yfsem, yrsem, psem, qsem, asem, dsem, dr, usem, ur, zsem, zrecv,
):
    s = lax.axis_index("section")
    e, d, z, y, right, left, opp = places()

    def near_x(k):
        return {"dp": (d + k) % 4}

    def near_y(k):
        return {"expert": z * NY + (y + k) % 4}

    def near_z(k):
        return {"expert": ((z + k) % NZ) * NY + y}

    barrier = pltpu.get_barrier_semaphore()
    peers = [{"section": 1 - s}]
    for near in (near_x, near_y):
        for k in (1, 3):
            peers += [{**near(k), "section": 0}, {**near(k), "section": 1}]
        peers.append(near(2))
    peers += [near_z(k) for k in range(1, NZ)]
    for peer in peers:
        pl.semaphore_signal(barrier, inc=1, device_id=peer, device_id_type=MESH)
    x_ring = Ring(s, d, near_x, xs, xg, xr, xssem, xfsem, xrsem)
    y_ring = Ring(s, y, near_y, ys, yg, yr, yssem, yfsem, yrsem)
    factors = ((n0, dl0, la0, dq0, dr0, mx0), (n1, dl1, la1, dq1, dr1, mx1))
    by_x, by_y, small = quarter_matrix(True), quarter_matrix(False), small_matrix()
    for layer, (n, dl, la, dq, _, _) in enumerate(factors):
        lay_out(n[...], by_x, xs, layer)
        moved = dot(la[...], small).astype(bf16)
        for q in range(4):
            xs[layer, q, :, 1024:1280] = dl[...]
            xs[layer, q, :, 1280:1536] = moved[:, q * 256 : (q + 1) * 256]
            xs[layer, q, :, 1536:1792] = dq[...]
    pl.semaphore_wait(barrier, len(peers))
    x_ring.start(0)
    x_ring.start(1)
    for layer, (_, _, _, _, dres, mx) in enumerate(factors):
        lay_out(dres[...], by_y, ys, layer)
        for q in range(4):
            ys[layer, q, :, 1024:1280] = mx[...]
    y_ring.start(0)
    y_ring.start(1)
    x_ring.own()
    y_ring.own()

    for k, (out, first_layer, second_layer) in enumerate(((act_o, act0, act1), (grad_o, grad0, grad1))):
        for here, keep, give in ((0, first_layer, second_layer), (1, second_layer, first_layer)):

            @pl.when(s == here)
            def _():
                pltpu.make_async_copy(keep, out.at[s], asem.at[k]).start()
                remote(give, out.at[s], psem, qsem.at[k], {"section": 1 - s}).start()

    x_ring.relay()
    y_ring.relay()

    def rows(ring, start, width):
        got = ring.got
        return jnp.concatenate(
            [got[m, q, :, start : start + width] for m in range(2) for q in range(4)], axis=0
        )

    x_ring.arrive()
    total = t_times(rows(x_ring, 0, 1024), rows(x_ring, 1024, 256)).astype(bf16)
    total_qk = t_times(rows(x_ring, 1280, 256), rows(x_ring, 1536, 256)).astype(bf16)
    for q in range(4):
        for c in range(4):
            td[q, c * 64 : (c + 1) * 64, :] = total[c * 256 + q * 64 : c * 256 + (q + 1) * 64]
        td[q, 256:320, :] = total_qk[q * 64 : (q + 1) * 64]
    for k in (2, 1, 3):
        remote(td.at[(y + k) % 4], sd.at[y], dsem, dr.at[4 - k - 1], near_y(k)).start()
    y_ring.arrive()
    total = t_times(rows(y_ring, 0, 1024), rows(y_ring, 1024, 256)).astype(bf16)
    for q in range(4):
        for c in range(4):
            tu[q, c * 64 : (c + 1) * 64, :] = total[c * 256 + q * 64 : c * 256 + (q + 1) * 64]
    for k in (2, 1, 3):
        remote(tu.at[(d + k) % 4], su.at[d], usem, ur.at[4 - k - 1], near_x(k)).start()

    def gathered(buf, recv, position):
        for k in (1, 2, 3):
            ref = buf.at[(position + k) % 4]
            remote(ref, ref, dsem, recv.at[k - 1], near_x(1)).wait_recv()
        return [buf[(position + k) % 4] for k in (1, 2, 3)]

    summed = fold([td[y]] + gathered(sd, dr, y)).astype(bf16)
    for k in range(NZ):
        zd[k, 0:32, :] = summed[k * 32 : (k + 1) * 32]
        zd[k, 32:40, :] = summed[256 + k * 8 : 264 + k * 8]
    for k in range(1, NZ):
        remote(zd.at[(z + k) % NZ], zr.at[z], zsem.at[0], zrecv.at[0, NZ - k - 1], near_z(k)).start()
    summed = fold([tu[d]] + gathered(su, ur, d)).astype(bf16)
    for k in range(NZ):
        zu[k] = summed[k * 32 : (k + 1) * 32]
    for k in range(1, NZ):
        remote(zu.at[(z + k) % NZ], zv.at[z], zsem.at[1], zrecv.at[1, NZ - k - 1], near_z(k)).start()

    def last(own, buf, which):
        for k in range(1, NZ):
            ref = buf.at[(z + k) % NZ]
            remote(ref, ref, zsem.at[0], zrecv.at[which, k - 1], near_z(1)).wait_recv()
        return fold([own[z]] + [buf[(z + k) % NZ] for k in range(1, NZ)])

    mine = last(zd, zr, 0)
    down_o[...] = mine[0:28]
    qk_o[...] = mine[32:34]
    mine = last(zu, zv, 1)
    up_o[...] = mine[0:28]

    x_ring.drain()
    y_ring.drain()
    for k, (out, some) in enumerate(((act_o, act0), (grad_o, grad0))):
        pltpu.make_async_copy(some, out.at[s], asem.at[k]).wait()
        remote(some, out.at[1 - s], psem, qsem.at[k], {"section": 1 - s}).wait_recv()
    whole = act_o
    remote(whole, whole, psem, qsem.at[0], {"section": 1 - s}).wait_send()
    ref = td.at[pl.ds(0, 3)]
    remote(ref, ref, dsem, dr.at[0], near_x(1)).wait_send()
    ref = tu.at[pl.ds(0, 3)]
    remote(ref, ref, usem, ur.at[0], near_x(1)).wait_send()
    ref = zd.at[pl.ds(0, NZ - 1)]
    remote(ref, ref, zsem.at[0], dr.at[0], near_x(1)).wait_send()
    ref = zu.at[pl.ds(0, NZ - 1)]
    remote(ref, ref, zsem.at[1], dr.at[0], near_x(1)).wait_send()


def weight_grads(layer0, layer1):
    dma = pltpu.SemaphoreType.DMA
    ring_sems = [dma, dma((2, 4)), dma((2,))]
    return pl.pallas_call(
        grads_kernel,
        name="weight_grads",
        out_shape=[
            jax.ShapeDtypeStruct((2, SEQ, WIDTH), bf16),
            jax.ShapeDtypeStruct((2, SEQ, WIDTH), bf16),
            jax.ShapeDtypeStruct((28, LAT), f32),
            jax.ShapeDtypeStruct((2, LAT), f32),
            jax.ShapeDtypeStruct((28, LAT), f32),
        ],
        in_specs=[VMEM] * 16,
        out_specs=[VMEM] * 5,
        scratch_shapes=[
            pltpu.VMEM((2, 4, SEQ, ROUND), bf16),
            pltpu.VMEM((2, 4, SEQ, ROUND), bf16),
            pltpu.VMEM((2, SEQ, ROUND), bf16),
            pltpu.VMEM((2, 4, SEQ, SIDE), bf16),
            pltpu.VMEM((2, 4, SEQ, SIDE), bf16),
            pltpu.VMEM((2, SEQ, SIDE), bf16),
            pltpu.VMEM((4, 320, LAT), bf16),
            pltpu.VMEM((4, 320, LAT), bf16),
            pltpu.VMEM((NZ, 40, LAT), bf16),
            pltpu.VMEM((NZ, 40, LAT), bf16),
            pltpu.VMEM((4, 256, LAT), bf16),
            pltpu.VMEM((4, 256, LAT), bf16),
            pltpu.VMEM((NZ, 32, LAT), bf16),
            pltpu.VMEM((NZ, 32, LAT), bf16),
        ]
        + ring_sems * 2
        + [dma, dma((2,)), dma((2,)), dma, dma((3,)), dma, dma((3,)), dma((2,)), dma((2, NZ - 1))],
        compiler_params=pltpu.CompilerParams(collective_id=2, has_side_effects=True),
    )(*layer0, *layer1)


def swap(value):
    return lax.ppermute(value, "section", [(0, 1), (1, 0)])


def body(x_in, dy_out, routes, gates, w_down, w_qk, w_up, e_gate, e_up, e_down):
    section = lax.axis_index("section")
    attn_own = (w_down[0], w_qk[0], w_up[0])
    experts_own = (e_gate[0, 0], e_up[0, 0], e_down[0, 0])
    attn = attn_own + tuple(swap(w) for w in attn_own)
    experts = experts_own + tuple(swap(w) for w in experts_own)
    x = lax.dynamic_index_in_dim(x_in[:, 0], section, 0, keepdims=False)
    dy = lax.dynamic_index_in_dim(dy_out[:, 0], section, 0, keepdims=False)

    def both_layers(table):
        other = swap(lax.dynamic_index_in_dim(table, 1 - section, 0, keepdims=False))
        own = lax.dynamic_index_in_dim(table, section, 0, keepdims=False)
        return (jnp.where(section == 0, own, other), jnp.where(section == 0, other, own))

    route_cols = both_layers(routes[0, :, 0])
    gate_cols = both_layers(gates[0, :, 0])
    route_rows = tuple(r.reshape(1, SEQ) for r in route_cols)

    whole = {
        "x": (x, VMEM),
        "dy": (dy, VMEM),
        **{f"route_row{k}": (route_rows[k], VMEM) for k in range(2)},
        **{f"route_col{k}": (route_cols[k], VMEM) for k in range(2)},
        **{f"gate_col{k}": (gate_cols[k], VMEM) for k in range(2)},
        **named("attn", [(w, ANY) for w in attn]),
        **named("expert", [(w, ANY) for w in experts]),
    }
    kept = fused(
        forward_run,
        "forward",
        whole,
        {
            "act0": shaped(*TOKENS),
            **kept_shapes(0),
            **kept_shapes(1),
            "gate0": shaped(*PRE, dtype=f32),
            "up0": shaped(*PRE, dtype=f32),
            "part1": shaped(*ROWS),
            "homeb": shaped(*HOME),
        },
        {
            **COMMON,
            "gate1": pltpu.VMEM(PRE, f32),
            "up1": pltpu.VMEM(PRE, f32),
            **dispatch_scratch("a"),
            **dispatch_scratch("b"),
            **dispatch_scratch("c"),
            **combine_scratch("a"),
            **combine_scratch("b", skip=("homeb",)),
        },
        0,
    )
    part1, back1 = kept.pop("part1"), kept.pop("homeb")
    done = fused(
        backward_run,
        "backward",
        {
            **whole,
            **{k: (v, VMEM) for k, v in kept.items()},
            "parta": (part1, VMEM),
            "back1": (back1, VMEM),
        },
        {"act1": shaped(*TOKENS), **factor_shapes(1), **factor_shapes(0)},
        {
            **COMMON,
            **dispatch_scratch("a"),
            **combine_scratch("a", skip=("parta",)),
            **combine_scratch("b"),
        },
        1,
    )
    layers = [
        tuple({**kept, **done}[f"{k}{layer}"] for k in ("n", "dl", "latent", "dq", "dr", "mixed", "act", "grad"))
        for layer in range(2)
    ]
    activations, grads_in, g_down, g_qk, g_up_t = weight_grads(*layers)
    return (
        activations[None, :, None],
        grads_in[None, :, None],
        g_down[None],
        g_qk[None],
        g_up_t[None],
    )


def solution(mesh):
    placed = (
        P(None, ("expert", "dp"), None, None),
        P(None, ("expert", "dp"), None, None),
        P("section", None, ("expert", "dp"), None, None),
        P("section", None, ("expert", "dp"), None, None),
        P("section", None, None),
        P("section", None, None),
        P("section", None, None),
        P("section", "expert", None, "dp"),
        P("section", "expert", None, "dp"),
        P("section", "expert", "dp", None),
    )
    return jax.shard_map(
        body,
        mesh=mesh,
        in_specs=placed,
        out_specs=(
            P("section", None, ("expert", "dp"), None, None),
            P("section", None, ("expert", "dp"), None, None),
            P("section", ("expert", "dp"), None),
            P("section", ("expert", "dp"), None),
            P("section", ("expert", "dp"), None),
        ),
        check_vma=False,
    )
```

```python
import functools

import jax
import jax.numpy as jnp
from jax import lax
from jax.experimental import pallas as pl
from jax.experimental.pallas import tpu as pltpu
from jax.sharding import PartitionSpec as P

epsilon = 1e-06
WIDTH = 3584
LAT = 256
FF = 256
SEQ = 64
EXPERTS = 32
DP = 4
CAP = 3
NZ = 8
NY = 4
PIECE = 512
PIECES = 7
BLOCK = (8, CAP * PIECE)
PACKED = PIECES * EXPERTS
ORDER = (0, 1, 7, 2, 6, 3, 5, 4)
MESH = pl.DeviceIdType.MESH
VMEM = pl.BlockSpec(memory_space=pltpu.VMEM)
ANY = pl.BlockSpec(memory_space=pl.ANY)
bf16 = jnp.bfloat16
f32 = jnp.float32


def dot(left, right):
    return jnp.dot(left, right, preferred_element_type=f32)


def times_t(left, right):
    return lax.dot_general(left, right, (((1,), (1,)), ((), ())), preferred_element_type=f32)


def t_times(left, right):
    return lax.dot_general(left, right, (((0,), (0,)), ((), ())), preferred_element_type=f32)


def rms_norm(values):
    inv_rms = lax.rsqrt(jnp.mean(values * values, axis=-1, keepdims=True) + epsilon)
    return (values * inv_rms, inv_rms)


def rms_back(normed, inv_rms, upstream):
    return inv_rms * (upstream - normed * jnp.mean(upstream * normed, axis=-1, keepdims=True))


def silu_parts(gate_pre):
    sigmoid = jax.nn.sigmoid(gate_pre)
    return (gate_pre * sigmoid, sigmoid * (1.0 + gate_pre * (1.0 - sigmoid)))


def spread_matrix():
    rows = lax.broadcasted_iota(jnp.int32, (EXPERTS * 8, PACKED), 0)
    cols = lax.broadcasted_iota(jnp.int32, (EXPERTS * 8, PACKED), 1)
    return ((rows % 8) * EXPERTS + rows // 8 == cols).astype(f32).astype(bf16)


def gather_matrix():
    rows = lax.broadcasted_iota(jnp.int32, (PACKED, EXPERTS * 8), 0)
    cols = lax.broadcasted_iota(jnp.int32, (PACKED, EXPERTS * 8), 1)
    return ((cols % 8) * EXPERTS + cols // 8 == rows).astype(f32).astype(bf16)


def slot_rows(route_row):
    experts = lax.broadcasted_iota(jnp.int32, (EXPERTS, SEQ), 0)
    hot = (experts == route_row).astype(f32)
    before = lax.broadcasted_iota(jnp.int32, (SEQ, SEQ), 0) < lax.broadcasted_iota(
        jnp.int32, (SEQ, SEQ), 1
    )
    rank = dot(hot.astype(bf16), before.astype(f32).astype(bf16))
    return jnp.concatenate(
        [(hot * (rank == float(s)).astype(f32)).astype(bf16) for s in range(CAP)], axis=0
    )


def slot_columns(route_col):
    experts = lax.broadcasted_iota(jnp.int32, (SEQ, EXPERTS), 1)
    hot = (experts == route_col).astype(f32)
    before = lax.broadcasted_iota(jnp.int32, (SEQ, SEQ), 0) > lax.broadcasted_iota(
        jnp.int32, (SEQ, SEQ), 1
    )
    rank = dot(before.astype(f32).astype(bf16), hot.astype(bf16))
    return jnp.concatenate(
        [(hot * (rank == float(s)).astype(f32)).astype(bf16) for s in range(CAP)], axis=1
    )


def pack_tokens(values_b, route_row, packed_ref, blocks_ref):
    picked = dot(slot_rows(route_row), values_b).astype(bf16)
    for s in range(CAP):
        for r in range(PIECES):
            packed_ref[r * EXPERTS : (r + 1) * EXPERTS, s * PIECE : (s + 1) * PIECE] = picked[
                s * EXPERTS : (s + 1) * EXPERTS, r * PIECE : (r + 1) * PIECE
            ]
    blocks_ref[...] = dot(spread_matrix(), packed_ref[...]).astype(bf16).reshape(HOME)


def unpack_tokens(blocks_ref, route_col, token_ref):
    packed = dot(gather_matrix(), blocks_ref[...].reshape(EXPERTS * 8, BLOCK[1])).astype(bf16)
    columns = slot_columns(route_col)
    for r in range(PIECES):
        stacked = jnp.concatenate(
            [
                packed[r * EXPERTS : (r + 1) * EXPERTS, s * PIECE : (s + 1) * PIECE]
                for s in range(CAP)
            ],
            axis=0,
        )
        token_ref[:, r * PIECE : (r + 1) * PIECE] = dot(columns, stacked)


def places():
    e = lax.axis_index("expert")
    d = lax.axis_index("dp")
    return e, d, e // NY, e % NY, (d + 1) % DP, (d + DP - 1) % DP, (d + 2) % DP


def greet(e, right, left):
    barrier = pltpu.get_barrier_semaphore()
    for k in range(1, EXPERTS):
        pl.semaphore_signal(
            barrier, inc=1, device_id={"expert": (e + k) % EXPERTS}, device_id_type=MESH
        )
    for side in (right, left):
        pl.semaphore_signal(barrier, inc=1, device_id={"dp": side}, device_id_type=MESH)
    partner = {"section": 1 - lax.axis_index("section")}
    pl.semaphore_signal(barrier, inc=1, device_id=partner, device_id_type=MESH)


def greeted():
    pl.semaphore_wait(pltpu.get_barrier_semaphore(), EXPERTS + 2)


def remote(src, dst, send, recv, where):
    return pltpu.make_async_remote_copy(
        src_ref=src, dst_ref=dst, send_sem=send, recv_sem=recv, device_id=where, device_id_type=MESH
    )


class Dispatch:
    sems = (
        pltpu.SemaphoreType.DMA,
        pltpu.SemaphoreType.DMA,
        pltpu.SemaphoreType.DMA((NZ,)),
        pltpu.SemaphoreType.DMA((NZ,)),
        pltpu.SemaphoreType.DMA((NZ,)),
        pltpu.SemaphoreType.DMA((NZ,)),
    )

    def __init__(self, blk, rows, sems):
        self.blk, self.rows = blk, rows
        self.s1, self.sx, self.r1, self.rl, self.rr, self.ro = sems
        self.e, self.d, self.z, self.y, self.right, self.left, self.opp = places()

    def start(self):
        for j in ORDER:
            for dy in range(NY):
                spot = self.rows.at[self.d * EXPERTS + self.e]
                if j == 0 and dy == 0:
                    pltpu.make_async_copy(self.blk.at[self.e], spot, self.r1.at[0]).start()
                else:
                    peer = ((self.z + j) % NZ) * NY + (self.y + dy) % NY
                    remote(
                        self.blk.at[peer], spot, self.s1, self.r1.at[(NZ - j) % NZ], {"expert": peer}
                    ).start()

    def group(self, owner, j):
        return self.rows.at[pl.ds(owner * EXPERTS + ((self.z + j) % NZ) * NY, NY)]

    def arrived(self, ref, sem):
        remote(ref, ref, self.s1, sem, {"dp": self.right}).wait_recv()

    def forward(self, i):
        j = ORDER[i]
        mine = self.group(self.d, j)
        self.arrived(mine, self.r1.at[j])
        remote(mine, mine, self.sx, self.rl.at[j], {"dp": self.right}).start()
        remote(mine, mine, self.sx, self.rr.at[j], {"dp": self.left}).start()

    def relay(self, i):
        j = ORDER[i]
        owner, sem, to = (
            (self.left, self.rl, self.right) if i % 2 == 0 else (self.right, self.rr, self.left)
        )
        ref = self.group(owner, j)
        self.arrived(ref, sem.at[j])
        remote(ref, ref, self.sx, self.ro.at[j], {"dp": to}).start()

    def wait_right(self):
        for i, j in enumerate(ORDER):
            if i % 2 == 0:
                self.arrived(self.group(self.right, j), self.rr.at[j])

    def wait_left(self):
        for i, j in enumerate(ORDER):
            if i % 2 == 1:
                self.arrived(self.group(self.left, j), self.rl.at[j])

    def wait_far(self):
        for j in ORDER:
            self.arrived(self.group(self.opp, j), self.ro.at[j])

    def chunks(self, use, near):
        @pl.loop(0, DP)
        def _(k):
            pl.when(k == 1)(self.wait_right)
            pl.when(k == 2)(self.wait_left)
            pl.when(k == 3)(self.wait_far)
            use((self.d + k + k // 2 - 2 * (k // 3)) % DP)
            pl.when(k == 2)(near)

    def drain(self):
        sent = self.blk.at[pl.ds(0, EXPERTS - 1)]
        remote(sent, sent, self.s1, self.r1.at[0], {"dp": self.right}).wait_send()
        sent = self.rows.at[pl.ds(0, 3 * EXPERTS)]
        remote(sent, sent, self.sx, self.r1.at[0], {"dp": self.right}).wait_send()


class Combine:
    sems = (
        pltpu.SemaphoreType.DMA,
        pltpu.SemaphoreType.DMA,
        pltpu.SemaphoreType.DMA((NZ,)),
        pltpu.SemaphoreType.DMA((NZ,)),
        pltpu.SemaphoreType.DMA((NZ,)),
        pltpu.SemaphoreType.DMA,
    )
    buffers = (pltpu.VMEM((EXPERTS, *BLOCK), bf16),) * 5

    def __init__(self, part, out, buffers, sems):
        self.part, self.out = part, out
        self.relayed, self.relay_sum, self.from_left, self.from_right, self.final = buffers
        self.sx, self.s1, self.ra, self.rl, self.rr, self.rh = sems
        self.e, self.d, self.z, self.y, self.right, self.left, self.opp = places()

    def group(self, owner, j):
        return self.part.at[pl.ds(owner * EXPERTS + ((self.z + j) % NZ) * NY, NY)]

    def spot(self, ref, i):
        return ref.at[pl.ds(i * NY, NY)]

    def arrived(self, ref, sem):
        remote(ref, ref, self.s1, sem, {"dp": self.right}).wait_recv()

    def start_far(self):
        for i, j in enumerate(ORDER):
            side = self.right if i % 2 == 0 else self.left
            remote(
                self.group(self.opp, j), self.spot(self.relayed, i), self.sx, self.ra.at[i], {"dp": side}
            ).start()

    def start_near(self):
        for i, j in enumerate(ORDER):
            if i % 2 == 0:
                ref, to, sem, side = self.left, self.from_right, self.rr, self.left
            else:
                ref, to, sem, side = self.right, self.from_left, self.rl, self.right
            remote(self.group(ref, j), self.spot(to, i), self.sx, sem.at[i], {"dp": side}).start()

    def relay(self, i):
        j = ORDER[i]
        self.arrived(self.spot(self.relayed, i), self.ra.at[i])
        side, to, sem = (
            (self.right, self.from_left, self.rl)
            if i % 2 == 0
            else (self.left, self.from_right, self.rr)
        )
        self.spot(self.relay_sum, i)[...] = (
            self.spot(self.relayed, i)[...].astype(f32) + self.group(side, j)[...].astype(f32)
        ).astype(bf16)
        remote(
            self.spot(self.relay_sum, i), self.spot(to, i), self.sx, sem.at[i], {"dp": side}
        ).start()

    def finish(self, i):
        j = ORDER[i]
        self.arrived(self.spot(self.from_left, i), self.rl.at[i])
        self.arrived(self.spot(self.from_right, i), self.rr.at[i])
        self.spot(self.final, i)[...] = (
            self.group(self.d, j)[...].astype(f32)
            + self.spot(self.from_left, i)[...].astype(f32)
            + self.spot(self.from_right, i)[...].astype(f32)
        ).astype(bf16)
        for dy in range(NY):
            yy = (self.y + dy) % NY
            spot = self.out.at[self.e]
            if j == 0 and dy == 0:
                pltpu.make_async_copy(self.final.at[i * NY + yy], spot, self.rh).start()
            else:
                peer = ((self.z + j) % NZ) * NY + yy
                remote(
                    self.final.at[i * NY + yy], spot, self.s1, self.rh, {"expert": peer}
                ).start()

    def arrive(self):
        self.arrived(self.out, self.rh)

    def drain(self):
        sent = self.part.at[pl.ds(0, 3 * EXPERTS)]
        remote(sent, sent, self.sx, self.rh, {"dp": self.right}).wait_send()
        sent = self.part.at[pl.ds(0, EXPERTS - 1)]
        remote(sent, sent, self.s1, self.rh, {"dp": self.right}).wait_send()


def fetch(layer, pairs, sems):
    mine = lax.axis_index("section") == layer
    for k, (own, other, dst) in enumerate(pairs):

        @pl.when(mine)
        def _():
            pltpu.make_async_copy(own, dst, sems.at[k]).start()

        @pl.when(jnp.logical_not(mine))
        def _():
            pltpu.make_async_copy(other, dst, sems.at[k]).start()

    def wait(k):
        own, _, dst = pairs[k]
        pltpu.make_async_copy(own, dst, sems.at[k]).wait()

    return wait


def attend(
    inputs, route_row, wd, wq, wu, wait, packed, blocks, residual, latent_o, queries_o, probs_o, mixed_o
):
    normed, _ = rms_norm(inputs.astype(f32))
    wait(0)
    latent = dot(normed.astype(bf16), wd[...]).astype(bf16)
    wait(1)
    queries = dot(latent, wq[...]).astype(bf16)
    scores = times_t(queries, latent) * (LAT ** (-0.5))
    causal = lax.broadcasted_iota(jnp.int32, (SEQ, SEQ), 0) >= lax.broadcasted_iota(
        jnp.int32, (SEQ, SEQ), 1
    )
    scores = jnp.where(causal, scores, -1e30)
    exponent = jnp.exp(scores - jnp.max(scores, axis=-1, keepdims=True))
    probs = exponent / jnp.sum(exponent, axis=-1, keepdims=True)
    mixed = dot(probs.astype(bf16), latent).astype(bf16)
    wait(2)
    resid = (inputs.astype(f32) + dot(mixed, wu[...])).astype(bf16)
    residual[...] = resid
    latent_o[...] = latent
    queries_o[...] = queries
    probs_o[...] = probs
    mixed_o[...] = mixed
    normed2, _ = rms_norm(resid.astype(f32))
    pack_tokens(normed2.astype(bf16), route_row, packed, blocks)


def attend_back(
    upstream, inputs, resid, latent, queries, probs, mixed, w, wait, tokens, normed_o, d_latent_o,
    d_queries_o, d_resid_o, grad,
):
    normed2, inv2 = rms_norm(resid.astype(f32))
    d_resid = upstream.astype(f32) + rms_back(normed2, inv2, tokens[...])
    d_resid_b = d_resid.astype(bf16)
    d_resid_o[...] = d_resid_b
    tokens[...] = d_resid
    wd, wq, wu = w
    wait(2)
    d_mixed = times_t(d_resid_b, wu[...]).astype(bf16)
    d_probs = times_t(d_mixed, latent)
    d_scores = (
        probs * (d_probs - jnp.sum(d_probs * probs, axis=-1, keepdims=True)) * (LAT ** (-0.5))
    ).astype(bf16)
    d_queries = dot(d_scores, latent).astype(bf16)
    wait(1)
    d_latent = (
        t_times(probs.astype(bf16), d_mixed)
        + t_times(d_scores, queries)
        + times_t(d_queries, wq[...])
    ).astype(bf16)
    wait(0)
    d_normed = times_t(d_latent, wd[...])
    normed, inv = rms_norm(inputs.astype(f32))
    normed_o[...] = normed.astype(bf16)
    d_latent_o[...] = d_latent
    d_queries_o[...] = d_queries
    grad[...] = (tokens[...] + rms_back(normed, inv, d_normed)).astype(bf16)


CHUNK = CAP * EXPERTS


def unpack_rows(rows, wide, g):
    packed = dot(
        gather_matrix(), rows[pl.ds(g * EXPERTS, EXPERTS)].reshape(EXPERTS * 8, BLOCK[1])
    ).astype(bf16)
    for s in range(CAP):
        for r in range(PIECES):
            wide[s * EXPERTS : (s + 1) * EXPERTS, r * PIECE : (r + 1) * PIECE] = packed[
                r * EXPERTS : (r + 1) * EXPERTS, s * PIECE : (s + 1) * PIECE
            ]
    return wide[...]


def pack_rows(piece, packed, out, g):
    for r in range(PIECES):
        rows = piece(slice(r * PIECE, (r + 1) * PIECE)).astype(bf16)
        for s in range(CAP):
            packed[r * EXPERTS : (r + 1) * EXPERTS, s * PIECE : (s + 1) * PIECE] = rows[
                s * EXPERTS : (s + 1) * EXPERTS
            ]
    out[pl.ds(g * EXPERTS, EXPERTS)] = (
        dot(spread_matrix(), packed[...]).astype(bf16).reshape(EXPERTS, *BLOCK)
    )


def chunk_rows(g):
    return pl.ds(pl.multiple_of(g * CHUNK, CHUNK), CHUNK)


def expert_out(hidden, dw):
    return lambda cols: dot(hidden, dw[:, cols])


def expert_back(rows, gate_pre, up_pre, gw, uw, dw):
    d_hidden = times_t(rows, dw[...])
    activated, slope = silu_parts(gate_pre)
    d_gate = (d_hidden * up_pre * slope).astype(bf16)
    d_up = (d_hidden * activated).astype(bf16)
    return lambda cols: times_t(d_gate, gw[cols, :]) + times_t(d_up, uw[cols, :])


class Refs:
    def __init__(self, names, refs):
        for name, ref in zip(names, refs, strict=True):
            setattr(self, name, ref)

    def some(self, prefix, count):
        return tuple(getattr(self, f"{prefix}{k}") for k in range(count))


def named(prefix, items):
    return {f"{prefix}{k}": item for k, item in enumerate(items)}


def fused(run, name, ins, outs, scratch, number):
    names = [*ins, *outs, *scratch]

    def kernel(*refs):
        run(Refs(names, refs))

    results = pl.pallas_call(
        kernel,
        name=name,
        out_shape=list(outs.values()),
        in_specs=[spec for _, spec in ins.values()],
        out_specs=[VMEM] * len(outs),
        scratch_shapes=list(scratch.values()),
        compiler_params=pltpu.CompilerParams(
            collective_id=number, has_side_effects=True, vmem_limit_bytes=60 * 1024 * 1024
        ),
    )(*[array for array, _ in ins.values()])
    return dict(zip(outs, results))


def shaped(*shape, dtype=bf16):
    return jax.ShapeDtypeStruct(shape, dtype)


TOKENS = (SEQ, WIDTH)
ROWS = (DP * EXPERTS, *BLOCK)
HOME = (EXPERTS, *BLOCK)
PRE = (CAP * DP * EXPERTS, FF)
COMMON = {
    "tokens": pltpu.VMEM(TOKENS, f32),
    "wide": pltpu.VMEM((CHUNK, WIDTH), bf16),
    "packed": pltpu.VMEM((PACKED, BLOCK[1]), bf16),
    "w0": pltpu.VMEM((WIDTH, LAT), bf16),
    "w1": pltpu.VMEM((LAT, LAT), bf16),
    "w2": pltpu.VMEM((LAT, WIDTH), bf16),
    "wsem": pltpu.SemaphoreType.DMA((3,)),
}
EXPERT_WEIGHTS = ((WIDTH, FF), (WIDTH, FF), (FF, WIDTH))


def fetch_attn(refs, layer):
    attn = refs.some("attn", 6)
    return fetch(layer, [(attn[k], attn[3 + k], getattr(refs, f"w{k}")) for k in range(3)], refs.wsem)


class Experts:
    @staticmethod
    def scratch(layers):
        return {
            **named("v", [pltpu.VMEM((layers, *shape), bf16) for shape in EXPERT_WEIGHTS]),
            "vsem": pltpu.SemaphoreType.DMA((layers, 3)),
            "vsent": pltpu.SemaphoreType.DMA((3,)),
        }

    def __init__(self, refs, layers):
        self.s = lax.axis_index("section")
        self.own = refs.some("expert", 3)
        self.v = refs.some("v", 3)
        self.sem, self.sent, self.layers = refs.vsem, refs.vsent, layers

    def each(self, act):
        def run():
            for k in range(3):
                act(k)

        if self.layers == 1:
            pl.when(self.s == 0)(run)
        else:
            run()

    def place(self):
        return self.s if self.layers == 2 else 0

    def copy(self, k):
        return pltpu.make_async_copy(
            self.own[k], self.v[k].at[self.place()], self.sem.at[self.place(), k]
        )

    def give(self, k):
        return remote(
            self.own[k],
            self.v[k].at[self.place()],
            self.sent.at[k],
            self.sem.at[self.place(), k],
            {"section": 1 - self.s},
        )

    def start(self):
        self.each(lambda k: self.copy(k).start())

    def send(self):
        self.each(lambda k: self.give(k).start())

    def drain(self):
        self.each(lambda k: self.give(k).wait_send())

    def ready(self, layer):
        for k in range(3):
            pltpu.make_async_copy(
                self.own[k], self.v[k].at[layer], self.sem.at[layer, k]
            ).wait()
        return [ref.at[layer] for ref in self.v]


def dispatch_of(refs, tag):
    return Dispatch(
        getattr(refs, "blk" + tag), getattr(refs, "rows" + tag), refs.some("ds" + tag + "_", 6)
    )


def dispatch_scratch(tag):
    return {
        "blk" + tag: pltpu.VMEM(HOME, bf16),
        "rows" + tag: pltpu.VMEM(ROWS, bf16),
        **named("ds" + tag + "_", Dispatch.sems),
    }


def combine_of(refs, tag):
    return Combine(
        getattr(refs, "part" + tag),
        getattr(refs, "home" + tag),
        refs.some("cb" + tag + "_", 5),
        refs.some("cs" + tag + "_", 6),
    )


def combine_scratch(tag, skip=()):
    whole = {
        "part" + tag: pltpu.VMEM(ROWS, bf16),
        "home" + tag: pltpu.VMEM(HOME, bf16),
        **named("cb" + tag + "_", Combine.buffers),
        **named("cs" + tag + "_", Combine.sems),
    }
    return {k: v for k, v in whole.items() if k not in skip}


def kept_shapes(layer):
    return {
        f"resid{layer}": shaped(*TOKENS),
        f"latent{layer}": shaped(SEQ, LAT),
        f"queries{layer}": shaped(SEQ, LAT),
        f"probs{layer}": shaped(SEQ, SEQ, dtype=f32),
        f"mixed{layer}": shaped(SEQ, LAT),
    }


def kept_refs(refs, layer):
    return [getattr(refs, f"{k}{layer}") for k in ("resid", "latent", "queries", "probs", "mixed")]


def forward_run(refs):
    e, _, _, _, right, left, _ = places()
    section = lax.axis_index("section")
    greet(e, right, left)
    wait_w = fetch_attn(refs, 0)
    experts = Experts(refs, 2)
    experts.start()
    first, early, second = (dispatch_of(refs, tag) for tag in ("a", "b", "c"))
    out0, back1 = combine_of(refs, "a"), combine_of(refs, "b")
    w = refs.some("w", 3)

    attend(
        refs.x[section], refs.route_row0[...], *w, wait_w, refs.packed, refs.blka,
        *kept_refs(refs, 0),
    )
    wait_w = fetch_attn(refs, 1)
    greeted()
    first.start()
    experts.send()
    scaled = (refs.gate_col1[...] * refs.dy[section].astype(f32)).astype(bf16)
    pack_tokens(scaled, refs.route_row1[...], refs.packed, refs.blkb)
    for i in range(NZ):
        first.forward(i)
        if i >= 2:
            first.relay(i - 2)
        if i == 5:
            early.start()
    first.relay(6)
    first.relay(7)
    gw, uw, dw = experts.ready(0)

    def forward0(g):
        at = chunk_rows(g)
        rows = unpack_rows(refs.rowsa, refs.wide, g)
        gate_pre, up_pre = dot(rows, gw[...]), dot(rows, uw[...])
        refs.gate0[at, :] = gate_pre
        refs.up0[at, :] = up_pre
        hidden = (silu_parts(gate_pre)[0] * up_pre).astype(bf16)
        pack_rows(expert_out(hidden, dw), refs.packed, out0.part, g)

    first.chunks(forward0, out0.start_near)
    out0.start_far()
    for i in range(NZ):
        out0.relay(i)
    for i in range(NZ):
        early.forward(i)
    for i in range(NZ):
        out0.finish(i)
    out0.arrive()

    unpack_tokens(refs.homea, refs.route_col0[...], refs.tokens)
    act0 = (refs.resid0[...].astype(f32) + refs.gate_col0[...] * refs.tokens[...]).astype(bf16)
    refs.act0[...] = act0
    attend(act0, refs.route_row1[...], *w, wait_w, refs.packed, refs.blkc, *kept_refs(refs, 1))
    second.start()
    for i in range(NZ):
        early.relay(i)
    for i in range(NZ):
        second.forward(i)
        if i >= 2:
            second.relay(i - 2)
    second.relay(6)
    second.relay(7)
    early.wait_right()
    early.wait_left()
    early.wait_far()
    gw1, uw1, dw1 = experts.ready(1)

    def both1(g):
        at = chunk_rows(g)
        rows = unpack_rows(refs.rowsc, refs.wide, g)
        gate_pre, up_pre = dot(rows, gw1[...]), dot(rows, uw1[...])
        refs.hidden[at, :] = (silu_parts(gate_pre)[0] * up_pre).astype(bf16)
        rows = unpack_rows(refs.rowsb, refs.wide, g)
        pack_rows(
            expert_back(rows, gate_pre, up_pre, gw1, uw1, dw1), refs.packed, back1.part, g
        )

    def out1(g):
        pack_rows(expert_out(refs.hidden[chunk_rows(g), :], dw1), refs.packed, refs.part1, g)

    second.chunks(both1, back1.start_near)
    back1.start_far()
    pl.loop(0, 2)(out1)
    for i in range(NZ):
        back1.relay(i)
    pl.loop(2, DP)(out1)
    for i in range(NZ):
        back1.finish(i)
    back1.arrive()
    for each in (first, early, second, out0, back1, experts):
        each.drain()


def backward_run(refs):
    e, _, _, _, right, left, _ = places()
    section = lax.axis_index("section")
    greet(e, right, left)
    wait_w = fetch_attn(refs, 1)
    experts = Experts(refs, 1)
    experts.start()
    again = dispatch_of(refs, "a")
    out1, back0 = combine_of(refs, "a"), combine_of(refs, "b")
    w = refs.some("w", 3)

    unpack_tokens(refs.back1, refs.route_col1[...], refs.tokens)
    greeted()
    out1.start_far()
    out1.start_near()
    experts.send()
    attend_back(
        refs.dy[section], refs.act0[...], *[ref[...] for ref in kept_refs(refs, 1)], w, wait_w,
        refs.tokens, refs.n1, refs.dl1, refs.dq1, refs.dr1, refs.grad1,
    )
    wait_w = fetch_attn(refs, 0)
    scaled = (refs.gate_col0[...] * refs.grad1[...].astype(f32)).astype(bf16)
    pack_tokens(scaled, refs.route_row0[...], refs.packed, refs.blka)
    again.start()
    for i in range(NZ):
        out1.relay(i)
    for i in range(NZ):
        again.forward(i)
        if i >= 2:
            again.relay(i - 2)
    again.relay(6)
    again.relay(7)
    for i in range(NZ):
        out1.finish(i)
    gw, uw, dw = experts.ready(0)

    def backward0(g):
        at = chunk_rows(g)
        rows = unpack_rows(refs.rowsa, refs.wide, g)
        pack_rows(
            expert_back(rows, refs.gate0[at, :], refs.up0[at, :], gw, uw, dw),
            refs.packed,
            back0.part,
            g,
        )

    again.chunks(backward0, back0.start_near)
    back0.start_far()
    for i in range(NZ):
        back0.relay(i)
    out1.arrive()
    unpack_tokens(refs.homea, refs.route_col1[...], refs.tokens)
    refs.act1[...] = (
        refs.resid1[...].astype(f32) + refs.gate_col1[...] * refs.tokens[...]
    ).astype(bf16)
    for i in range(NZ):
        back0.finish(i)
    back0.arrive()
    unpack_tokens(refs.homeb, refs.route_col0[...], refs.tokens)
    attend_back(
        refs.grad1[...], refs.x[section], *[ref[...] for ref in kept_refs(refs, 0)], w, wait_w,
        refs.tokens, refs.n0, refs.dl0, refs.dq0, refs.dr0, refs.grad0,
    )
    for each in (again, out1, back0, experts):
        each.drain()


def factor_shapes(layer):
    return {
        f"n{layer}": shaped(*TOKENS),
        f"dl{layer}": shaped(SEQ, LAT),
        f"dq{layer}": shaped(SEQ, LAT),
        f"dr{layer}": shaped(*TOKENS),
        f"grad{layer}": shaped(*TOKENS),
    }


ROUND = 1792
SIDE = 1280


def quarter_matrix(first_is_dp):
    out = lax.broadcasted_iota(jnp.int32, (1, 1024), 1)
    one, two, zz, i = out // 256, (out // 64) % 4, (out // 32) % 2, out % 32
    y, x = (two, one) if first_is_dp else (one, two)
    source = jnp.where(i < 28, zz * 448 + y * 112 + x * 28 + i, -1)
    return (lax.broadcasted_iota(jnp.int32, (896, 1024), 0) == source).astype(f32).astype(bf16)


def small_matrix():
    out = lax.broadcasted_iota(jnp.int32, (1, 1024), 1)
    x, y, z, i = out // 256, (out // 64) % 4, (out // 8) % 8, out % 8
    source = jnp.where(i < 2, z * 32 + y * 8 + x * 2 + i, -1)
    return (lax.broadcasted_iota(jnp.int32, (LAT, 1024), 0) == source).astype(f32).astype(bf16)


def lay_out(factor, matrix, sent, layer):
    stacked = jnp.concatenate([factor[:, c * 896 : (c + 1) * 896] for c in range(4)], axis=0)
    moved = dot(stacked, matrix).astype(bf16)
    for q in range(4):
        for c in range(4):
            sent[layer, q, :, c * 256 : (c + 1) * 256] = moved[
                c * SEQ : (c + 1) * SEQ, q * 256 : (q + 1) * 256
            ]


class Ring:
    def __init__(self, section, position, near, sent, got, relay, ssem, fsem, rsem):
        self.section, self.position, self.near = section, position, near
        self.sent, self.got, self.relay_buf = sent, got, relay
        self.ssem, self.fsem, self.rsem = ssem, fsem, rsem

    def start(self, layer):
        pos, s = self.position, self.section
        way = 1 if layer == 0 else 3
        remote(
            self.sent.at[layer, (pos + 2) % 4],
            self.relay_buf.at[layer],
            self.ssem,
            self.rsem.at[layer],
            self.near(way),
        ).start()
        for step, back in ((1, 1), (3, 0)):
            remote(
                self.sent.at[layer, (pos + step) % 4],
                self.got.at[s, pos],
                self.ssem,
                self.fsem.at[s, back],
                {**self.near(step), "section": layer},
            ).start()

    def own(self):
        pos, s = self.position, self.section
        pltpu.make_async_copy(self.sent.at[s, pos], self.got.at[s, pos], self.fsem.at[s, 3]).start()
        remote(
            self.sent.at[1 - s, pos],
            self.got.at[s, pos],
            self.ssem,
            self.fsem.at[s, 3],
            {"section": 1 - s},
        ).start()

    def relay(self):
        for layer, way in ((0, 1), (1, 3)):
            buf = self.relay_buf.at[layer]
            remote(buf, buf, self.ssem, self.rsem.at[layer], self.near(1)).wait_recv()
            origin = (self.position + 4 - way) % 4
            remote(
                buf,
                self.got.at[self.section, origin],
                self.ssem,
                self.fsem.at[self.section, 2],
                {**self.near(way), "section": layer},
            ).start()

    def arrive(self):
        for m in range(2):
            for k, step in enumerate((1, 3, 2, 0)):
                ref = self.got.at[m, (self.position + step) % 4]
                remote(ref, ref, self.ssem, self.fsem.at[m, k], self.near(1)).wait_recv()

    def drain(self):
        for layer in range(2):
            ref = self.sent.at[layer]
            remote(ref, ref, self.ssem, self.rsem.at[0], self.near(1)).wait_send()
        ref = self.sent.at[0, 0]
        remote(ref, ref, self.ssem, self.rsem.at[0], self.near(1)).wait_send()


def fold(pieces):
    total = pieces[0].astype(f32)
    for piece in pieces[1:]:
        total = total + piece.astype(f32)
    return total


def grads_kernel(
    n0, dl0, la0, dq0, dr0, mx0, act0, grad0, n1, dl1, la1, dq1, dr1, mx1, act1, grad1,
    act_o, grad_o, down_o, qk_o, up_o,
    xs, xg, xr, ys, yg, yr, td, sd, zd, zr, tu, su, zu, zv,
    xssem, xfsem, xrsem, yssem, yfsem, yrsem, psem, qsem, asem, dsem, dr, usem, ur, zsem, zrecv,
):
    s = lax.axis_index("section")
    e, d, z, y, right, left, opp = places()

    def near_x(k):
        return {"dp": (d + k) % 4}

    def near_y(k):
        return {"expert": z * NY + (y + k) % 4}

    def near_z(k):
        return {"expert": ((z + k) % NZ) * NY + y}

    barrier = pltpu.get_barrier_semaphore()
    peers = [{"section": 1 - s}]
    for near in (near_x, near_y):
        for k in (1, 3):
            peers += [{**near(k), "section": 0}, {**near(k), "section": 1}]
        peers.append(near(2))
    peers += [near_z(k) for k in range(1, NZ)]
    for peer in peers:
        pl.semaphore_signal(barrier, inc=1, device_id=peer, device_id_type=MESH)
    x_ring = Ring(s, d, near_x, xs, xg, xr, xssem, xfsem, xrsem)
    y_ring = Ring(s, y, near_y, ys, yg, yr, yssem, yfsem, yrsem)
    factors = ((n0, dl0, la0, dq0, dr0, mx0), (n1, dl1, la1, dq1, dr1, mx1))
    by_x, by_y, small = quarter_matrix(True), quarter_matrix(False), small_matrix()
    for layer, (n, dl, la, dq, _, _) in enumerate(factors):
        lay_out(n[...], by_x, xs, layer)
        moved = dot(la[...], small).astype(bf16)
        for q in range(4):
            xs[layer, q, :, 1024:1280] = dl[...]
            xs[layer, q, :, 1280:1536] = moved[:, q * 256 : (q + 1) * 256]
            xs[layer, q, :, 1536:1792] = dq[...]
    pl.semaphore_wait(barrier, len(peers))
    x_ring.start(0)
    x_ring.start(1)
    for layer, (_, _, _, _, dres, mx) in enumerate(factors):
        lay_out(dres[...], by_y, ys, layer)
        for q in range(4):
            ys[layer, q, :, 1024:1280] = mx[...]
    y_ring.start(0)
    y_ring.start(1)
    x_ring.own()
    y_ring.own()

    for k, (out, first_layer, second_layer) in enumerate(((act_o, act0, act1), (grad_o, grad0, grad1))):
        for here, keep, give in ((0, first_layer, second_layer), (1, second_layer, first_layer)):

            @pl.when(s == here)
            def _():
                pltpu.make_async_copy(keep, out.at[s], asem.at[k]).start()
                remote(give, out.at[s], psem, qsem.at[k], {"section": 1 - s}).start()

    x_ring.relay()
    y_ring.relay()

    def rows(ring, start, width):
        got = ring.got
        return jnp.concatenate(
            [got[m, q, :, start : start + width] for m in range(2) for q in range(4)], axis=0
        )

    x_ring.arrive()
    total = t_times(rows(x_ring, 0, 1024), rows(x_ring, 1024, 256)).astype(bf16)
    total_qk = t_times(rows(x_ring, 1280, 256), rows(x_ring, 1536, 256)).astype(bf16)
    for q in range(4):
        for c in range(4):
            td[q, c * 64 : (c + 1) * 64, :] = total[c * 256 + q * 64 : c * 256 + (q + 1) * 64]
        td[q, 256:320, :] = total_qk[q * 64 : (q + 1) * 64]
    for k in (2, 1, 3):
        remote(td.at[(y + k) % 4], sd.at[y], dsem, dr.at[4 - k - 1], near_y(k)).start()
    y_ring.arrive()
    total = t_times(rows(y_ring, 0, 1024), rows(y_ring, 1024, 256)).astype(bf16)
    for q in range(4):
        for c in range(4):
            tu[q, c * 64 : (c + 1) * 64, :] = total[c * 256 + q * 64 : c * 256 + (q + 1) * 64]
    for k in (2, 1, 3):
        remote(tu.at[(d + k) % 4], su.at[d], usem, ur.at[4 - k - 1], near_x(k)).start()

    def gathered(buf, recv, position):
        for k in (1, 2, 3):
            ref = buf.at[(position + k) % 4]
            remote(ref, ref, dsem, recv.at[k - 1], near_x(1)).wait_recv()
        return [buf[(position + k) % 4] for k in (1, 2, 3)]

    summed = fold([td[y]] + gathered(sd, dr, y)).astype(bf16)
    for k in range(NZ):
        zd[k, 0:32, :] = summed[k * 32 : (k + 1) * 32]
        zd[k, 32:40, :] = summed[256 + k * 8 : 264 + k * 8]
    for k in range(1, NZ):
        remote(zd.at[(z + k) % NZ], zr.at[z], zsem.at[0], zrecv.at[0, NZ - k - 1], near_z(k)).start()
    summed = fold([tu[d]] + gathered(su, ur, d)).astype(bf16)
    for k in range(NZ):
        zu[k] = summed[k * 32 : (k + 1) * 32]
    for k in range(1, NZ):
        remote(zu.at[(z + k) % NZ], zv.at[z], zsem.at[1], zrecv.at[1, NZ - k - 1], near_z(k)).start()

    def last(own, buf, which):
        for k in range(1, NZ):
            ref = buf.at[(z + k) % NZ]
            remote(ref, ref, zsem.at[0], zrecv.at[which, k - 1], near_z(1)).wait_recv()
        return fold([own[z]] + [buf[(z + k) % NZ] for k in range(1, NZ)])

    mine = last(zd, zr, 0)
    down_o[...] = mine[0:28]
    qk_o[...] = mine[32:34]
    mine = last(zu, zv, 1)
    up_o[...] = mine[0:28]

    x_ring.drain()
    y_ring.drain()
    for k, (out, some) in enumerate(((act_o, act0), (grad_o, grad0))):
        pltpu.make_async_copy(some, out.at[s], asem.at[k]).wait()
        remote(some, out.at[1 - s], psem, qsem.at[k], {"section": 1 - s}).wait_recv()
    whole = act_o
    remote(whole, whole, psem, qsem.at[0], {"section": 1 - s}).wait_send()
    ref = td.at[pl.ds(0, 3)]
    remote(ref, ref, dsem, dr.at[0], near_x(1)).wait_send()
    ref = tu.at[pl.ds(0, 3)]
    remote(ref, ref, usem, ur.at[0], near_x(1)).wait_send()
    ref = zd.at[pl.ds(0, NZ - 1)]
    remote(ref, ref, zsem.at[0], dr.at[0], near_x(1)).wait_send()
    ref = zu.at[pl.ds(0, NZ - 1)]
    remote(ref, ref, zsem.at[1], dr.at[0], near_x(1)).wait_send()


def weight_grads(layer0, layer1):
    dma = pltpu.SemaphoreType.DMA
    ring_sems = [dma, dma((2, 4)), dma((2,))]
    return pl.pallas_call(
        grads_kernel,
        name="weight_grads",
        out_shape=[
            jax.ShapeDtypeStruct((2, SEQ, WIDTH), bf16),
            jax.ShapeDtypeStruct((2, SEQ, WIDTH), bf16),
            jax.ShapeDtypeStruct((28, LAT), f32),
            jax.ShapeDtypeStruct((2, LAT), f32),
            jax.ShapeDtypeStruct((28, LAT), f32),
        ],
        in_specs=[VMEM] * 16,
        out_specs=[VMEM] * 5,
        scratch_shapes=[
            pltpu.VMEM((2, 4, SEQ, ROUND), bf16),
            pltpu.VMEM((2, 4, SEQ, ROUND), bf16),
            pltpu.VMEM((2, SEQ, ROUND), bf16),
            pltpu.VMEM((2, 4, SEQ, SIDE), bf16),
            pltpu.VMEM((2, 4, SEQ, SIDE), bf16),
            pltpu.VMEM((2, SEQ, SIDE), bf16),
            pltpu.VMEM((4, 320, LAT), bf16),
            pltpu.VMEM((4, 320, LAT), bf16),
            pltpu.VMEM((NZ, 40, LAT), bf16),
            pltpu.VMEM((NZ, 40, LAT), bf16),
            pltpu.VMEM((4, 256, LAT), bf16),
            pltpu.VMEM((4, 256, LAT), bf16),
            pltpu.VMEM((NZ, 32, LAT), bf16),
            pltpu.VMEM((NZ, 32, LAT), bf16),
        ]
        + ring_sems * 2
        + [dma, dma((2,)), dma((2,)), dma, dma((3,)), dma, dma((3,)), dma((2,)), dma((2, NZ - 1))],
        compiler_params=pltpu.CompilerParams(collective_id=2, has_side_effects=True),
    )(*layer0, *layer1)


def swap(value):
    return lax.ppermute(value, "section", [(0, 1), (1, 0)])


def body(x_in, dy_out, routes, gates, w_down, w_qk, w_up, e_gate, e_up, e_down):
    section = lax.axis_index("section")
    attn_own = (w_down[0], w_qk[0], w_up[0])
    experts_own = (e_gate[0, 0], e_up[0, 0], e_down[0, 0])
    attn = attn_own + tuple(swap(w) for w in attn_own)
    def both_layers(table):
        other = swap(lax.dynamic_index_in_dim(table, 1 - section, 0, keepdims=False))
        own = lax.dynamic_index_in_dim(table, section, 0, keepdims=False)
        return (jnp.where(section == 0, own, other), jnp.where(section == 0, other, own))

    route_cols = both_layers(routes[0, :, 0])
    gate_cols = both_layers(gates[0, :, 0])
    route_rows = tuple(r.reshape(1, SEQ) for r in route_cols)

    whole = {
        "x": (x_in[:, 0], VMEM),
        "dy": (dy_out[:, 0], VMEM),
        **{f"route_row{k}": (route_rows[k], VMEM) for k in range(2)},
        **{f"route_col{k}": (route_cols[k], VMEM) for k in range(2)},
        **{f"gate_col{k}": (gate_cols[k], VMEM) for k in range(2)},
        **named("attn", [(w, ANY) for w in attn]),
        **named("expert", [(w, ANY) for w in experts_own]),
    }
    kept = fused(
        forward_run,
        "forward",
        whole,
        {
            "act0": shaped(*TOKENS),
            **kept_shapes(0),
            **kept_shapes(1),
            "gate0": shaped(*PRE, dtype=f32),
            "up0": shaped(*PRE, dtype=f32),
            "part1": shaped(*ROWS),
            "homeb": shaped(*HOME),
        },
        {
            **COMMON,
            **Experts.scratch(2),
            "hidden": pltpu.VMEM(PRE, bf16),
            **dispatch_scratch("a"),
            **dispatch_scratch("b"),
            **dispatch_scratch("c"),
            **combine_scratch("a"),
            **combine_scratch("b", skip=("homeb",)),
        },
        0,
    )
    part1, back1 = kept.pop("part1"), kept.pop("homeb")
    done = fused(
        backward_run,
        "backward",
        {
            **whole,
            **{k: (v, VMEM) for k, v in kept.items()},
            "parta": (part1, VMEM),
            "back1": (back1, VMEM),
        },
        {"act1": shaped(*TOKENS), **factor_shapes(1), **factor_shapes(0)},
        {
            **COMMON,
            **Experts.scratch(1),
            **dispatch_scratch("a"),
            **combine_scratch("a", skip=("parta",)),
            **combine_scratch("b"),
        },
        1,
    )
    layers = [
        tuple({**kept, **done}[f"{k}{layer}"] for k in ("n", "dl", "latent", "dq", "dr", "mixed", "act", "grad"))
        for layer in range(2)
    ]
    activations, grads_in, g_down, g_qk, g_up_t = weight_grads(*layers)
    return (
        activations[None, :, None],
        grads_in[None, :, None],
        g_down[None],
        g_qk[None],
        g_up_t[None],
    )


def solution(mesh):
    placed = (
        P(None, ("expert", "dp"), None, None),
        P(None, ("expert", "dp"), None, None),
        P("section", None, ("expert", "dp"), None, None),
        P("section", None, ("expert", "dp"), None, None),
        P("section", None, None),
        P("section", None, None),
        P("section", None, None),
        P("section", "expert", None, "dp"),
        P("section", "expert", None, "dp"),
        P("section", "expert", "dp", None),
    )
    return jax.shard_map(
        body,
        mesh=mesh,
        in_specs=placed,
        out_specs=(
            P("section", None, ("expert", "dp"), None, None),
            P("section", None, ("expert", "dp"), None, None),
            P("section", ("expert", "dp"), None),
            P("section", ("expert", "dp"), None),
            P("section", ("expert", "dp"), None),
        ),
        check_vma=False,
    )
```

```python
import functools

import jax
import jax.numpy as jnp
from jax import lax
from jax.experimental import pallas as pl
from jax.experimental.pallas import tpu as pltpu
from jax.sharding import PartitionSpec as P

epsilon = 1e-06
WIDTH = 3584
LAT = 256
FF = 256
SEQ = 64
EXPERTS = 32
DP = 4
CAP = 3
NZ = 8
NY = 4
PIECE = 896
PIECES = 4
BLOCK = (PIECES, CAP * PIECE)
PACKED = PIECES * EXPERTS
ORDER = (0, 1, 7, 2, 6, 3, 5, 4)
MESH = pl.DeviceIdType.MESH
VMEM = pl.BlockSpec(memory_space=pltpu.VMEM)
ANY = pl.BlockSpec(memory_space=pl.ANY)
bf16 = jnp.bfloat16
f32 = jnp.float32


def dot(left, right):
    return jnp.dot(left, right, preferred_element_type=f32)


def times_t(left, right):
    return lax.dot_general(left, right, (((1,), (1,)), ((), ())), preferred_element_type=f32)


def t_times(left, right):
    return lax.dot_general(left, right, (((0,), (0,)), ((), ())), preferred_element_type=f32)


def rms_norm(values):
    inv_rms = lax.rsqrt(jnp.mean(values * values, axis=-1, keepdims=True) + epsilon)
    return (values * inv_rms, inv_rms)


def rms_back(normed, inv_rms, upstream):
    return inv_rms * (upstream - normed * jnp.mean(upstream * normed, axis=-1, keepdims=True))


def silu_parts(gate_pre):
    sigmoid = jax.nn.sigmoid(gate_pre)
    return (gate_pre * sigmoid, sigmoid * (1.0 + gate_pre * (1.0 - sigmoid)))


def spread_matrix():
    rows = lax.broadcasted_iota(jnp.int32, (PACKED, PACKED), 0)
    cols = lax.broadcasted_iota(jnp.int32, (PACKED, PACKED), 1)
    return ((rows % PIECES) * EXPERTS + rows // PIECES == cols).astype(f32).astype(bf16)


def gather_matrix():
    rows = lax.broadcasted_iota(jnp.int32, (PACKED, PACKED), 0)
    cols = lax.broadcasted_iota(jnp.int32, (PACKED, PACKED), 1)
    return ((cols % PIECES) * EXPERTS + cols // PIECES == rows).astype(f32).astype(bf16)


def slot_rows(route_row):
    experts = lax.broadcasted_iota(jnp.int32, (EXPERTS, SEQ), 0)
    hot = (experts == route_row).astype(f32)
    before = lax.broadcasted_iota(jnp.int32, (SEQ, SEQ), 0) < lax.broadcasted_iota(
        jnp.int32, (SEQ, SEQ), 1
    )
    rank = dot(hot.astype(bf16), before.astype(f32).astype(bf16))
    return jnp.concatenate(
        [(hot * (rank == float(s)).astype(f32)).astype(bf16) for s in range(CAP)], axis=0
    )


def slot_columns(route_col):
    experts = lax.broadcasted_iota(jnp.int32, (SEQ, EXPERTS), 1)
    hot = (experts == route_col).astype(f32)
    before = lax.broadcasted_iota(jnp.int32, (SEQ, SEQ), 0) > lax.broadcasted_iota(
        jnp.int32, (SEQ, SEQ), 1
    )
    rank = dot(before.astype(f32).astype(bf16), hot.astype(bf16))
    return jnp.concatenate(
        [(hot * (rank == float(s)).astype(f32)).astype(bf16) for s in range(CAP)], axis=1
    )


def pack_tokens(values_b, route_row, packed_ref, blocks_ref):
    picked = dot(slot_rows(route_row), values_b).astype(bf16)
    for s in range(CAP):
        for r in range(PIECES):
            packed_ref[r * EXPERTS : (r + 1) * EXPERTS, s * PIECE : (s + 1) * PIECE] = picked[
                s * EXPERTS : (s + 1) * EXPERTS, r * PIECE : (r + 1) * PIECE
            ]
    blocks_ref[...] = dot(spread_matrix(), packed_ref[...]).astype(bf16).reshape(HOME)


def unpack_tokens(blocks_ref, route_col, token_ref):
    packed = dot(gather_matrix(), blocks_ref[...].reshape(PACKED, BLOCK[1])).astype(bf16)
    columns = slot_columns(route_col)
    for r in range(PIECES):
        stacked = jnp.concatenate(
            [
                packed[r * EXPERTS : (r + 1) * EXPERTS, s * PIECE : (s + 1) * PIECE]
                for s in range(CAP)
            ],
            axis=0,
        )
        token_ref[:, r * PIECE : (r + 1) * PIECE] = dot(columns, stacked)


def places():
    e = lax.axis_index("expert")
    d = lax.axis_index("dp")
    return e, d, e // NY, e % NY, (d + 1) % DP, (d + DP - 1) % DP, (d + 2) % DP


def greet(e, right, left):
    barrier = pltpu.get_barrier_semaphore()
    for k in range(1, EXPERTS):
        pl.semaphore_signal(
            barrier, inc=1, device_id={"expert": (e + k) % EXPERTS}, device_id_type=MESH
        )
    for side in (right, left):
        pl.semaphore_signal(barrier, inc=1, device_id={"dp": side}, device_id_type=MESH)
    partner = {"section": 1 - lax.axis_index("section")}
    pl.semaphore_signal(barrier, inc=1, device_id=partner, device_id_type=MESH)


def greeted():
    pl.semaphore_wait(pltpu.get_barrier_semaphore(), EXPERTS + 2)


def remote(src, dst, send, recv, where):
    return pltpu.make_async_remote_copy(
        src_ref=src, dst_ref=dst, send_sem=send, recv_sem=recv, device_id=where, device_id_type=MESH
    )


class Dispatch:
    sems = (
        pltpu.SemaphoreType.DMA,
        pltpu.SemaphoreType.DMA,
        pltpu.SemaphoreType.DMA((NZ,)),
        pltpu.SemaphoreType.DMA((NZ,)),
        pltpu.SemaphoreType.DMA((NZ,)),
        pltpu.SemaphoreType.DMA((NZ,)),
    )

    def __init__(self, blk, rows, sems):
        self.blk, self.rows = blk, rows
        self.s1, self.sx, self.r1, self.rl, self.rr, self.ro = sems
        self.e, self.d, self.z, self.y, self.right, self.left, self.opp = places()

    def start(self):
        for j in ORDER:
            for dy in range(NY):
                spot = self.rows.at[self.d * EXPERTS + self.e]
                if j == 0 and dy == 0:
                    pltpu.make_async_copy(self.blk.at[self.e], spot, self.r1.at[0]).start()
                else:
                    peer = ((self.z + j) % NZ) * NY + (self.y + dy) % NY
                    remote(
                        self.blk.at[peer], spot, self.s1, self.r1.at[(NZ - j) % NZ], {"expert": peer}
                    ).start()

    def group(self, owner, j):
        return self.rows.at[pl.ds(owner * EXPERTS + ((self.z + j) % NZ) * NY, NY)]

    def arrived(self, ref, sem):
        remote(ref, ref, self.s1, sem, {"dp": self.right}).wait_recv()

    def forward(self, i):
        j = ORDER[i]
        mine = self.group(self.d, j)
        self.arrived(mine, self.r1.at[j])
        remote(mine, mine, self.sx, self.rl.at[j], {"dp": self.right}).start()
        remote(mine, mine, self.sx, self.rr.at[j], {"dp": self.left}).start()

    def relay(self, i):
        j = ORDER[i]
        owner, sem, to = (
            (self.left, self.rl, self.right) if i % 2 == 0 else (self.right, self.rr, self.left)
        )
        ref = self.group(owner, j)
        self.arrived(ref, sem.at[j])
        remote(ref, ref, self.sx, self.ro.at[j], {"dp": to}).start()

    def wait_right(self):
        for i, j in enumerate(ORDER):
            if i % 2 == 0:
                self.arrived(self.group(self.right, j), self.rr.at[j])

    def wait_left(self):
        for i, j in enumerate(ORDER):
            if i % 2 == 1:
                self.arrived(self.group(self.left, j), self.rl.at[j])

    def wait_far(self):
        for j in ORDER:
            self.arrived(self.group(self.opp, j), self.ro.at[j])

    def chunks(self, use, near):
        @pl.loop(0, DP)
        def _(k):
            pl.when(k == 1)(self.wait_right)
            pl.when(k == 2)(self.wait_left)
            pl.when(k == 3)(self.wait_far)
            use((self.d + k + k // 2 - 2 * (k // 3)) % DP)
            pl.when(k == 2)(near)

    def drain(self):
        sent = self.blk.at[pl.ds(0, EXPERTS - 1)]
        remote(sent, sent, self.s1, self.r1.at[0], {"dp": self.right}).wait_send()
        sent = self.rows.at[pl.ds(0, 3 * EXPERTS)]
        remote(sent, sent, self.sx, self.r1.at[0], {"dp": self.right}).wait_send()


class Combine:
    sems = (
        pltpu.SemaphoreType.DMA,
        pltpu.SemaphoreType.DMA,
        pltpu.SemaphoreType.DMA((NZ,)),
        pltpu.SemaphoreType.DMA((NZ,)),
        pltpu.SemaphoreType.DMA((NZ,)),
        pltpu.SemaphoreType.DMA,
    )
    buffers = (pltpu.VMEM((EXPERTS, *BLOCK), bf16),) * 5

    def __init__(self, part, out, buffers, sems):
        self.part, self.out = part, out
        self.relayed, self.relay_sum, self.from_left, self.from_right, self.final = buffers
        self.sx, self.s1, self.ra, self.rl, self.rr, self.rh = sems
        self.e, self.d, self.z, self.y, self.right, self.left, self.opp = places()

    def group(self, owner, j):
        return self.part.at[pl.ds(owner * EXPERTS + ((self.z + j) % NZ) * NY, NY)]

    def spot(self, ref, i):
        return ref.at[pl.ds(i * NY, NY)]

    def arrived(self, ref, sem):
        remote(ref, ref, self.s1, sem, {"dp": self.right}).wait_recv()

    def start_far(self):
        for i, j in enumerate(ORDER):
            side = self.right if i % 2 == 0 else self.left
            remote(
                self.group(self.opp, j), self.spot(self.relayed, i), self.sx, self.ra.at[i], {"dp": side}
            ).start()

    def start_near(self):
        for i, j in enumerate(ORDER):
            if i % 2 == 0:
                ref, to, sem, side = self.left, self.from_right, self.rr, self.left
            else:
                ref, to, sem, side = self.right, self.from_left, self.rl, self.right
            remote(self.group(ref, j), self.spot(to, i), self.sx, sem.at[i], {"dp": side}).start()

    def relay(self, i):
        j = ORDER[i]
        self.arrived(self.spot(self.relayed, i), self.ra.at[i])
        side, to, sem = (
            (self.right, self.from_left, self.rl)
            if i % 2 == 0
            else (self.left, self.from_right, self.rr)
        )
        self.spot(self.relay_sum, i)[...] = (
            self.spot(self.relayed, i)[...].astype(f32) + self.group(side, j)[...].astype(f32)
        ).astype(bf16)
        remote(
            self.spot(self.relay_sum, i), self.spot(to, i), self.sx, sem.at[i], {"dp": side}
        ).start()

    def finish(self, i):
        j = ORDER[i]
        self.arrived(self.spot(self.from_left, i), self.rl.at[i])
        self.arrived(self.spot(self.from_right, i), self.rr.at[i])
        self.spot(self.final, i)[...] = (
            self.group(self.d, j)[...].astype(f32)
            + self.spot(self.from_left, i)[...].astype(f32)
            + self.spot(self.from_right, i)[...].astype(f32)
        ).astype(bf16)
        for dy in range(NY):
            yy = (self.y + dy) % NY
            spot = self.out.at[self.e]
            if j == 0 and dy == 0:
                pltpu.make_async_copy(self.final.at[i * NY + yy], spot, self.rh).start()
            else:
                peer = ((self.z + j) % NZ) * NY + yy
                remote(
                    self.final.at[i * NY + yy], spot, self.s1, self.rh, {"expert": peer}
                ).start()

    def arrive(self):
        self.arrived(self.out, self.rh)

    def drain(self):
        sent = self.part.at[pl.ds(0, 3 * EXPERTS)]
        remote(sent, sent, self.sx, self.rh, {"dp": self.right}).wait_send()
        sent = self.part.at[pl.ds(0, EXPERTS - 1)]
        remote(sent, sent, self.s1, self.rh, {"dp": self.right}).wait_send()


def fetch(layer, pairs, sems):
    mine = lax.axis_index("section") == layer
    for k, (own, other, dst) in enumerate(pairs):

        @pl.when(mine)
        def _():
            pltpu.make_async_copy(own, dst, sems.at[k]).start()

        @pl.when(jnp.logical_not(mine))
        def _():
            pltpu.make_async_copy(other, dst, sems.at[k]).start()

    def wait(k):
        own, _, dst = pairs[k]
        pltpu.make_async_copy(own, dst, sems.at[k]).wait()

    return wait


def attend(
    inputs, route_row, wd, wq, wu, wait, packed, blocks, residual, latent_o, queries_o, probs_o, mixed_o
):
    normed, _ = rms_norm(inputs.astype(f32))
    wait(0)
    latent = dot(normed.astype(bf16), wd[...]).astype(bf16)
    wait(1)
    queries = dot(latent, wq[...]).astype(bf16)
    scores = times_t(queries, latent) * (LAT ** (-0.5))
    causal = lax.broadcasted_iota(jnp.int32, (SEQ, SEQ), 0) >= lax.broadcasted_iota(
        jnp.int32, (SEQ, SEQ), 1
    )
    scores = jnp.where(causal, scores, -1e30)
    exponent = jnp.exp(scores - jnp.max(scores, axis=-1, keepdims=True))
    probs = exponent / jnp.sum(exponent, axis=-1, keepdims=True)
    mixed = dot(probs.astype(bf16), latent).astype(bf16)
    wait(2)
    resid = (inputs.astype(f32) + dot(mixed, wu[...])).astype(bf16)
    residual[...] = resid
    latent_o[...] = latent
    queries_o[...] = queries
    probs_o[...] = probs
    mixed_o[...] = mixed
    normed2, _ = rms_norm(resid.astype(f32))
    pack_tokens(normed2.astype(bf16), route_row, packed, blocks)


def attend_back(
    upstream, inputs, resid, latent, queries, probs, mixed, w, wait, tokens, normed_o, d_latent_o,
    d_queries_o, d_resid_o, grad,
):
    normed2, inv2 = rms_norm(resid.astype(f32))
    d_resid = upstream.astype(f32) + rms_back(normed2, inv2, tokens[...])
    d_resid_b = d_resid.astype(bf16)
    d_resid_o[...] = d_resid_b
    tokens[...] = d_resid
    wd, wq, wu = w
    wait(2)
    d_mixed = times_t(d_resid_b, wu[...]).astype(bf16)
    d_probs = times_t(d_mixed, latent)
    d_scores = (
        probs * (d_probs - jnp.sum(d_probs * probs, axis=-1, keepdims=True)) * (LAT ** (-0.5))
    ).astype(bf16)
    d_queries = dot(d_scores, latent).astype(bf16)
    wait(1)
    d_latent = (
        t_times(probs.astype(bf16), d_mixed)
        + t_times(d_scores, queries)
        + times_t(d_queries, wq[...])
    ).astype(bf16)
    wait(0)
    d_normed = times_t(d_latent, wd[...])
    normed, inv = rms_norm(inputs.astype(f32))
    normed_o[...] = normed.astype(bf16)
    d_latent_o[...] = d_latent
    d_queries_o[...] = d_queries
    grad[...] = (tokens[...] + rms_back(normed, inv, d_normed)).astype(bf16)


CHUNK = CAP * EXPERTS


def unpack_rows(rows, wide, g):
    packed = dot(
        gather_matrix(), rows[pl.ds(g * EXPERTS, EXPERTS)].reshape(PACKED, BLOCK[1])
    ).astype(bf16)
    for s in range(CAP):
        for r in range(PIECES):
            wide[s * EXPERTS : (s + 1) * EXPERTS, r * PIECE : (r + 1) * PIECE] = packed[
                r * EXPERTS : (r + 1) * EXPERTS, s * PIECE : (s + 1) * PIECE
            ]
    return wide[...]


def pack_rows(piece, packed, out, g):
    for r in range(PIECES):
        rows = piece(slice(r * PIECE, (r + 1) * PIECE)).astype(bf16)
        for s in range(CAP):
            packed[r * EXPERTS : (r + 1) * EXPERTS, s * PIECE : (s + 1) * PIECE] = rows[
                s * EXPERTS : (s + 1) * EXPERTS
            ]
    out[pl.ds(g * EXPERTS, EXPERTS)] = (
        dot(spread_matrix(), packed[...]).astype(bf16).reshape(EXPERTS, *BLOCK)
    )


def chunk_rows(g):
    return pl.ds(pl.multiple_of(g * CHUNK, CHUNK), CHUNK)


def expert_out(hidden, dw):
    return lambda cols: dot(hidden, dw[:, cols])


def expert_back(rows, gate_pre, up_pre, gw, uw, dw):
    d_hidden = times_t(rows, dw[...])
    activated, slope = silu_parts(gate_pre)
    d_gate = (d_hidden * up_pre * slope).astype(bf16)
    d_up = (d_hidden * activated).astype(bf16)
    return lambda cols: times_t(d_gate, gw[cols, :]) + times_t(d_up, uw[cols, :])


class Refs:
    def __init__(self, names, refs):
        for name, ref in zip(names, refs, strict=True):
            setattr(self, name, ref)

    def some(self, prefix, count):
        return tuple(getattr(self, f"{prefix}{k}") for k in range(count))


def named(prefix, items):
    return {f"{prefix}{k}": item for k, item in enumerate(items)}


def fused(run, name, ins, outs, scratch, number):
    names = [*ins, *outs, *scratch]

    def kernel(*refs):
        run(Refs(names, refs))

    results = pl.pallas_call(
        kernel,
        name=name,
        out_shape=list(outs.values()),
        in_specs=[spec for _, spec in ins.values()],
        out_specs=[VMEM] * len(outs),
        scratch_shapes=list(scratch.values()),
        compiler_params=pltpu.CompilerParams(
            collective_id=number, has_side_effects=True, vmem_limit_bytes=60 * 1024 * 1024
        ),
    )(*[array for array, _ in ins.values()])
    return dict(zip(outs, results))


def shaped(*shape, dtype=bf16):
    return jax.ShapeDtypeStruct(shape, dtype)


TOKENS = (SEQ, WIDTH)
ROWS = (DP * EXPERTS, *BLOCK)
HOME = (EXPERTS, *BLOCK)
PRE = (CAP * DP * EXPERTS, FF)
COMMON = {
    "tokens": pltpu.VMEM(TOKENS, f32),
    "wide": pltpu.VMEM((CHUNK, WIDTH), bf16),
    "packed": pltpu.VMEM((PACKED, BLOCK[1]), bf16),
    "w0": pltpu.VMEM((WIDTH, LAT), bf16),
    "w1": pltpu.VMEM((LAT, LAT), bf16),
    "w2": pltpu.VMEM((LAT, WIDTH), bf16),
    "wsem": pltpu.SemaphoreType.DMA((3,)),
}
EXPERT_WEIGHTS = ((WIDTH, FF), (WIDTH, FF), (FF, WIDTH))


def fetch_attn(refs, layer):
    attn = refs.some("attn", 6)
    return fetch(layer, [(attn[k], attn[3 + k], getattr(refs, f"w{k}")) for k in range(3)], refs.wsem)


class Experts:
    @staticmethod
    def scratch(layers):
        return {
            **named("v", [pltpu.VMEM((layers, *shape), bf16) for shape in EXPERT_WEIGHTS]),
            "vsem": pltpu.SemaphoreType.DMA((layers, 3)),
            "vsent": pltpu.SemaphoreType.DMA((3,)),
        }

    def __init__(self, refs, layers):
        self.s = lax.axis_index("section")
        self.own = refs.some("expert", 3)
        self.v = refs.some("v", 3)
        self.sem, self.sent, self.layers = refs.vsem, refs.vsent, layers

    def each(self, act):
        def run():
            for k in range(3):
                act(k)

        if self.layers == 1:
            pl.when(self.s == 0)(run)
        else:
            run()

    def place(self):
        return self.s if self.layers == 2 else 0

    def copy(self, k):
        return pltpu.make_async_copy(
            self.own[k], self.v[k].at[self.place()], self.sem.at[self.place(), k]
        )

    def give(self, k):
        return remote(
            self.own[k],
            self.v[k].at[self.place()],
            self.sent.at[k],
            self.sem.at[self.place(), k],
            {"section": 1 - self.s},
        )

    def start(self):
        self.each(lambda k: self.copy(k).start())

    def send(self):
        self.each(lambda k: self.give(k).start())

    def drain(self):
        self.each(lambda k: self.give(k).wait_send())

    def ready(self, layer):
        for k in range(3):
            pltpu.make_async_copy(
                self.own[k], self.v[k].at[layer], self.sem.at[layer, k]
            ).wait()
        return [ref.at[layer] for ref in self.v]


def dispatch_of(refs, tag):
    return Dispatch(
        getattr(refs, "blk" + tag), getattr(refs, "rows" + tag), refs.some("ds" + tag + "_", 6)
    )


def dispatch_scratch(tag):
    return {
        "blk" + tag: pltpu.VMEM(HOME, bf16),
        "rows" + tag: pltpu.VMEM(ROWS, bf16),
        **named("ds" + tag + "_", Dispatch.sems),
    }


def combine_of(refs, tag):
    return Combine(
        getattr(refs, "part" + tag),
        getattr(refs, "home" + tag),
        refs.some("cb" + tag + "_", 5),
        refs.some("cs" + tag + "_", 6),
    )


def combine_scratch(tag, skip=()):
    whole = {
        "part" + tag: pltpu.VMEM(ROWS, bf16),
        "home" + tag: pltpu.VMEM(HOME, bf16),
        **named("cb" + tag + "_", Combine.buffers),
        **named("cs" + tag + "_", Combine.sems),
    }
    return {k: v for k, v in whole.items() if k not in skip}


def kept_shapes(layer):
    return {
        f"resid{layer}": shaped(*TOKENS),
        f"latent{layer}": shaped(SEQ, LAT),
        f"queries{layer}": shaped(SEQ, LAT),
        f"probs{layer}": shaped(SEQ, SEQ, dtype=f32),
        f"mixed{layer}": shaped(SEQ, LAT),
    }


def kept_refs(refs, layer):
    return [getattr(refs, f"{k}{layer}") for k in ("resid", "latent", "queries", "probs", "mixed")]


def forward_run(refs):
    e, _, _, _, right, left, _ = places()
    section = lax.axis_index("section")
    greet(e, right, left)
    wait_w = fetch_attn(refs, 0)
    experts = Experts(refs, 2)
    experts.start()
    first, early, second = (dispatch_of(refs, tag) for tag in ("a", "b", "c"))
    out0, back1 = combine_of(refs, "a"), combine_of(refs, "b")
    w = refs.some("w", 3)

    attend(
        refs.x[section], refs.route_row0[...], *w, wait_w, refs.packed, refs.blka,
        *kept_refs(refs, 0),
    )
    wait_w = fetch_attn(refs, 1)
    greeted()
    first.start()
    experts.send()
    scaled = (refs.gate_col1[...] * refs.dy[section].astype(f32)).astype(bf16)
    pack_tokens(scaled, refs.route_row1[...], refs.packed, refs.blkb)
    for i in range(NZ):
        first.forward(i)
        if i >= 2:
            first.relay(i - 2)
        if i == 5:
            early.start()
    first.relay(6)
    first.relay(7)
    gw, uw, dw = experts.ready(0)

    def forward0(g):
        at = chunk_rows(g)
        rows = unpack_rows(refs.rowsa, refs.wide, g)
        gate_pre, up_pre = dot(rows, gw[...]), dot(rows, uw[...])
        refs.gate0[at, :] = gate_pre
        refs.up0[at, :] = up_pre
        hidden = (silu_parts(gate_pre)[0] * up_pre).astype(bf16)
        pack_rows(expert_out(hidden, dw), refs.packed, out0.part, g)

    first.chunks(forward0, out0.start_near)
    out0.start_far()
    for i in range(NZ):
        out0.relay(i)
    for i in range(NZ):
        early.forward(i)
    for i in range(NZ):
        out0.finish(i)
    out0.arrive()

    unpack_tokens(refs.homea, refs.route_col0[...], refs.tokens)
    act0 = (refs.resid0[...].astype(f32) + refs.gate_col0[...] * refs.tokens[...]).astype(bf16)
    refs.act0[...] = act0
    attend(act0, refs.route_row1[...], *w, wait_w, refs.packed, refs.blkc, *kept_refs(refs, 1))
    second.start()
    for i in range(NZ):
        early.relay(i)
    for i in range(NZ):
        second.forward(i)
        if i >= 2:
            second.relay(i - 2)
    second.relay(6)
    second.relay(7)
    early.wait_right()
    early.wait_left()
    early.wait_far()
    gw1, uw1, dw1 = experts.ready(1)

    def both1(g):
        at = chunk_rows(g)
        rows = unpack_rows(refs.rowsc, refs.wide, g)
        gate_pre, up_pre = dot(rows, gw1[...]), dot(rows, uw1[...])
        refs.hidden[at, :] = (silu_parts(gate_pre)[0] * up_pre).astype(bf16)
        rows = unpack_rows(refs.rowsb, refs.wide, g)
        pack_rows(
            expert_back(rows, gate_pre, up_pre, gw1, uw1, dw1), refs.packed, back1.part, g
        )

    def out1(g):
        pack_rows(expert_out(refs.hidden[chunk_rows(g), :], dw1), refs.packed, refs.part1, g)

    second.chunks(both1, back1.start_near)
    back1.start_far()
    pl.loop(0, 2)(out1)
    for i in range(NZ):
        back1.relay(i)
    pl.loop(2, DP)(out1)
    for i in range(NZ):
        back1.finish(i)
    back1.arrive()
    for each in (first, early, second, out0, back1, experts):
        each.drain()


def backward_run(refs):
    e, _, _, _, right, left, _ = places()
    section = lax.axis_index("section")
    greet(e, right, left)
    wait_w = fetch_attn(refs, 1)
    experts = Experts(refs, 1)
    experts.start()
    again = dispatch_of(refs, "a")
    out1, back0 = combine_of(refs, "a"), combine_of(refs, "b")
    w = refs.some("w", 3)

    unpack_tokens(refs.back1, refs.route_col1[...], refs.tokens)
    greeted()
    out1.start_far()
    out1.start_near()
    experts.send()
    attend_back(
        refs.dy[section], refs.act0[...], *[ref[...] for ref in kept_refs(refs, 1)], w, wait_w,
        refs.tokens, refs.n1, refs.dl1, refs.dq1, refs.dr1, refs.grad1,
    )
    wait_w = fetch_attn(refs, 0)
    scaled = (refs.gate_col0[...] * refs.grad1[...].astype(f32)).astype(bf16)
    pack_tokens(scaled, refs.route_row0[...], refs.packed, refs.blka)
    again.start()
    for i in range(NZ):
        out1.relay(i)
    for i in range(NZ):
        again.forward(i)
        if i >= 2:
            again.relay(i - 2)
    again.relay(6)
    again.relay(7)
    for i in range(NZ):
        out1.finish(i)
    gw, uw, dw = experts.ready(0)

    def backward0(g):
        at = chunk_rows(g)
        rows = unpack_rows(refs.rowsa, refs.wide, g)
        pack_rows(
            expert_back(rows, refs.gate0[at, :], refs.up0[at, :], gw, uw, dw),
            refs.packed,
            back0.part,
            g,
        )

    again.chunks(backward0, back0.start_near)
    back0.start_far()
    for i in range(NZ):
        back0.relay(i)
    out1.arrive()
    unpack_tokens(refs.homea, refs.route_col1[...], refs.tokens)
    refs.act1[...] = (
        refs.resid1[...].astype(f32) + refs.gate_col1[...] * refs.tokens[...]
    ).astype(bf16)
    for i in range(NZ):
        back0.finish(i)
    back0.arrive()
    unpack_tokens(refs.homeb, refs.route_col0[...], refs.tokens)
    attend_back(
        refs.grad1[...], refs.x[section], *[ref[...] for ref in kept_refs(refs, 0)], w, wait_w,
        refs.tokens, refs.n0, refs.dl0, refs.dq0, refs.dr0, refs.grad0,
    )
    for each in (again, out1, back0, experts):
        each.drain()


def factor_shapes(layer):
    return {
        f"n{layer}": shaped(*TOKENS),
        f"dl{layer}": shaped(SEQ, LAT),
        f"dq{layer}": shaped(SEQ, LAT),
        f"dr{layer}": shaped(*TOKENS),
        f"grad{layer}": shaped(*TOKENS),
    }


ROUND = 1792
SIDE = 1280


def quarter_matrix(first_is_dp):
    out = lax.broadcasted_iota(jnp.int32, (1, 1024), 1)
    one, two, zz, i = out // 256, (out // 64) % 4, (out // 32) % 2, out % 32
    y, x = (two, one) if first_is_dp else (one, two)
    source = jnp.where(i < 28, zz * 448 + y * 112 + x * 28 + i, -1)
    return (lax.broadcasted_iota(jnp.int32, (896, 1024), 0) == source).astype(f32).astype(bf16)


def small_matrix():
    out = lax.broadcasted_iota(jnp.int32, (1, 1024), 1)
    x, y, z, i = out // 256, (out // 64) % 4, (out // 8) % 8, out % 8
    source = jnp.where(i < 2, z * 32 + y * 8 + x * 2 + i, -1)
    return (lax.broadcasted_iota(jnp.int32, (LAT, 1024), 0) == source).astype(f32).astype(bf16)


def lay_out(factor, matrix, sent, layer):
    stacked = jnp.concatenate([factor[:, c * 896 : (c + 1) * 896] for c in range(4)], axis=0)
    moved = dot(stacked, matrix).astype(bf16)
    for q in range(4):
        for c in range(4):
            sent[layer, q, :, c * 256 : (c + 1) * 256] = moved[
                c * SEQ : (c + 1) * SEQ, q * 256 : (q + 1) * 256
            ]


class Ring:
    def __init__(self, section, position, near, sent, got, relay, ssem, fsem, rsem):
        self.section, self.position, self.near = section, position, near
        self.sent, self.got, self.relay_buf = sent, got, relay
        self.ssem, self.fsem, self.rsem = ssem, fsem, rsem

    def start(self, layer):
        pos, s = self.position, self.section
        way = 1 if layer == 0 else 3
        remote(
            self.sent.at[layer, (pos + 2) % 4],
            self.relay_buf.at[layer],
            self.ssem,
            self.rsem.at[layer],
            self.near(way),
        ).start()
        for step, back in ((1, 1), (3, 0)):
            remote(
                self.sent.at[layer, (pos + step) % 4],
                self.got.at[s, pos],
                self.ssem,
                self.fsem.at[s, back],
                {**self.near(step), "section": layer},
            ).start()

    def own(self):
        pos, s = self.position, self.section
        pltpu.make_async_copy(self.sent.at[s, pos], self.got.at[s, pos], self.fsem.at[s, 3]).start()
        remote(
            self.sent.at[1 - s, pos],
            self.got.at[s, pos],
            self.ssem,
            self.fsem.at[s, 3],
            {"section": 1 - s},
        ).start()

    def relay(self):
        for layer, way in ((0, 1), (1, 3)):
            buf = self.relay_buf.at[layer]
            remote(buf, buf, self.ssem, self.rsem.at[layer], self.near(1)).wait_recv()
            origin = (self.position + 4 - way) % 4
            remote(
                buf,
                self.got.at[self.section, origin],
                self.ssem,
                self.fsem.at[self.section, 2],
                {**self.near(way), "section": layer},
            ).start()

    def arrive(self):
        for m in range(2):
            for k, step in enumerate((1, 3, 2, 0)):
                ref = self.got.at[m, (self.position + step) % 4]
                remote(ref, ref, self.ssem, self.fsem.at[m, k], self.near(1)).wait_recv()

    def drain(self):
        for layer in range(2):
            ref = self.sent.at[layer]
            remote(ref, ref, self.ssem, self.rsem.at[0], self.near(1)).wait_send()
        ref = self.sent.at[0, 0]
        remote(ref, ref, self.ssem, self.rsem.at[0], self.near(1)).wait_send()


def fold(pieces):
    total = pieces[0].astype(f32)
    for piece in pieces[1:]:
        total = total + piece.astype(f32)
    return total


def grads_kernel(
    n0, dl0, la0, dq0, dr0, mx0, act0, grad0, n1, dl1, la1, dq1, dr1, mx1, act1, grad1,
    act_o, grad_o, down_o, qk_o, up_o,
    xs, xg, xr, ys, yg, yr, td, sd, zd, zr, tu, su, zu, zv,
    xssem, xfsem, xrsem, yssem, yfsem, yrsem, psem, qsem, asem, dsem, dr, usem, ur, zsem, zrecv,
):
    s = lax.axis_index("section")
    e, d, z, y, right, left, opp = places()

    def near_x(k):
        return {"dp": (d + k) % 4}

    def near_y(k):
        return {"expert": z * NY + (y + k) % 4}

    def near_z(k):
        return {"expert": ((z + k) % NZ) * NY + y}

    barrier = pltpu.get_barrier_semaphore()
    peers = [{"section": 1 - s}]
    for near in (near_x, near_y):
        for k in (1, 3):
            peers += [{**near(k), "section": 0}, {**near(k), "section": 1}]
        peers.append(near(2))
    peers += [near_z(k) for k in range(1, NZ)]
    for peer in peers:
        pl.semaphore_signal(barrier, inc=1, device_id=peer, device_id_type=MESH)
    x_ring = Ring(s, d, near_x, xs, xg, xr, xssem, xfsem, xrsem)
    y_ring = Ring(s, y, near_y, ys, yg, yr, yssem, yfsem, yrsem)
    factors = ((n0, dl0, la0, dq0, dr0, mx0), (n1, dl1, la1, dq1, dr1, mx1))
    by_x, by_y, small = quarter_matrix(True), quarter_matrix(False), small_matrix()
    for layer, (n, dl, la, dq, _, _) in enumerate(factors):
        lay_out(n[...], by_x, xs, layer)
        moved = dot(la[...], small).astype(bf16)
        for q in range(4):
            xs[layer, q, :, 1024:1280] = dl[...]
            xs[layer, q, :, 1280:1536] = moved[:, q * 256 : (q + 1) * 256]
            xs[layer, q, :, 1536:1792] = dq[...]
    pl.semaphore_wait(barrier, len(peers))
    x_ring.start(0)
    x_ring.start(1)
    for layer, (_, _, _, _, dres, mx) in enumerate(factors):
        lay_out(dres[...], by_y, ys, layer)
        for q in range(4):
            ys[layer, q, :, 1024:1280] = mx[...]
    y_ring.start(0)
    y_ring.start(1)
    x_ring.own()
    y_ring.own()

    for k, (out, first_layer, second_layer) in enumerate(((act_o, act0, act1), (grad_o, grad0, grad1))):
        for here, keep, give in ((0, first_layer, second_layer), (1, second_layer, first_layer)):

            @pl.when(s == here)
            def _():
                pltpu.make_async_copy(keep, out.at[s], asem.at[k]).start()
                remote(give, out.at[s], psem, qsem.at[k], {"section": 1 - s}).start()

    x_ring.relay()
    y_ring.relay()

    def rows(ring, start, width):
        got = ring.got
        return jnp.concatenate(
            [got[m, q, :, start : start + width] for m in range(2) for q in range(4)], axis=0
        )

    x_ring.arrive()
    total = t_times(rows(x_ring, 0, 1024), rows(x_ring, 1024, 256)).astype(bf16)
    total_qk = t_times(rows(x_ring, 1280, 256), rows(x_ring, 1536, 256)).astype(bf16)
    for q in range(4):
        for c in range(4):
            td[q, c * 64 : (c + 1) * 64, :] = total[c * 256 + q * 64 : c * 256 + (q + 1) * 64]
        td[q, 256:320, :] = total_qk[q * 64 : (q + 1) * 64]
    for k in (2, 1, 3):
        remote(td.at[(y + k) % 4], sd.at[y], dsem, dr.at[4 - k - 1], near_y(k)).start()
    y_ring.arrive()
    total = t_times(rows(y_ring, 0, 1024), rows(y_ring, 1024, 256)).astype(bf16)
    for q in range(4):
        for c in range(4):
            tu[q, c * 64 : (c + 1) * 64, :] = total[c * 256 + q * 64 : c * 256 + (q + 1) * 64]
    for k in (2, 1, 3):
        remote(tu.at[(d + k) % 4], su.at[d], usem, ur.at[4 - k - 1], near_x(k)).start()

    def gathered(buf, recv, position):
        for k in (1, 2, 3):
            ref = buf.at[(position + k) % 4]
            remote(ref, ref, dsem, recv.at[k - 1], near_x(1)).wait_recv()
        return [buf[(position + k) % 4] for k in (1, 2, 3)]

    summed = fold([td[y]] + gathered(sd, dr, y)).astype(bf16)
    for k in range(NZ):
        zd[k, 0:32, :] = summed[k * 32 : (k + 1) * 32]
        zd[k, 32:40, :] = summed[256 + k * 8 : 264 + k * 8]
    for k in range(1, NZ):
        remote(zd.at[(z + k) % NZ], zr.at[z], zsem.at[0], zrecv.at[0, NZ - k - 1], near_z(k)).start()
    summed = fold([tu[d]] + gathered(su, ur, d)).astype(bf16)
    for k in range(NZ):
        zu[k] = summed[k * 32 : (k + 1) * 32]
    for k in range(1, NZ):
        remote(zu.at[(z + k) % NZ], zv.at[z], zsem.at[1], zrecv.at[1, NZ - k - 1], near_z(k)).start()

    def last(own, buf, which):
        for k in range(1, NZ):
            ref = buf.at[(z + k) % NZ]
            remote(ref, ref, zsem.at[0], zrecv.at[which, k - 1], near_z(1)).wait_recv()
        return fold([own[z]] + [buf[(z + k) % NZ] for k in range(1, NZ)])

    mine = last(zd, zr, 0)
    down_o[...] = mine[0:28]
    qk_o[...] = mine[32:34]
    mine = last(zu, zv, 1)
    up_o[...] = mine[0:28]

    x_ring.drain()
    y_ring.drain()
    for k, (out, some) in enumerate(((act_o, act0), (grad_o, grad0))):
        pltpu.make_async_copy(some, out.at[s], asem.at[k]).wait()
        remote(some, out.at[1 - s], psem, qsem.at[k], {"section": 1 - s}).wait_recv()
    whole = act_o
    remote(whole, whole, psem, qsem.at[0], {"section": 1 - s}).wait_send()
    ref = td.at[pl.ds(0, 3)]
    remote(ref, ref, dsem, dr.at[0], near_x(1)).wait_send()
    ref = tu.at[pl.ds(0, 3)]
    remote(ref, ref, usem, ur.at[0], near_x(1)).wait_send()
    ref = zd.at[pl.ds(0, NZ - 1)]
    remote(ref, ref, zsem.at[0], dr.at[0], near_x(1)).wait_send()
    ref = zu.at[pl.ds(0, NZ - 1)]
    remote(ref, ref, zsem.at[1], dr.at[0], near_x(1)).wait_send()


def weight_grads(layer0, layer1):
    dma = pltpu.SemaphoreType.DMA
    ring_sems = [dma, dma((2, 4)), dma((2,))]
    return pl.pallas_call(
        grads_kernel,
        name="weight_grads",
        out_shape=[
            jax.ShapeDtypeStruct((2, SEQ, WIDTH), bf16),
            jax.ShapeDtypeStruct((2, SEQ, WIDTH), bf16),
            jax.ShapeDtypeStruct((28, LAT), f32),
            jax.ShapeDtypeStruct((2, LAT), f32),
            jax.ShapeDtypeStruct((28, LAT), f32),
        ],
        in_specs=[VMEM] * 16,
        out_specs=[VMEM] * 5,
        scratch_shapes=[
            pltpu.VMEM((2, 4, SEQ, ROUND), bf16),
            pltpu.VMEM((2, 4, SEQ, ROUND), bf16),
            pltpu.VMEM((2, SEQ, ROUND), bf16),
            pltpu.VMEM((2, 4, SEQ, SIDE), bf16),
            pltpu.VMEM((2, 4, SEQ, SIDE), bf16),
            pltpu.VMEM((2, SEQ, SIDE), bf16),
            pltpu.VMEM((4, 320, LAT), bf16),
            pltpu.VMEM((4, 320, LAT), bf16),
            pltpu.VMEM((NZ, 40, LAT), bf16),
            pltpu.VMEM((NZ, 40, LAT), bf16),
            pltpu.VMEM((4, 256, LAT), bf16),
            pltpu.VMEM((4, 256, LAT), bf16),
            pltpu.VMEM((NZ, 32, LAT), bf16),
            pltpu.VMEM((NZ, 32, LAT), bf16),
        ]
        + ring_sems * 2
        + [dma, dma((2,)), dma((2,)), dma, dma((3,)), dma, dma((3,)), dma((2,)), dma((2, NZ - 1))],
        compiler_params=pltpu.CompilerParams(collective_id=2, has_side_effects=True),
    )(*layer0, *layer1)


def place_kernel(act, grad, down, qk, up, act_o, grad_o, down_o, qk_o, up_o):
    act_o[...] = act[...]
    grad_o[...] = grad[...]
    down_o[...] = down[...].reshape(28, 1, LAT)
    qk_o[...] = qk[...]
    up_o[...] = up[...].reshape(28, 1, LAT)


def place_results(results):
    return pl.pallas_call(
        place_kernel,
        name="place_results",
        out_shape=[
            shaped(2, *TOKENS),
            shaped(2, *TOKENS),
            shaped(28, 1, LAT, dtype=f32),
            shaped(2, LAT, dtype=f32),
            shaped(28, 1, LAT, dtype=f32),
        ],
        in_specs=[VMEM] * 5,
        out_specs=[VMEM] * 5,
    )(*results)


def swap(value):
    return lax.ppermute(value, "section", [(0, 1), (1, 0)])


def body(x_in, dy_out, routes, gates, w_down, w_qk, w_up, e_gate, e_up, e_down):
    section = lax.axis_index("section")
    attn_own = (w_down[0], w_qk[0], w_up[0])
    experts_own = (e_gate[0, 0], e_up[0, 0], e_down[0, 0])
    attn = attn_own + tuple(swap(w) for w in attn_own)
    def both_layers(table):
        other = swap(lax.dynamic_index_in_dim(table, 1 - section, 0, keepdims=False))
        own = lax.dynamic_index_in_dim(table, section, 0, keepdims=False)
        return (jnp.where(section == 0, own, other), jnp.where(section == 0, other, own))

    route_cols = both_layers(routes[0, :, 0])
    gate_cols = both_layers(gates[0, :, 0])
    route_rows = tuple(r.reshape(1, SEQ) for r in route_cols)

    whole = {
        "x": (x_in[:, 0], VMEM),
        "dy": (dy_out[:, 0], VMEM),
        **{f"route_row{k}": (route_rows[k], VMEM) for k in range(2)},
        **{f"route_col{k}": (route_cols[k], VMEM) for k in range(2)},
        **{f"gate_col{k}": (gate_cols[k], VMEM) for k in range(2)},
        **named("attn", [(w, ANY) for w in attn]),
        **named("expert", [(w, ANY) for w in experts_own]),
    }
    kept = fused(
        forward_run,
        "forward",
        whole,
        {
            "act0": shaped(*TOKENS),
            **kept_shapes(0),
            **kept_shapes(1),
            "gate0": shaped(*PRE, dtype=f32),
            "up0": shaped(*PRE, dtype=f32),
            "part1": shaped(*ROWS),
            "homeb": shaped(*HOME),
        },
        {
            **COMMON,
            **Experts.scratch(2),
            "hidden": pltpu.VMEM(PRE, bf16),
            **dispatch_scratch("a"),
            **dispatch_scratch("b"),
            **dispatch_scratch("c"),
            **combine_scratch("a"),
            **combine_scratch("b", skip=("homeb",)),
        },
        0,
    )
    part1, back1 = kept.pop("part1"), kept.pop("homeb")
    done = fused(
        backward_run,
        "backward",
        {
            **whole,
            **{k: (v, VMEM) for k, v in kept.items()},
            "parta": (part1, VMEM),
            "back1": (back1, VMEM),
        },
        {"act1": shaped(*TOKENS), **factor_shapes(1), **factor_shapes(0)},
        {
            **COMMON,
            **Experts.scratch(1),
            **dispatch_scratch("a"),
            **combine_scratch("a", skip=("parta",)),
            **combine_scratch("b"),
        },
        1,
    )
    layers = [
        tuple({**kept, **done}[f"{k}{layer}"] for k in ("n", "dl", "latent", "dq", "dr", "mixed", "act", "grad"))
        for layer in range(2)
    ]
    activations, grads_in, g_down, g_qk, g_up_t = place_results(weight_grads(*layers))
    return (
        activations[None, :, None],
        grads_in[None, :, None],
        jnp.swapaxes(g_down, 0, 1),
        g_qk[None],
        jnp.swapaxes(g_up_t, 0, 1),
    )


def solution(mesh):
    placed = (
        P(None, ("expert", "dp"), None, None),
        P(None, ("expert", "dp"), None, None),
        P("section", None, ("expert", "dp"), None, None),
        P("section", None, ("expert", "dp"), None, None),
        P("section", None, None),
        P("section", None, None),
        P("section", None, None),
        P("section", "expert", None, "dp"),
        P("section", "expert", None, "dp"),
        P("section", "expert", "dp", None),
    )
    return jax.shard_map(
        body,
        mesh=mesh,
        in_specs=placed,
        out_specs=(
            P("section", None, ("expert", "dp"), None, None),
            P("section", None, ("expert", "dp"), None, None),
            P("section", ("expert", "dp"), None),
            P("section", ("expert", "dp"), None),
            P("section", ("expert", "dp"), None),
        ),
        check_vma=False,
    )
```

```python
import functools

import jax
import jax.numpy as jnp
from jax import lax
from jax.experimental import pallas as pl
from jax.experimental.pallas import tpu as pltpu
from jax.sharding import PartitionSpec as P

epsilon = 1e-06
WIDTH = 3584
LAT = 256
FF = 256
SEQ = 64
EXPERTS = 32
DP = 4
CAP = 3
NZ = 8
NY = 4
PIECE = 896
PIECES = 4
BLOCK = (PIECES, CAP * PIECE)
PACKED = PIECES * EXPERTS
ORDER = (0, 1, 7, 2, 6, 3, 5, 4)
MESH = pl.DeviceIdType.MESH
VMEM = pl.BlockSpec(memory_space=pltpu.VMEM)
ANY = pl.BlockSpec(memory_space=pl.ANY)
bf16 = jnp.bfloat16
f32 = jnp.float32


def dot(left, right):
    return jnp.dot(left, right, preferred_element_type=f32)


def times_t(left, right):
    return lax.dot_general(left, right, (((1,), (1,)), ((), ())), preferred_element_type=f32)


def t_times(left, right):
    return lax.dot_general(left, right, (((0,), (0,)), ((), ())), preferred_element_type=f32)


def rms_norm(values):
    inv_rms = lax.rsqrt(jnp.mean(values * values, axis=-1, keepdims=True) + epsilon)
    return (values * inv_rms, inv_rms)


def rms_back(normed, inv_rms, upstream):
    return inv_rms * (upstream - normed * jnp.mean(upstream * normed, axis=-1, keepdims=True))


def silu_parts(gate_pre):
    sigmoid = jax.nn.sigmoid(gate_pre)
    return (gate_pre * sigmoid, sigmoid * (1.0 + gate_pre * (1.0 - sigmoid)))


def spread_matrix():
    rows = lax.broadcasted_iota(jnp.int32, (PACKED, PACKED), 0)
    cols = lax.broadcasted_iota(jnp.int32, (PACKED, PACKED), 1)
    return ((rows % PIECES) * EXPERTS + rows // PIECES == cols).astype(f32).astype(bf16)


def gather_matrix():
    rows = lax.broadcasted_iota(jnp.int32, (PACKED, PACKED), 0)
    cols = lax.broadcasted_iota(jnp.int32, (PACKED, PACKED), 1)
    return ((cols % PIECES) * EXPERTS + cols // PIECES == rows).astype(f32).astype(bf16)


def slot_rows(route_row):
    experts = lax.broadcasted_iota(jnp.int32, (EXPERTS, SEQ), 0)
    hot = (experts == route_row).astype(f32)
    before = lax.broadcasted_iota(jnp.int32, (SEQ, SEQ), 0) < lax.broadcasted_iota(
        jnp.int32, (SEQ, SEQ), 1
    )
    rank = dot(hot.astype(bf16), before.astype(f32).astype(bf16))
    return jnp.concatenate(
        [(hot * (rank == float(s)).astype(f32)).astype(bf16) for s in range(CAP)], axis=0
    )


def slot_columns(route_col):
    experts = lax.broadcasted_iota(jnp.int32, (SEQ, EXPERTS), 1)
    hot = (experts == route_col).astype(f32)
    before = lax.broadcasted_iota(jnp.int32, (SEQ, SEQ), 0) > lax.broadcasted_iota(
        jnp.int32, (SEQ, SEQ), 1
    )
    rank = dot(before.astype(f32).astype(bf16), hot.astype(bf16))
    return jnp.concatenate(
        [(hot * (rank == float(s)).astype(f32)).astype(bf16) for s in range(CAP)], axis=1
    )


def pack_tokens(values_b, route_row, packed_ref, blocks_ref):
    picked = dot(slot_rows(route_row), values_b).astype(bf16)
    for s in range(CAP):
        for r in range(PIECES):
            packed_ref[r * EXPERTS : (r + 1) * EXPERTS, s * PIECE : (s + 1) * PIECE] = picked[
                s * EXPERTS : (s + 1) * EXPERTS, r * PIECE : (r + 1) * PIECE
            ]
    blocks_ref[...] = dot(spread_matrix(), packed_ref[...]).astype(bf16).reshape(HOME)


def unpack_tokens(blocks_ref, route_col, token_ref):
    packed = dot(gather_matrix(), blocks_ref[...].reshape(PACKED, BLOCK[1])).astype(bf16)
    columns = slot_columns(route_col)
    for r in range(PIECES):
        stacked = jnp.concatenate(
            [
                packed[r * EXPERTS : (r + 1) * EXPERTS, s * PIECE : (s + 1) * PIECE]
                for s in range(CAP)
            ],
            axis=0,
        )
        token_ref[:, r * PIECE : (r + 1) * PIECE] = dot(columns, stacked)


def places():
    e = lax.axis_index("expert")
    d = lax.axis_index("dp")
    return e, d, e // NY, e % NY, (d + 1) % DP, (d + DP - 1) % DP, (d + 2) % DP


def greet(e, right, left, more=()):
    barrier = pltpu.get_barrier_semaphore()
    for k in range(1, EXPERTS):
        pl.semaphore_signal(
            barrier, inc=1, device_id={"expert": (e + k) % EXPERTS}, device_id_type=MESH
        )
    for side in (right, left):
        pl.semaphore_signal(barrier, inc=1, device_id={"dp": side}, device_id_type=MESH)
    partner = {"section": 1 - lax.axis_index("section")}
    for peer in (partner, *more):
        pl.semaphore_signal(barrier, inc=1, device_id=peer, device_id_type=MESH)


def greeted(more=0):
    pl.semaphore_wait(pltpu.get_barrier_semaphore(), EXPERTS + 2 + more)


def remote(src, dst, send, recv, where):
    return pltpu.make_async_remote_copy(
        src_ref=src, dst_ref=dst, send_sem=send, recv_sem=recv, device_id=where, device_id_type=MESH
    )


class Dispatch:
    sems = (
        pltpu.SemaphoreType.DMA,
        pltpu.SemaphoreType.DMA,
        pltpu.SemaphoreType.DMA((NZ,)),
        pltpu.SemaphoreType.DMA((NZ,)),
        pltpu.SemaphoreType.DMA((NZ,)),
        pltpu.SemaphoreType.DMA((NZ,)),
    )

    def __init__(self, blk, rows, sems):
        self.blk, self.rows = blk, rows
        self.s1, self.sx, self.r1, self.rl, self.rr, self.ro = sems
        self.e, self.d, self.z, self.y, self.right, self.left, self.opp = places()

    def start(self):
        for j in ORDER:
            for dy in range(NY):
                spot = self.rows.at[self.d * EXPERTS + self.e]
                if j == 0 and dy == 0:
                    pltpu.make_async_copy(self.blk.at[self.e], spot, self.r1.at[0]).start()
                else:
                    peer = ((self.z + j) % NZ) * NY + (self.y + dy) % NY
                    remote(
                        self.blk.at[peer], spot, self.s1, self.r1.at[(NZ - j) % NZ], {"expert": peer}
                    ).start()

    def group(self, owner, j):
        return self.rows.at[pl.ds(owner * EXPERTS + ((self.z + j) % NZ) * NY, NY)]

    def arrived(self, ref, sem):
        remote(ref, ref, self.s1, sem, {"dp": self.right}).wait_recv()

    def forward(self, i):
        j = ORDER[i]
        mine = self.group(self.d, j)
        self.arrived(mine, self.r1.at[j])
        remote(mine, mine, self.sx, self.rl.at[j], {"dp": self.right}).start()
        remote(mine, mine, self.sx, self.rr.at[j], {"dp": self.left}).start()

    def relay(self, i):
        j = ORDER[i]
        owner, sem, to = (
            (self.left, self.rl, self.right) if i % 2 == 0 else (self.right, self.rr, self.left)
        )
        ref = self.group(owner, j)
        self.arrived(ref, sem.at[j])
        remote(ref, ref, self.sx, self.ro.at[j], {"dp": to}).start()

    def wait_right(self):
        for i, j in enumerate(ORDER):
            if i % 2 == 0:
                self.arrived(self.group(self.right, j), self.rr.at[j])

    def wait_left(self):
        for i, j in enumerate(ORDER):
            if i % 2 == 1:
                self.arrived(self.group(self.left, j), self.rl.at[j])

    def wait_far(self):
        for j in ORDER:
            self.arrived(self.group(self.opp, j), self.ro.at[j])

    def chunks(self, use, near):
        @pl.loop(0, DP)
        def _(k):
            pl.when(k == 1)(self.wait_right)
            pl.when(k == 2)(self.wait_left)
            pl.when(k == 3)(self.wait_far)
            use((self.d + k + k // 2 - 2 * (k // 3)) % DP)
            pl.when(k == 2)(near)

    def drain(self):
        sent = self.blk.at[pl.ds(0, EXPERTS - 1)]
        remote(sent, sent, self.s1, self.r1.at[0], {"dp": self.right}).wait_send()
        sent = self.rows.at[pl.ds(0, 3 * EXPERTS)]
        remote(sent, sent, self.sx, self.r1.at[0], {"dp": self.right}).wait_send()


class Combine:
    sems = (
        pltpu.SemaphoreType.DMA,
        pltpu.SemaphoreType.DMA,
        pltpu.SemaphoreType.DMA((NZ,)),
        pltpu.SemaphoreType.DMA((NZ,)),
        pltpu.SemaphoreType.DMA((NZ,)),
        pltpu.SemaphoreType.DMA,
    )
    buffers = (pltpu.VMEM((EXPERTS, *BLOCK), bf16),) * 5

    def __init__(self, part, out, buffers, sems):
        self.part, self.out = part, out
        self.relayed, self.relay_sum, self.from_left, self.from_right, self.final = buffers
        self.sx, self.s1, self.ra, self.rl, self.rr, self.rh = sems
        self.e, self.d, self.z, self.y, self.right, self.left, self.opp = places()

    def group(self, owner, j):
        return self.part.at[pl.ds(owner * EXPERTS + ((self.z + j) % NZ) * NY, NY)]

    def spot(self, ref, i):
        return ref.at[pl.ds(i * NY, NY)]

    def arrived(self, ref, sem):
        remote(ref, ref, self.s1, sem, {"dp": self.right}).wait_recv()

    def start_far(self):
        for i, j in enumerate(ORDER):
            side = self.right if i % 2 == 0 else self.left
            remote(
                self.group(self.opp, j), self.spot(self.relayed, i), self.sx, self.ra.at[i], {"dp": side}
            ).start()

    def start_near(self):
        for i, j in enumerate(ORDER):
            if i % 2 == 0:
                ref, to, sem, side = self.left, self.from_right, self.rr, self.left
            else:
                ref, to, sem, side = self.right, self.from_left, self.rl, self.right
            remote(self.group(ref, j), self.spot(to, i), self.sx, sem.at[i], {"dp": side}).start()

    def relay(self, i):
        j = ORDER[i]
        self.arrived(self.spot(self.relayed, i), self.ra.at[i])
        side, to, sem = (
            (self.right, self.from_left, self.rl)
            if i % 2 == 0
            else (self.left, self.from_right, self.rr)
        )
        self.spot(self.relay_sum, i)[...] = (
            self.spot(self.relayed, i)[...].astype(f32) + self.group(side, j)[...].astype(f32)
        ).astype(bf16)
        remote(
            self.spot(self.relay_sum, i), self.spot(to, i), self.sx, sem.at[i], {"dp": side}
        ).start()

    def finish(self, i):
        j = ORDER[i]
        self.arrived(self.spot(self.from_left, i), self.rl.at[i])
        self.arrived(self.spot(self.from_right, i), self.rr.at[i])
        self.spot(self.final, i)[...] = (
            self.group(self.d, j)[...].astype(f32)
            + self.spot(self.from_left, i)[...].astype(f32)
            + self.spot(self.from_right, i)[...].astype(f32)
        ).astype(bf16)
        for dy in range(NY):
            yy = (self.y + dy) % NY
            spot = self.out.at[self.e]
            if j == 0 and dy == 0:
                pltpu.make_async_copy(self.final.at[i * NY + yy], spot, self.rh).start()
            else:
                peer = ((self.z + j) % NZ) * NY + yy
                remote(
                    self.final.at[i * NY + yy], spot, self.s1, self.rh, {"expert": peer}
                ).start()

    def arrive(self):
        self.arrived(self.out, self.rh)

    def drain(self):
        sent = self.part.at[pl.ds(0, 3 * EXPERTS)]
        remote(sent, sent, self.sx, self.rh, {"dp": self.right}).wait_send()
        sent = self.part.at[pl.ds(0, EXPERTS - 1)]
        remote(sent, sent, self.s1, self.rh, {"dp": self.right}).wait_send()


def fetch(layer, pairs, sems):
    mine = lax.axis_index("section") == layer
    for k, (own, other, dst) in enumerate(pairs):

        @pl.when(mine)
        def _():
            pltpu.make_async_copy(own, dst, sems.at[k]).start()

        @pl.when(jnp.logical_not(mine))
        def _():
            pltpu.make_async_copy(other, dst, sems.at[k]).start()

    def wait(k):
        own, _, dst = pairs[k]
        pltpu.make_async_copy(own, dst, sems.at[k]).wait()

    return wait


def attend(
    inputs, route_row, wd, wq, wu, wait, packed, blocks, residual, latent_o, queries_o, probs_o, mixed_o
):
    normed, _ = rms_norm(inputs.astype(f32))
    wait(0)
    latent = dot(normed.astype(bf16), wd[...]).astype(bf16)
    wait(1)
    queries = dot(latent, wq[...]).astype(bf16)
    scores = times_t(queries, latent) * (LAT ** (-0.5))
    causal = lax.broadcasted_iota(jnp.int32, (SEQ, SEQ), 0) >= lax.broadcasted_iota(
        jnp.int32, (SEQ, SEQ), 1
    )
    scores = jnp.where(causal, scores, -1e30)
    exponent = jnp.exp(scores - jnp.max(scores, axis=-1, keepdims=True))
    probs = exponent / jnp.sum(exponent, axis=-1, keepdims=True)
    mixed = dot(probs.astype(bf16), latent).astype(bf16)
    wait(2)
    resid = (inputs.astype(f32) + dot(mixed, wu[...])).astype(bf16)
    residual[...] = resid
    latent_o[...] = latent
    queries_o[...] = queries
    probs_o[...] = probs
    mixed_o[...] = mixed
    normed2, _ = rms_norm(resid.astype(f32))
    pack_tokens(normed2.astype(bf16), route_row, packed, blocks)


def attend_back(
    upstream, inputs, resid, latent, queries, probs, mixed, w, wait, tokens, normed_o, d_latent_o,
    d_queries_o, d_resid_o, grad,
):
    normed2, inv2 = rms_norm(resid.astype(f32))
    d_resid = upstream.astype(f32) + rms_back(normed2, inv2, tokens[...])
    d_resid_b = d_resid.astype(bf16)
    d_resid_o[...] = d_resid_b
    tokens[...] = d_resid
    wd, wq, wu = w
    wait(2)
    d_mixed = times_t(d_resid_b, wu[...]).astype(bf16)
    d_probs = times_t(d_mixed, latent)
    d_scores = (
        probs * (d_probs - jnp.sum(d_probs * probs, axis=-1, keepdims=True)) * (LAT ** (-0.5))
    ).astype(bf16)
    d_queries = dot(d_scores, latent).astype(bf16)
    wait(1)
    d_latent = (
        t_times(probs.astype(bf16), d_mixed)
        + t_times(d_scores, queries)
        + times_t(d_queries, wq[...])
    ).astype(bf16)
    wait(0)
    d_normed = times_t(d_latent, wd[...])
    normed, inv = rms_norm(inputs.astype(f32))
    normed_o[...] = normed.astype(bf16)
    d_latent_o[...] = d_latent
    d_queries_o[...] = d_queries
    grad[...] = (tokens[...] + rms_back(normed, inv, d_normed)).astype(bf16)


CHUNK = CAP * EXPERTS


def unpack_rows(rows, wide, g):
    packed = dot(
        gather_matrix(), rows[pl.ds(g * EXPERTS, EXPERTS)].reshape(PACKED, BLOCK[1])
    ).astype(bf16)
    for s in range(CAP):
        for r in range(PIECES):
            wide[s * EXPERTS : (s + 1) * EXPERTS, r * PIECE : (r + 1) * PIECE] = packed[
                r * EXPERTS : (r + 1) * EXPERTS, s * PIECE : (s + 1) * PIECE
            ]
    return wide[...]


def pack_rows(piece, packed, out, g):
    for r in range(PIECES):
        rows = piece(slice(r * PIECE, (r + 1) * PIECE)).astype(bf16)
        for s in range(CAP):
            packed[r * EXPERTS : (r + 1) * EXPERTS, s * PIECE : (s + 1) * PIECE] = rows[
                s * EXPERTS : (s + 1) * EXPERTS
            ]
    out[pl.ds(g * EXPERTS, EXPERTS)] = (
        dot(spread_matrix(), packed[...]).astype(bf16).reshape(EXPERTS, *BLOCK)
    )


def chunk_rows(g):
    return pl.ds(pl.multiple_of(g * CHUNK, CHUNK), CHUNK)


def expert_out(hidden, dw):
    return lambda cols: dot(hidden, dw[:, cols])


def expert_back(rows, gate_pre, up_pre, gw, uw, dw):
    d_hidden = times_t(rows, dw[...])
    activated, slope = silu_parts(gate_pre)
    d_gate = (d_hidden * up_pre * slope).astype(bf16)
    d_up = (d_hidden * activated).astype(bf16)
    return lambda cols: times_t(d_gate, gw[cols, :]) + times_t(d_up, uw[cols, :])


class Refs:
    def __init__(self, names, refs):
        for name, ref in zip(names, refs, strict=True):
            setattr(self, name, ref)

    def some(self, prefix, count):
        return tuple(getattr(self, f"{prefix}{k}") for k in range(count))


def named(prefix, items):
    return {f"{prefix}{k}": item for k, item in enumerate(items)}


def fused(run, name, ins, outs, scratch, number):
    names = [*ins, *outs, *scratch]

    def kernel(*refs):
        run(Refs(names, refs))

    results = pl.pallas_call(
        kernel,
        name=name,
        out_shape=list(outs.values()),
        in_specs=[spec for _, spec in ins.values()],
        out_specs=[VMEM] * len(outs),
        scratch_shapes=list(scratch.values()),
        compiler_params=pltpu.CompilerParams(
            collective_id=number, has_side_effects=True, vmem_limit_bytes=60 * 1024 * 1024
        ),
    )(*[array for array, _ in ins.values()])
    return dict(zip(outs, results))


def shaped(*shape, dtype=bf16):
    return jax.ShapeDtypeStruct(shape, dtype)


TOKENS = (SEQ, WIDTH)
ROWS = (DP * EXPERTS, *BLOCK)
HOME = (EXPERTS, *BLOCK)
PRE = (CAP * DP * EXPERTS, FF)
COMMON = {
    "tokens": pltpu.VMEM(TOKENS, f32),
    "wide": pltpu.VMEM((CHUNK, WIDTH), bf16),
    "packed": pltpu.VMEM((PACKED, BLOCK[1]), bf16),
    "w0": pltpu.VMEM((WIDTH, LAT), bf16),
    "w1": pltpu.VMEM((LAT, LAT), bf16),
    "w2": pltpu.VMEM((LAT, WIDTH), bf16),
    "wsem": pltpu.SemaphoreType.DMA((3,)),
}
EXPERT_WEIGHTS = ((WIDTH, FF), (WIDTH, FF), (FF, WIDTH))


def fetch_attn(refs, layer):
    attn = refs.some("attn", 6)
    return fetch(layer, [(attn[k], attn[3 + k], getattr(refs, f"w{k}")) for k in range(3)], refs.wsem)


class Experts:
    @staticmethod
    def scratch(layers):
        return {
            **named("v", [pltpu.VMEM((layers, *shape), bf16) for shape in EXPERT_WEIGHTS]),
            "vsem": pltpu.SemaphoreType.DMA((layers, 3)),
            "vsent": pltpu.SemaphoreType.DMA((3,)),
        }

    def __init__(self, refs, layers):
        self.s = lax.axis_index("section")
        self.own = refs.some("expert", 3)
        self.v = refs.some("v", 3)
        self.sem, self.sent, self.layers = refs.vsem, refs.vsent, layers

    def each(self, act):
        def run():
            for k in range(3):
                act(k)

        if self.layers == 1:
            pl.when(self.s == 0)(run)
        else:
            run()

    def place(self):
        return self.s if self.layers == 2 else 0

    def copy(self, k):
        return pltpu.make_async_copy(
            self.own[k], self.v[k].at[self.place()], self.sem.at[self.place(), k]
        )

    def give(self, k):
        return remote(
            self.own[k],
            self.v[k].at[self.place()],
            self.sent.at[k],
            self.sem.at[self.place(), k],
            {"section": 1 - self.s},
        )

    def start(self):
        self.each(lambda k: self.copy(k).start())

    def send(self):
        self.each(lambda k: self.give(k).start())

    def drain(self):
        self.each(lambda k: self.give(k).wait_send())

    def ready(self, layer):
        for k in range(3):
            pltpu.make_async_copy(
                self.own[k], self.v[k].at[layer], self.sem.at[layer, k]
            ).wait()
        return [ref.at[layer] for ref in self.v]


def dispatch_of(refs, tag):
    return Dispatch(
        getattr(refs, "blk" + tag), getattr(refs, "rows" + tag), refs.some("ds" + tag + "_", 6)
    )


def dispatch_scratch(tag):
    return {
        "blk" + tag: pltpu.VMEM(HOME, bf16),
        "rows" + tag: pltpu.VMEM(ROWS, bf16),
        **named("ds" + tag + "_", Dispatch.sems),
    }


def combine_of(refs, tag):
    return Combine(
        getattr(refs, "part" + tag),
        getattr(refs, "home" + tag),
        refs.some("cb" + tag + "_", 5),
        refs.some("cs" + tag + "_", 6),
    )


def combine_scratch(tag, skip=()):
    whole = {
        "part" + tag: pltpu.VMEM(ROWS, bf16),
        "home" + tag: pltpu.VMEM(HOME, bf16),
        **named("cb" + tag + "_", Combine.buffers),
        **named("cs" + tag + "_", Combine.sems),
    }
    return {k: v for k, v in whole.items() if k not in skip}


def kept_shapes(layer):
    return {
        f"resid{layer}": shaped(*TOKENS),
        f"latent{layer}": shaped(SEQ, LAT),
        f"queries{layer}": shaped(SEQ, LAT),
        f"probs{layer}": shaped(SEQ, SEQ, dtype=f32),
        f"mixed{layer}": shaped(SEQ, LAT),
    }


def kept_refs(refs, layer):
    return [getattr(refs, f"{k}{layer}") for k in ("resid", "latent", "queries", "probs", "mixed")]


def forward_run(refs):
    e, _, _, _, right, left, _ = places()
    section = lax.axis_index("section")
    greet(e, right, left)
    wait_w = fetch_attn(refs, 0)
    experts = Experts(refs, 2)
    experts.start()
    first, early, second = (dispatch_of(refs, tag) for tag in ("a", "b", "c"))
    out0, back1 = combine_of(refs, "a"), combine_of(refs, "b")
    w = refs.some("w", 3)

    attend(
        refs.x[section], refs.route_row0[...], *w, wait_w, refs.packed, refs.blka,
        *kept_refs(refs, 0),
    )
    wait_w = fetch_attn(refs, 1)
    greeted()
    first.start()
    experts.send()
    scaled = (refs.gate_col1[...] * refs.dy[section].astype(f32)).astype(bf16)
    pack_tokens(scaled, refs.route_row1[...], refs.packed, refs.blkb)
    for i in range(NZ):
        first.forward(i)
        if i >= 2:
            first.relay(i - 2)
        if i == 5:
            early.start()
    first.relay(6)
    first.relay(7)
    gw, uw, dw = experts.ready(0)

    def forward0(g):
        at = chunk_rows(g)
        rows = unpack_rows(refs.rowsa, refs.wide, g)
        gate_pre, up_pre = dot(rows, gw[...]), dot(rows, uw[...])
        refs.gate0[at, :] = gate_pre
        refs.up0[at, :] = up_pre
        hidden = (silu_parts(gate_pre)[0] * up_pre).astype(bf16)
        pack_rows(expert_out(hidden, dw), refs.packed, out0.part, g)

    first.chunks(forward0, out0.start_near)
    out0.start_far()
    for i in range(NZ):
        out0.relay(i)
    for i in range(NZ):
        early.forward(i)
    for i in range(NZ):
        out0.finish(i)
    out0.arrive()

    unpack_tokens(refs.homea, refs.route_col0[...], refs.tokens)
    act0 = (refs.resid0[...].astype(f32) + refs.gate_col0[...] * refs.tokens[...]).astype(bf16)
    refs.act0[...] = act0
    attend(act0, refs.route_row1[...], *w, wait_w, refs.packed, refs.blkc, *kept_refs(refs, 1))
    second.start()
    for i in range(NZ):
        early.relay(i)
    for i in range(NZ):
        second.forward(i)
        if i >= 2:
            second.relay(i - 2)
    second.relay(6)
    second.relay(7)
    early.wait_right()
    early.wait_left()
    early.wait_far()
    gw1, uw1, dw1 = experts.ready(1)

    def both1(g):
        at = chunk_rows(g)
        rows = unpack_rows(refs.rowsc, refs.wide, g)
        gate_pre, up_pre = dot(rows, gw1[...]), dot(rows, uw1[...])
        refs.hidden[at, :] = (silu_parts(gate_pre)[0] * up_pre).astype(bf16)
        rows = unpack_rows(refs.rowsb, refs.wide, g)
        pack_rows(
            expert_back(rows, gate_pre, up_pre, gw1, uw1, dw1), refs.packed, back1.part, g
        )

    def out1(g):
        pack_rows(expert_out(refs.hidden[chunk_rows(g), :], dw1), refs.packed, refs.part1, g)

    second.chunks(both1, back1.start_near)
    back1.start_far()
    pl.loop(0, 2)(out1)
    for i in range(NZ):
        back1.relay(i)
    pl.loop(2, DP)(out1)
    for i in range(NZ):
        back1.finish(i)
    back1.arrive()
    for each in (first, early, second, out0, back1, experts):
        each.drain()


def backward_run(refs):
    e, _, _, _, right, left, _ = places()
    section = lax.axis_index("section")
    grads = Grads(refs)
    more = grads.peers()
    greet(e, right, left, more)
    wait_w = fetch_attn(refs, 1)
    experts = Experts(refs, 1)
    experts.start()
    again = dispatch_of(refs, "a")
    out1, back0 = combine_of(refs, "a"), combine_of(refs, "b")
    w = refs.some("w", 3)

    unpack_tokens(refs.back1, refs.route_col1[...], refs.tokens)
    greeted(len(more))
    out1.start_far()
    out1.start_near()
    experts.send()
    attend_back(
        refs.dy[section], refs.act0[...], *[ref[...] for ref in kept_refs(refs, 1)], w, wait_w,
        refs.tokens, refs.n1, refs.dl1, refs.dq1, refs.dr1, refs.grad1,
    )
    wait_w = fetch_attn(refs, 0)
    scaled = (refs.gate_col0[...] * refs.grad1[...].astype(f32)).astype(bf16)
    pack_tokens(scaled, refs.route_row0[...], refs.packed, refs.blka)
    again.start()
    for i in range(NZ):
        out1.relay(i)
    for i in range(NZ):
        again.forward(i)
        if i >= 2:
            again.relay(i - 2)
    again.relay(6)
    again.relay(7)
    for i in range(NZ):
        out1.finish(i)
    gw, uw, dw = experts.ready(0)

    def backward0(g):
        at = chunk_rows(g)
        rows = unpack_rows(refs.rowsa, refs.wide, g)
        pack_rows(
            expert_back(rows, refs.gate0[at, :], refs.up0[at, :], gw, uw, dw),
            refs.packed,
            back0.part,
            g,
        )

    again.chunks(backward0, back0.start_near)
    back0.start_far()
    grads.lay_x(1, refs.n1, refs.dl1, refs.latent1, refs.dq1)
    for i in range(NZ):
        back0.relay(i)
    grads.x_ring.start(1)
    grads.lay_y(1, refs.dr1, refs.mixed1)
    grads.y_ring.start(1)
    out1.arrive()
    unpack_tokens(refs.homea, refs.route_col1[...], refs.tokens)
    refs.act1[...] = (
        refs.resid1[...].astype(f32) + refs.gate_col1[...] * refs.tokens[...]
    ).astype(bf16)
    grads.trade(0, refs.act_o, refs.act0, refs.act1)
    for i in range(NZ):
        back0.finish(i)
    grads.x_ring.relay(1)
    grads.y_ring.relay(1)
    back0.arrive()
    unpack_tokens(refs.homeb, refs.route_col0[...], refs.tokens)
    attend_back(
        refs.grad1[...], refs.x[section], *[ref[...] for ref in kept_refs(refs, 0)], w, wait_w,
        refs.tokens, refs.n0, refs.dl0, refs.dq0, refs.dr0, refs.grad0,
    )
    grads.lay_x(0, refs.n0, refs.dl0, refs.latent0, refs.dq0)
    grads.x_ring.start(0)
    grads.x_ring.own()
    grads.lay_y(0, refs.dr0, refs.mixed0)
    grads.y_ring.start(0)
    grads.y_ring.own()
    grads.trade(1, refs.grad_o, refs.grad0, refs.grad1)
    grads.x_ring.relay(0)
    grads.y_ring.relay(0)
    grads.sums()
    for each in (again, out1, back0, experts, grads):
        each.drain()


def factor_scratch(layer):
    return {
        f"n{layer}": pltpu.VMEM(TOKENS, bf16),
        f"dl{layer}": pltpu.VMEM((SEQ, LAT), bf16),
        f"dq{layer}": pltpu.VMEM((SEQ, LAT), bf16),
        f"dr{layer}": pltpu.VMEM(TOKENS, bf16),
        f"grad{layer}": pltpu.VMEM(TOKENS, bf16),
    }


ROUND = 1792
SIDE = 1280


def quarter_matrix(first_is_dp):
    out = lax.broadcasted_iota(jnp.int32, (1, 1024), 1)
    one, two, zz, i = out // 256, (out // 64) % 4, (out // 32) % 2, out % 32
    y, x = (two, one) if first_is_dp else (one, two)
    source = jnp.where(i < 28, zz * 448 + y * 112 + x * 28 + i, -1)
    return (lax.broadcasted_iota(jnp.int32, (896, 1024), 0) == source).astype(f32).astype(bf16)


def small_matrix():
    out = lax.broadcasted_iota(jnp.int32, (1, 1024), 1)
    x, y, z, i = out // 256, (out // 64) % 4, (out // 8) % 8, out % 8
    source = jnp.where(i < 2, z * 32 + y * 8 + x * 2 + i, -1)
    return (lax.broadcasted_iota(jnp.int32, (LAT, 1024), 0) == source).astype(f32).astype(bf16)


def lay_out(factor, matrix, sent, layer):
    stacked = jnp.concatenate([factor[:, c * 896 : (c + 1) * 896] for c in range(4)], axis=0)
    moved = dot(stacked, matrix).astype(bf16)
    for q in range(4):
        for c in range(4):
            sent[layer, q, :, c * 256 : (c + 1) * 256] = moved[
                c * SEQ : (c + 1) * SEQ, q * 256 : (q + 1) * 256
            ]


class Ring:
    def __init__(self, section, position, near, sent, got, relay, ssem, fsem, rsem):
        self.section, self.position, self.near = section, position, near
        self.sent, self.got, self.relay_buf = sent, got, relay
        self.ssem, self.fsem, self.rsem = ssem, fsem, rsem

    def start(self, layer):
        pos, s = self.position, self.section
        way = 1 if layer == 0 else 3
        remote(
            self.sent.at[layer, (pos + 2) % 4],
            self.relay_buf.at[layer],
            self.ssem,
            self.rsem.at[layer],
            self.near(way),
        ).start()
        for step, back in ((1, 1), (3, 0)):
            remote(
                self.sent.at[layer, (pos + step) % 4],
                self.got.at[s, pos],
                self.ssem,
                self.fsem.at[s, back],
                {**self.near(step), "section": layer},
            ).start()

    def own(self):
        pos, s = self.position, self.section
        pltpu.make_async_copy(self.sent.at[s, pos], self.got.at[s, pos], self.fsem.at[s, 3]).start()
        remote(
            self.sent.at[1 - s, pos],
            self.got.at[s, pos],
            self.ssem,
            self.fsem.at[s, 3],
            {"section": 1 - s},
        ).start()

    def relay(self, layer):
        way = 1 if layer == 0 else 3
        buf = self.relay_buf.at[layer]
        remote(buf, buf, self.ssem, self.rsem.at[layer], self.near(1)).wait_recv()
        origin = (self.position + 4 - way) % 4
        remote(
            buf,
            self.got.at[self.section, origin],
            self.ssem,
            self.fsem.at[self.section, 2],
            {**self.near(way), "section": layer},
        ).start()

    def arrive(self):
        for m in range(2):
            for k, step in enumerate((1, 3, 2, 0)):
                ref = self.got.at[m, (self.position + step) % 4]
                remote(ref, ref, self.ssem, self.fsem.at[m, k], self.near(1)).wait_recv()

    def drain(self):
        for layer in range(2):
            ref = self.sent.at[layer]
            remote(ref, ref, self.ssem, self.rsem.at[0], self.near(1)).wait_send()
        ref = self.sent.at[0, 0]
        remote(ref, ref, self.ssem, self.rsem.at[0], self.near(1)).wait_send()


def fold(pieces):
    total = pieces[0].astype(f32)
    for piece in pieces[1:]:
        total = total + piece.astype(f32)
    return total


class Grads:
    def __init__(self, refs):
        self.refs = refs
        self.s = lax.axis_index("section")
        _, self.d, self.z, self.y, _, _, _ = places()
        self.x_ring = Ring(
            self.s, self.d, self.near_x, refs.xs, refs.xg, refs.xr, refs.xssem, refs.xfsem, refs.xrsem
        )
        self.y_ring = Ring(
            self.s, self.y, self.near_y, refs.ys, refs.yg, refs.yr, refs.yssem, refs.yfsem, refs.yrsem
        )

    def near_x(self, k):
        return {"dp": (self.d + k) % 4}

    def near_y(self, k):
        return {"expert": self.z * NY + (self.y + k) % 4}

    def near_z(self, k):
        return {"expert": ((self.z + k) % NZ) * NY + self.y}

    def peers(self):
        other = {"section": 1 - self.s}
        return [
            {**self.near_x(1), **other},
            {**self.near_x(3), **other},
            {**self.near_y(1), **other},
            {**self.near_y(3), **other},
            self.near_x(2),
        ]

    def lay_x(self, layer, n, dl, la, dq):
        xs = self.refs.xs
        lay_out(n[...], quarter_matrix(True), xs, layer)
        moved = dot(la[...], small_matrix()).astype(bf16)
        for q in range(4):
            xs[layer, q, :, 1024:1280] = dl[...]
            xs[layer, q, :, 1280:1536] = moved[:, q * 256 : (q + 1) * 256]
            xs[layer, q, :, 1536:1792] = dq[...]

    def lay_y(self, layer, dres, mx):
        lay_out(dres[...], quarter_matrix(False), self.refs.ys, layer)
        for q in range(4):
            self.refs.ys[layer, q, :, 1024:1280] = mx[...]

    def trade(self, k, out, first_layer, second_layer):
        refs, s = self.refs, self.s
        for here, keep, give in ((0, first_layer, second_layer), (1, second_layer, first_layer)):

            @pl.when(s == here)
            def _():
                pltpu.make_async_copy(keep, out.at[s], refs.asem.at[k]).start()
                remote(give, out.at[s], refs.psem, refs.qsem.at[k], {"section": 1 - s}).start()

    def sums(self):
        refs, s, d, z, y = self.refs, self.s, self.d, self.z, self.y

        def rows(ring, start, width):
            got = ring.got
            return jnp.concatenate(
                [got[m, q, :, start : start + width] for m in range(2) for q in range(4)], axis=0
            )

        x_ring, y_ring = self.x_ring, self.y_ring
        x_ring.arrive()
        total = t_times(rows(x_ring, 0, 1024), rows(x_ring, 1024, 256)).astype(bf16)
        total_qk = t_times(rows(x_ring, 1280, 256), rows(x_ring, 1536, 256)).astype(bf16)
        for q in range(4):
            for c in range(4):
                refs.td[q, c * 64 : (c + 1) * 64, :] = total[c * 256 + q * 64 : c * 256 + (q + 1) * 64]
            refs.td[q, 256:320, :] = total_qk[q * 64 : (q + 1) * 64]
        for k in (2, 1, 3):
            remote(refs.td.at[(y + k) % 4], refs.sd.at[y], refs.dsem, refs.dr.at[4 - k - 1], self.near_y(k)).start()
        y_ring.arrive()
        total = t_times(rows(y_ring, 0, 1024), rows(y_ring, 1024, 256)).astype(bf16)
        for q in range(4):
            for c in range(4):
                refs.tu[q, c * 64 : (c + 1) * 64, :] = total[c * 256 + q * 64 : c * 256 + (q + 1) * 64]
        for k in (2, 1, 3):
            remote(refs.tu.at[(d + k) % 4], refs.su.at[d], refs.usem, refs.ur.at[4 - k - 1], self.near_x(k)).start()

        def gathered(buf, recv, position):
            for k in (1, 2, 3):
                ref = buf.at[(position + k) % 4]
                remote(ref, ref, refs.dsem, recv.at[k - 1], self.near_x(1)).wait_recv()
            return [buf[(position + k) % 4] for k in (1, 2, 3)]

        summed = fold([refs.td[y]] + gathered(refs.sd, refs.dr, y)).astype(bf16)
        for k in range(NZ):
            refs.zd[k, 0:32, :] = summed[k * 32 : (k + 1) * 32]
            refs.zd[k, 32:40, :] = summed[256 + k * 8 : 264 + k * 8]
        for k in range(1, NZ):
            remote(refs.zd.at[(z + k) % NZ], refs.zr.at[z], refs.zsem.at[0], refs.zrecv.at[0, NZ - k - 1], self.near_z(k)).start()
        summed = fold([refs.tu[d]] + gathered(refs.su, refs.ur, d)).astype(bf16)
        for k in range(NZ):
            refs.zu[k] = summed[k * 32 : (k + 1) * 32]
        for k in range(1, NZ):
            remote(refs.zu.at[(z + k) % NZ], refs.zv.at[z], refs.zsem.at[1], refs.zrecv.at[1, NZ - k - 1], self.near_z(k)).start()

        def last(own, buf, which):
            for k in range(1, NZ):
                ref = buf.at[(z + k) % NZ]
                remote(ref, ref, refs.zsem.at[0], refs.zrecv.at[which, k - 1], self.near_z(1)).wait_recv()
            return fold([own[z]] + [buf[(z + k) % NZ] for k in range(1, NZ)])

        mine = last(refs.zd, refs.zr, 0)
        refs.down_o[...] = mine[0:28]
        refs.qk_o[...] = mine[32:34]
        mine = last(refs.zu, refs.zv, 1)
        refs.up_o[...] = mine[0:28]

    def drain(self):
        refs = self.refs
        self.x_ring.drain()
        self.y_ring.drain()
        for k, (out, some) in enumerate(((refs.act_o, refs.act0), (refs.grad_o, refs.grad0))):
            pltpu.make_async_copy(some, out.at[self.s], refs.asem.at[k]).wait()
            remote(some, out.at[1 - self.s], refs.psem, refs.qsem.at[k], {"section": 1 - self.s}).wait_recv()
        whole = refs.act_o
        remote(whole, whole, refs.psem, refs.qsem.at[0], {"section": 1 - self.s}).wait_send()
        ref = refs.td.at[pl.ds(0, 3)]
        remote(ref, ref, refs.dsem, refs.dr.at[0], self.near_x(1)).wait_send()
        ref = refs.tu.at[pl.ds(0, 3)]
        remote(ref, ref, refs.usem, refs.ur.at[0], self.near_x(1)).wait_send()
        ref = refs.zd.at[pl.ds(0, NZ - 1)]
        remote(ref, ref, refs.zsem.at[0], refs.dr.at[0], self.near_x(1)).wait_send()
        ref = refs.zu.at[pl.ds(0, NZ - 1)]
        remote(ref, ref, refs.zsem.at[1], refs.dr.at[0], self.near_x(1)).wait_send()


def grads_scratch():
    dma = pltpu.SemaphoreType.DMA
    buffers = {
        "xs": (2, 4, SEQ, ROUND),
        "xg": (2, 4, SEQ, ROUND),
        "xr": (2, SEQ, ROUND),
        "ys": (2, 4, SEQ, SIDE),
        "yg": (2, 4, SEQ, SIDE),
        "yr": (2, SEQ, SIDE),
        "td": (4, 320, LAT),
        "sd": (4, 320, LAT),
        "zd": (NZ, 40, LAT),
        "zr": (NZ, 40, LAT),
        "tu": (4, 256, LAT),
        "su": (4, 256, LAT),
        "zu": (NZ, 32, LAT),
        "zv": (NZ, 32, LAT),
    }
    sems = {
        "xssem": dma,
        "xfsem": dma((2, 4)),
        "xrsem": dma((2,)),
        "yssem": dma,
        "yfsem": dma((2, 4)),
        "yrsem": dma((2,)),
        "psem": dma,
        "qsem": dma((2,)),
        "asem": dma((2,)),
        "dsem": dma,
        "dr": dma((3,)),
        "usem": dma,
        "ur": dma((3,)),
        "zsem": dma((2,)),
        "zrecv": dma((2, NZ - 1)),
    }
    return {**{k: pltpu.VMEM(v, bf16) for k, v in buffers.items()}, **sems}


def place_kernel(act, grad, down, qk, up, act_o, grad_o, down_o, qk_o, up_o):
    act_o[...] = act[...]
    grad_o[...] = grad[...]
    down_o[...] = down[...].reshape(28, 1, LAT)
    qk_o[...] = qk[...]
    up_o[...] = up[...].reshape(28, 1, LAT)


def place_results(results):
    return pl.pallas_call(
        place_kernel,
        name="place_results",
        out_shape=[
            shaped(2, *TOKENS),
            shaped(2, *TOKENS),
            shaped(28, 1, LAT, dtype=f32),
            shaped(2, LAT, dtype=f32),
            shaped(28, 1, LAT, dtype=f32),
        ],
        in_specs=[VMEM] * 5,
        out_specs=[VMEM] * 5,
    )(*results)


def swap(value):
    return lax.ppermute(value, "section", [(0, 1), (1, 0)])


def body(x_in, dy_out, routes, gates, w_down, w_qk, w_up, e_gate, e_up, e_down):
    section = lax.axis_index("section")
    attn_own = (w_down[0], w_qk[0], w_up[0])
    experts_own = (e_gate[0, 0], e_up[0, 0], e_down[0, 0])
    attn = attn_own + tuple(swap(w) for w in attn_own)
    def both_layers(table):
        other = swap(lax.dynamic_index_in_dim(table, 1 - section, 0, keepdims=False))
        own = lax.dynamic_index_in_dim(table, section, 0, keepdims=False)
        return (jnp.where(section == 0, own, other), jnp.where(section == 0, other, own))

    route_cols = both_layers(routes[0, :, 0])
    gate_cols = both_layers(gates[0, :, 0])
    route_rows = tuple(r.reshape(1, SEQ) for r in route_cols)

    whole = {
        "x": (x_in[:, 0], VMEM),
        "dy": (dy_out[:, 0], VMEM),
        **{f"route_row{k}": (route_rows[k], VMEM) for k in range(2)},
        **{f"route_col{k}": (route_cols[k], VMEM) for k in range(2)},
        **{f"gate_col{k}": (gate_cols[k], VMEM) for k in range(2)},
        **named("attn", [(w, ANY) for w in attn]),
        **named("expert", [(w, ANY) for w in experts_own]),
    }
    kept = fused(
        forward_run,
        "forward",
        whole,
        {
            "act0": shaped(*TOKENS),
            **kept_shapes(0),
            **kept_shapes(1),
            "gate0": shaped(*PRE, dtype=f32),
            "up0": shaped(*PRE, dtype=f32),
            "part1": shaped(*ROWS),
            "homeb": shaped(*HOME),
        },
        {
            **COMMON,
            **Experts.scratch(2),
            "hidden": pltpu.VMEM(PRE, bf16),
            **dispatch_scratch("a"),
            **dispatch_scratch("b"),
            **dispatch_scratch("c"),
            **combine_scratch("a"),
            **combine_scratch("b", skip=("homeb",)),
        },
        0,
    )
    part1, back1 = kept.pop("part1"), kept.pop("homeb")
    done = fused(
        backward_run,
        "backward",
        {
            **whole,
            **{k: (v, VMEM) for k, v in kept.items()},
            "parta": (part1, VMEM),
            "back1": (back1, VMEM),
        },
        {
            "act_o": shaped(2, *TOKENS),
            "grad_o": shaped(2, *TOKENS),
            "down_o": shaped(28, LAT, dtype=f32),
            "qk_o": shaped(2, LAT, dtype=f32),
            "up_o": shaped(28, LAT, dtype=f32),
        },
        {
            **COMMON,
            "act1": pltpu.VMEM(TOKENS, bf16),
            **factor_scratch(0),
            **factor_scratch(1),
            **grads_scratch(),
            **Experts.scratch(1),
            **dispatch_scratch("a"),
            **combine_scratch("a", skip=("parta",)),
            **combine_scratch("b"),
        },
        1,
    )
    activations, grads_in, g_down, g_qk, g_up_t = place_results(list(done.values()))
    return (
        activations[None, :, None],
        grads_in[None, :, None],
        jnp.swapaxes(g_down, 0, 1),
        g_qk[None],
        jnp.swapaxes(g_up_t, 0, 1),
    )


def solution(mesh):
    placed = (
        P(None, ("expert", "dp"), None, None),
        P(None, ("expert", "dp"), None, None),
        P("section", None, ("expert", "dp"), None, None),
        P("section", None, ("expert", "dp"), None, None),
        P("section", None, None),
        P("section", None, None),
        P("section", None, None),
        P("section", "expert", None, "dp"),
        P("section", "expert", None, "dp"),
        P("section", "expert", "dp", None),
    )
    return jax.shard_map(
        body,
        mesh=mesh,
        in_specs=placed,
        out_specs=(
            P("section", None, ("expert", "dp"), None, None),
            P("section", None, ("expert", "dp"), None, None),
            P("section", ("expert", "dp"), None),
            P("section", ("expert", "dp"), None),
            P("section", ("expert", "dp"), None),
        ),
        check_vma=False,
    )
```

```python
import functools

import jax
import jax.numpy as jnp
from jax import lax
from jax.experimental import pallas as pl
from jax.experimental.pallas import tpu as pltpu
from jax.sharding import PartitionSpec as P

epsilon = 1e-06
WIDTH = 3584
LAT = 256
FF = 256
SEQ = 64
EXPERTS = 32
DP = 4
CAP = 3
NZ = 8
NY = 4
PIECE = 896
PIECES = 4
BLOCK = (PIECES, CAP * PIECE)
PACKED = PIECES * EXPERTS
ORDER = (0, 1, 7, 2, 6, 3, 5, 4)
MESH = pl.DeviceIdType.MESH
VMEM = pl.BlockSpec(memory_space=pltpu.VMEM)
ANY = pl.BlockSpec(memory_space=pl.ANY)
bf16 = jnp.bfloat16
f32 = jnp.float32


def dot(left, right):
    return jnp.dot(left, right, preferred_element_type=f32)


def times_t(left, right):
    return lax.dot_general(left, right, (((1,), (1,)), ((), ())), preferred_element_type=f32)


def t_times(left, right):
    return lax.dot_general(left, right, (((0,), (0,)), ((), ())), preferred_element_type=f32)


def rms_norm(values):
    inv_rms = lax.rsqrt(jnp.mean(values * values, axis=-1, keepdims=True) + epsilon)
    return (values * inv_rms, inv_rms)


def rms_back(normed, inv_rms, upstream):
    return inv_rms * (upstream - normed * jnp.mean(upstream * normed, axis=-1, keepdims=True))


def silu_parts(gate_pre):
    sigmoid = jax.nn.sigmoid(gate_pre)
    return (gate_pre * sigmoid, sigmoid * (1.0 + gate_pre * (1.0 - sigmoid)))


def spread_matrix():
    rows = lax.broadcasted_iota(jnp.int32, (PACKED, PACKED), 0)
    cols = lax.broadcasted_iota(jnp.int32, (PACKED, PACKED), 1)
    return ((rows % PIECES) * EXPERTS + rows // PIECES == cols).astype(f32).astype(bf16)


def gather_matrix():
    rows = lax.broadcasted_iota(jnp.int32, (PACKED, PACKED), 0)
    cols = lax.broadcasted_iota(jnp.int32, (PACKED, PACKED), 1)
    return ((cols % PIECES) * EXPERTS + cols // PIECES == rows).astype(f32).astype(bf16)


def slot_rows(route_row):
    experts = lax.broadcasted_iota(jnp.int32, (EXPERTS, SEQ), 0)
    hot = (experts == route_row).astype(f32)
    before = lax.broadcasted_iota(jnp.int32, (SEQ, SEQ), 0) < lax.broadcasted_iota(
        jnp.int32, (SEQ, SEQ), 1
    )
    rank = dot(hot.astype(bf16), before.astype(f32).astype(bf16))
    return jnp.concatenate(
        [(hot * (rank == float(s)).astype(f32)).astype(bf16) for s in range(CAP)], axis=0
    )


def slot_columns(route_col):
    experts = lax.broadcasted_iota(jnp.int32, (SEQ, EXPERTS), 1)
    hot = (experts == route_col).astype(f32)
    before = lax.broadcasted_iota(jnp.int32, (SEQ, SEQ), 0) > lax.broadcasted_iota(
        jnp.int32, (SEQ, SEQ), 1
    )
    rank = dot(before.astype(f32).astype(bf16), hot.astype(bf16))
    return jnp.concatenate(
        [(hot * (rank == float(s)).astype(f32)).astype(bf16) for s in range(CAP)], axis=1
    )


def pack_tokens(values_b, route_row, packed_ref, blocks_ref):
    picked = dot(slot_rows(route_row), values_b).astype(bf16)
    for s in range(CAP):
        for r in range(PIECES):
            packed_ref[r * EXPERTS : (r + 1) * EXPERTS, s * PIECE : (s + 1) * PIECE] = picked[
                s * EXPERTS : (s + 1) * EXPERTS, r * PIECE : (r + 1) * PIECE
            ]
    blocks_ref[...] = dot(spread_matrix(), packed_ref[...]).astype(bf16).reshape(HOME)


def unpack_tokens(blocks_ref, route_col, token_ref):
    packed = dot(gather_matrix(), blocks_ref[...].reshape(PACKED, BLOCK[1])).astype(bf16)
    columns = slot_columns(route_col)
    for r in range(PIECES):
        stacked = jnp.concatenate(
            [
                packed[r * EXPERTS : (r + 1) * EXPERTS, s * PIECE : (s + 1) * PIECE]
                for s in range(CAP)
            ],
            axis=0,
        )
        token_ref[:, r * PIECE : (r + 1) * PIECE] = dot(columns, stacked)


def places():
    e = lax.axis_index("expert")
    d = lax.axis_index("dp")
    return e, d, e // NY, e % NY, (d + 1) % DP, (d + DP - 1) % DP, (d + 2) % DP


def greet(e, right, left, more=()):
    barrier = pltpu.get_barrier_semaphore()
    for k in range(1, EXPERTS):
        pl.semaphore_signal(
            barrier, inc=1, device_id={"expert": (e + k) % EXPERTS}, device_id_type=MESH
        )
    for side in (right, left):
        pl.semaphore_signal(barrier, inc=1, device_id={"dp": side}, device_id_type=MESH)
    partner = {"section": 1 - lax.axis_index("section")}
    for peer in (partner, *more):
        pl.semaphore_signal(barrier, inc=1, device_id=peer, device_id_type=MESH)


def greeted(more=0):
    pl.semaphore_wait(pltpu.get_barrier_semaphore(), EXPERTS + 2 + more)


def remote(src, dst, send, recv, where):
    return pltpu.make_async_remote_copy(
        src_ref=src, dst_ref=dst, send_sem=send, recv_sem=recv, device_id=where, device_id_type=MESH
    )


class Dispatch:
    sems = (
        pltpu.SemaphoreType.DMA,
        pltpu.SemaphoreType.DMA,
        pltpu.SemaphoreType.DMA((NZ,)),
        pltpu.SemaphoreType.DMA((NZ,)),
        pltpu.SemaphoreType.DMA((NZ,)),
        pltpu.SemaphoreType.DMA((NZ,)),
    )

    def __init__(self, blk, rows, sems):
        self.blk, self.rows = blk, rows
        self.s1, self.sx, self.r1, self.rl, self.rr, self.ro = sems
        self.e, self.d, self.z, self.y, self.right, self.left, self.opp = places()

    def start(self):
        for j in ORDER:
            for dy in range(NY):
                spot = self.rows.at[self.d * EXPERTS + self.e]
                if j == 0 and dy == 0:
                    pltpu.make_async_copy(self.blk.at[self.e], spot, self.r1.at[0]).start()
                else:
                    peer = ((self.z + j) % NZ) * NY + (self.y + dy) % NY
                    remote(
                        self.blk.at[peer], spot, self.s1, self.r1.at[(NZ - j) % NZ], {"expert": peer}
                    ).start()

    def group(self, owner, j):
        return self.rows.at[pl.ds(owner * EXPERTS + ((self.z + j) % NZ) * NY, NY)]

    def arrived(self, ref, sem):
        remote(ref, ref, self.s1, sem, {"dp": self.right}).wait_recv()

    def forward(self, i):
        j = ORDER[i]
        mine = self.group(self.d, j)
        self.arrived(mine, self.r1.at[j])
        remote(mine, mine, self.sx, self.rl.at[j], {"dp": self.right}).start()
        remote(mine, mine, self.sx, self.rr.at[j], {"dp": self.left}).start()

    def relay(self, i):
        j = ORDER[i]
        owner, sem, to = (
            (self.left, self.rl, self.right) if i % 2 == 0 else (self.right, self.rr, self.left)
        )
        ref = self.group(owner, j)
        self.arrived(ref, sem.at[j])
        remote(ref, ref, self.sx, self.ro.at[j], {"dp": to}).start()

    def wait_right(self):
        for i, j in enumerate(ORDER):
            if i % 2 == 0:
                self.arrived(self.group(self.right, j), self.rr.at[j])

    def wait_left(self):
        for i, j in enumerate(ORDER):
            if i % 2 == 1:
                self.arrived(self.group(self.left, j), self.rl.at[j])

    def wait_far(self):
        for j in ORDER:
            self.arrived(self.group(self.opp, j), self.ro.at[j])

    def chunks(self, use, near):
        @pl.loop(0, DP)
        def _(k):
            pl.when(k == 1)(self.wait_right)
            pl.when(k == 2)(self.wait_left)
            pl.when(k == 3)(self.wait_far)
            use((self.d + k + k // 2 - 2 * (k // 3)) % DP)
            pl.when(k == 2)(near)

    def drain(self):
        sent = self.blk.at[pl.ds(0, EXPERTS - 1)]
        remote(sent, sent, self.s1, self.r1.at[0], {"dp": self.right}).wait_send()
        sent = self.rows.at[pl.ds(0, 3 * EXPERTS)]
        remote(sent, sent, self.sx, self.r1.at[0], {"dp": self.right}).wait_send()


class Combine:
    sems = (
        pltpu.SemaphoreType.DMA,
        pltpu.SemaphoreType.DMA,
        pltpu.SemaphoreType.DMA((NZ,)),
        pltpu.SemaphoreType.DMA((NZ,)),
        pltpu.SemaphoreType.DMA((NZ,)),
        pltpu.SemaphoreType.DMA,
    )
    buffers = (pltpu.VMEM((EXPERTS, *BLOCK), bf16),) * 5

    def __init__(self, part, out, buffers, sems):
        self.part, self.out = part, out
        self.relayed, self.relay_sum, self.from_left, self.from_right, self.final = buffers
        self.sx, self.s1, self.ra, self.rl, self.rr, self.rh = sems
        self.e, self.d, self.z, self.y, self.right, self.left, self.opp = places()

    def group(self, owner, j):
        return self.part.at[pl.ds(owner * EXPERTS + ((self.z + j) % NZ) * NY, NY)]

    def spot(self, ref, i):
        return ref.at[pl.ds(i * NY, NY)]

    def arrived(self, ref, sem):
        remote(ref, ref, self.s1, sem, {"dp": self.right}).wait_recv()

    def start_far(self):
        for i, j in enumerate(ORDER):
            side = self.right if i % 2 == 0 else self.left
            remote(
                self.group(self.opp, j), self.spot(self.relayed, i), self.sx, self.ra.at[i], {"dp": side}
            ).start()

    def start_near(self):
        for i, j in enumerate(ORDER):
            if i % 2 == 0:
                ref, to, sem, side = self.left, self.from_right, self.rr, self.left
            else:
                ref, to, sem, side = self.right, self.from_left, self.rl, self.right
            remote(self.group(ref, j), self.spot(to, i), self.sx, sem.at[i], {"dp": side}).start()

    def relay(self, i):
        j = ORDER[i]
        self.arrived(self.spot(self.relayed, i), self.ra.at[i])
        side, to, sem = (
            (self.right, self.from_left, self.rl)
            if i % 2 == 0
            else (self.left, self.from_right, self.rr)
        )
        self.spot(self.relay_sum, i)[...] = (
            self.spot(self.relayed, i)[...].astype(f32) + self.group(side, j)[...].astype(f32)
        ).astype(bf16)
        remote(
            self.spot(self.relay_sum, i), self.spot(to, i), self.sx, sem.at[i], {"dp": side}
        ).start()

    def finish(self, i):
        j = ORDER[i]
        self.arrived(self.spot(self.from_left, i), self.rl.at[i])
        self.arrived(self.spot(self.from_right, i), self.rr.at[i])
        self.spot(self.final, i)[...] = (
            self.group(self.d, j)[...].astype(f32)
            + self.spot(self.from_left, i)[...].astype(f32)
            + self.spot(self.from_right, i)[...].astype(f32)
        ).astype(bf16)
        for dy in range(NY):
            yy = (self.y + dy) % NY
            spot = self.out.at[self.e]
            if j == 0 and dy == 0:
                pltpu.make_async_copy(self.final.at[i * NY + yy], spot, self.rh).start()
            else:
                peer = ((self.z + j) % NZ) * NY + yy
                remote(
                    self.final.at[i * NY + yy], spot, self.s1, self.rh, {"expert": peer}
                ).start()

    def arrive(self):
        self.arrived(self.out, self.rh)

    def drain(self):
        sent = self.part.at[pl.ds(0, 3 * EXPERTS)]
        remote(sent, sent, self.sx, self.rh, {"dp": self.right}).wait_send()
        sent = self.part.at[pl.ds(0, EXPERTS - 1)]
        remote(sent, sent, self.s1, self.rh, {"dp": self.right}).wait_send()


def fetch(layer, pairs, sems):
    mine = lax.axis_index("section") == layer
    for k, (own, other, dst) in enumerate(pairs):

        @pl.when(mine)
        def _():
            pltpu.make_async_copy(own, dst, sems.at[k]).start()

        @pl.when(jnp.logical_not(mine))
        def _():
            pltpu.make_async_copy(other, dst, sems.at[k]).start()

    def wait(k):
        own, _, dst = pairs[k]
        pltpu.make_async_copy(own, dst, sems.at[k]).wait()

    return wait


def attend(
    inputs, route_row, wd, wq, wu, wait, packed, blocks, residual, latent_o, queries_o, probs_o, mixed_o
):
    normed, _ = rms_norm(inputs.astype(f32))
    wait(0)
    latent = dot(normed.astype(bf16), wd[...]).astype(bf16)
    wait(1)
    queries = dot(latent, wq[...]).astype(bf16)
    scores = times_t(queries, latent) * (LAT ** (-0.5))
    causal = lax.broadcasted_iota(jnp.int32, (SEQ, SEQ), 0) >= lax.broadcasted_iota(
        jnp.int32, (SEQ, SEQ), 1
    )
    scores = jnp.where(causal, scores, -1e30)
    exponent = jnp.exp(scores - jnp.max(scores, axis=-1, keepdims=True))
    probs = exponent / jnp.sum(exponent, axis=-1, keepdims=True)
    mixed = dot(probs.astype(bf16), latent).astype(bf16)
    wait(2)
    resid = (inputs.astype(f32) + dot(mixed, wu[...])).astype(bf16)
    residual[...] = resid
    latent_o[...] = latent
    queries_o[...] = queries
    probs_o[...] = probs
    mixed_o[...] = mixed
    normed2, _ = rms_norm(resid.astype(f32))
    pack_tokens(normed2.astype(bf16), route_row, packed, blocks)


def attend_back(
    upstream, inputs, resid, latent, queries, probs, mixed, w, wait, tokens, normed_o, d_latent_o,
    d_queries_o, d_resid_o, grad,
):
    normed2, inv2 = rms_norm(resid.astype(f32))
    d_resid = upstream.astype(f32) + rms_back(normed2, inv2, tokens[...])
    d_resid_b = d_resid.astype(bf16)
    d_resid_o[...] = d_resid_b
    tokens[...] = d_resid
    wd, wq, wu = w
    wait(2)
    d_mixed = times_t(d_resid_b, wu[...]).astype(bf16)
    d_probs = times_t(d_mixed, latent)
    d_scores = (
        probs * (d_probs - jnp.sum(d_probs * probs, axis=-1, keepdims=True)) * (LAT ** (-0.5))
    ).astype(bf16)
    d_queries = dot(d_scores, latent).astype(bf16)
    wait(1)
    d_latent = (
        t_times(probs.astype(bf16), d_mixed)
        + t_times(d_scores, queries)
        + times_t(d_queries, wq[...])
    ).astype(bf16)
    wait(0)
    d_normed = times_t(d_latent, wd[...])
    normed, inv = rms_norm(inputs.astype(f32))
    normed_o[...] = normed.astype(bf16)
    d_latent_o[...] = d_latent
    d_queries_o[...] = d_queries
    grad[...] = (tokens[...] + rms_back(normed, inv, d_normed)).astype(bf16)


CHUNK = CAP * EXPERTS


def unpack_rows(rows, wide, g):
    packed = dot(
        gather_matrix(), rows[pl.ds(g * EXPERTS, EXPERTS)].reshape(PACKED, BLOCK[1])
    ).astype(bf16)
    for s in range(CAP):
        for r in range(PIECES):
            wide[s * EXPERTS : (s + 1) * EXPERTS, r * PIECE : (r + 1) * PIECE] = packed[
                r * EXPERTS : (r + 1) * EXPERTS, s * PIECE : (s + 1) * PIECE
            ]
    return wide[...]


def pack_rows(piece, packed, out, g):
    for r in range(PIECES):
        rows = piece(slice(r * PIECE, (r + 1) * PIECE)).astype(bf16)
        for s in range(CAP):
            packed[r * EXPERTS : (r + 1) * EXPERTS, s * PIECE : (s + 1) * PIECE] = rows[
                s * EXPERTS : (s + 1) * EXPERTS
            ]
    out[pl.ds(g * EXPERTS, EXPERTS)] = (
        dot(spread_matrix(), packed[...]).astype(bf16).reshape(EXPERTS, *BLOCK)
    )


def chunk_rows(g):
    return pl.ds(pl.multiple_of(g * CHUNK, CHUNK), CHUNK)


def expert_out(hidden, dw):
    return lambda cols: dot(hidden, dw[:, cols])


def expert_back(rows, gate_pre, up_pre, gw, uw, dw):
    d_hidden = times_t(rows, dw[...])
    activated, slope = silu_parts(gate_pre)
    d_gate = (d_hidden * up_pre * slope).astype(bf16)
    d_up = (d_hidden * activated).astype(bf16)
    return lambda cols: times_t(d_gate, gw[cols, :]) + times_t(d_up, uw[cols, :])


class Refs:
    def __init__(self, names, refs):
        for name, ref in zip(names, refs, strict=True):
            setattr(self, name, ref)

    def some(self, prefix, count):
        return tuple(getattr(self, f"{prefix}{k}") for k in range(count))


def named(prefix, items):
    return {f"{prefix}{k}": item for k, item in enumerate(items)}


def fused(run, name, ins, outs, scratch, number):
    names = [*ins, *outs, *scratch]

    def kernel(*refs):
        run(Refs(names, refs))

    results = pl.pallas_call(
        kernel,
        name=name,
        out_shape=list(outs.values()),
        in_specs=[spec for _, spec in ins.values()],
        out_specs=[VMEM] * len(outs),
        scratch_shapes=list(scratch.values()),
        compiler_params=pltpu.CompilerParams(
            collective_id=number, has_side_effects=True, vmem_limit_bytes=60 * 1024 * 1024
        ),
    )(*[array for array, _ in ins.values()])
    return dict(zip(outs, results))


def shaped(*shape, dtype=bf16):
    return jax.ShapeDtypeStruct(shape, dtype)


TOKENS = (SEQ, WIDTH)
ROWS = (DP * EXPERTS, *BLOCK)
HOME = (EXPERTS, *BLOCK)
PRE = (CAP * DP * EXPERTS, FF)
COMMON = {
    "tokens": pltpu.VMEM(TOKENS, f32),
    "wide": pltpu.VMEM((CHUNK, WIDTH), bf16),
    "packed": pltpu.VMEM((PACKED, BLOCK[1]), bf16),
    "w0": pltpu.VMEM((WIDTH, LAT), bf16),
    "w1": pltpu.VMEM((LAT, LAT), bf16),
    "w2": pltpu.VMEM((LAT, WIDTH), bf16),
    "wsem": pltpu.SemaphoreType.DMA((3,)),
}
EXPERT_WEIGHTS = ((WIDTH, FF), (WIDTH, FF), (FF, WIDTH))


def fetch_attn(refs, layer):
    attn = refs.some("attn", 6)
    return fetch(layer, [(attn[k], attn[3 + k], getattr(refs, f"w{k}")) for k in range(3)], refs.wsem)


class Experts:
    @staticmethod
    def scratch(layers):
        return {
            **named("v", [pltpu.VMEM((layers, *shape), bf16) for shape in EXPERT_WEIGHTS]),
            "vsem": pltpu.SemaphoreType.DMA((layers, 3)),
            "vsent": pltpu.SemaphoreType.DMA((3,)),
        }

    def __init__(self, refs, layers):
        self.s = lax.axis_index("section")
        self.own = refs.some("expert", 3)
        self.v = refs.some("v", 3)
        self.sem, self.sent, self.layers = refs.vsem, refs.vsent, layers

    def each(self, act):
        def run():
            for k in range(3):
                act(k)

        if self.layers == 1:
            pl.when(self.s == 0)(run)
        else:
            run()

    def place(self):
        return self.s if self.layers == 2 else 0

    def copy(self, k):
        return pltpu.make_async_copy(
            self.own[k], self.v[k].at[self.place()], self.sem.at[self.place(), k]
        )

    def give(self, k):
        return remote(
            self.own[k],
            self.v[k].at[self.place()],
            self.sent.at[k],
            self.sem.at[self.place(), k],
            {"section": 1 - self.s},
        )

    def start(self):
        self.each(lambda k: self.copy(k).start())

    def send(self):
        self.each(lambda k: self.give(k).start())

    def drain(self):
        self.each(lambda k: self.give(k).wait_send())

    def ready(self, layer):
        for k in range(3):
            pltpu.make_async_copy(
                self.own[k], self.v[k].at[layer], self.sem.at[layer, k]
            ).wait()
        return [ref.at[layer] for ref in self.v]


def dispatch_of(refs, tag):
    return Dispatch(
        getattr(refs, "blk" + tag), getattr(refs, "rows" + tag), refs.some("ds" + tag + "_", 6)
    )


def dispatch_scratch(tag):
    return {
        "blk" + tag: pltpu.VMEM(HOME, bf16),
        "rows" + tag: pltpu.VMEM(ROWS, bf16),
        **named("ds" + tag + "_", Dispatch.sems),
    }


def combine_of(refs, tag):
    return Combine(
        getattr(refs, "part" + tag),
        getattr(refs, "home" + tag),
        refs.some("cb" + tag + "_", 5),
        refs.some("cs" + tag + "_", 6),
    )


def combine_scratch(tag, skip=()):
    whole = {
        "part" + tag: pltpu.VMEM(ROWS, bf16),
        "home" + tag: pltpu.VMEM(HOME, bf16),
        **named("cb" + tag + "_", Combine.buffers),
        **named("cs" + tag + "_", Combine.sems),
    }
    return {k: v for k, v in whole.items() if k not in skip}


def kept_shapes(layer):
    return {
        f"resid{layer}": shaped(*TOKENS),
        f"latent{layer}": shaped(SEQ, LAT),
        f"queries{layer}": shaped(SEQ, LAT),
        f"probs{layer}": shaped(SEQ, SEQ, dtype=f32),
        f"mixed{layer}": shaped(SEQ, LAT),
    }


def kept_refs(refs, layer):
    return [getattr(refs, f"{k}{layer}") for k in ("resid", "latent", "queries", "probs", "mixed")]


def forward_run(refs):
    e, _, _, _, right, left, _ = places()
    section = lax.axis_index("section")
    greet(e, right, left)
    wait_w = fetch_attn(refs, 0)
    experts = Experts(refs, 2)
    experts.start()
    first, early, second = (dispatch_of(refs, tag) for tag in ("a", "b", "c"))
    out0, back1 = combine_of(refs, "a"), combine_of(refs, "b")
    w = refs.some("w", 3)

    attend(
        refs.x[section], refs.route_row0[...], *w, wait_w, refs.packed, refs.blka,
        *kept_refs(refs, 0),
    )
    wait_w = fetch_attn(refs, 1)
    greeted()
    first.start()
    experts.send()
    scaled = (refs.gate_col1[...] * refs.dy[section].astype(f32)).astype(bf16)
    pack_tokens(scaled, refs.route_row1[...], refs.packed, refs.blkb)
    for i in range(NZ):
        first.forward(i)
        if i >= 2:
            first.relay(i - 2)
        if i == 5:
            early.start()
    first.relay(6)
    first.relay(7)
    gw, uw, dw = experts.ready(0)

    def forward0(g):
        at = chunk_rows(g)
        rows = unpack_rows(refs.rowsa, refs.wide, g)
        gate_pre, up_pre = dot(rows, gw[...]), dot(rows, uw[...])
        refs.gate0[at, :] = gate_pre
        refs.up0[at, :] = up_pre
        hidden = (silu_parts(gate_pre)[0] * up_pre).astype(bf16)
        pack_rows(expert_out(hidden, dw), refs.packed, out0.part, g)

    first.chunks(forward0, out0.start_near)
    out0.start_far()
    for i in range(NZ):
        out0.relay(i)
    for i in range(NZ):
        early.forward(i)
    for i in range(NZ):
        out0.finish(i)
    out0.arrive()

    unpack_tokens(refs.homea, refs.route_col0[...], refs.tokens)
    act0 = (refs.resid0[...].astype(f32) + refs.gate_col0[...] * refs.tokens[...]).astype(bf16)
    refs.act0[...] = act0
    for i in range(4):
        early.relay(i)
    attend(act0, refs.route_row1[...], *w, wait_w, refs.packed, refs.blkc, *kept_refs(refs, 1))
    second.start()
    for i in range(4, NZ):
        early.relay(i)
    for i in range(NZ):
        second.forward(i)
        if i >= 2:
            second.relay(i - 2)
    second.relay(6)
    second.relay(7)
    early.wait_right()
    early.wait_left()
    early.wait_far()
    gw1, uw1, dw1 = experts.ready(1)

    def both1(g):
        at = chunk_rows(g)
        rows = unpack_rows(refs.rowsc, refs.wide, g)
        gate_pre, up_pre = dot(rows, gw1[...]), dot(rows, uw1[...])
        refs.hidden[at, :] = (silu_parts(gate_pre)[0] * up_pre).astype(bf16)
        rows = unpack_rows(refs.rowsb, refs.wide, g)
        pack_rows(
            expert_back(rows, gate_pre, up_pre, gw1, uw1, dw1), refs.packed, back1.part, g
        )

    def out1(g):
        pack_rows(expert_out(refs.hidden[chunk_rows(g), :], dw1), refs.packed, refs.part1, g)

    second.chunks(both1, back1.start_near)
    back1.start_far()
    pl.loop(0, 2)(out1)
    for i in range(NZ):
        back1.relay(i)
    pl.loop(2, DP)(out1)
    for i in range(NZ):
        back1.finish(i)
    back1.arrive()
    for each in (first, early, second, out0, back1, experts):
        each.drain()


def backward_run(refs):
    e, _, _, _, right, left, _ = places()
    section = lax.axis_index("section")
    grads = Grads(refs)
    more = grads.peers()
    greet(e, right, left, more)
    wait_w = fetch_attn(refs, 1)
    experts = Experts(refs, 1)
    experts.start()
    again = dispatch_of(refs, "a")
    out1, back0 = combine_of(refs, "a"), combine_of(refs, "b")
    w = refs.some("w", 3)

    unpack_tokens(refs.back1, refs.route_col1[...], refs.tokens)
    greeted(len(more))
    out1.start_far()
    out1.start_near()
    experts.send()
    attend_back(
        refs.dy[section], refs.act0[...], *[ref[...] for ref in kept_refs(refs, 1)], w, wait_w,
        refs.tokens, refs.n1, refs.dl1, refs.dq1, refs.dr1, refs.grad1,
    )
    wait_w = fetch_attn(refs, 0)
    scaled = (refs.gate_col0[...] * refs.grad1[...].astype(f32)).astype(bf16)
    pack_tokens(scaled, refs.route_row0[...], refs.packed, refs.blka)
    again.start()
    for i in range(NZ):
        again.forward(i)
        if i >= 2:
            again.relay(i - 2)
    again.relay(6)
    again.relay(7)
    gw, uw, dw = experts.ready(0)

    def backward0(g):
        at = chunk_rows(g)
        rows = unpack_rows(refs.rowsa, refs.wide, g)
        pack_rows(
            expert_back(rows, refs.gate0[at, :], refs.up0[at, :], gw, uw, dw),
            refs.packed,
            back0.part,
            g,
        )

    again.chunks(backward0, back0.start_near)
    back0.start_far()
    grads.lay_x(1, refs.n1, refs.dl1, refs.latent1, refs.dq1)
    for i in range(NZ):
        back0.relay(i)
    for i in range(NZ):
        out1.relay(i)
    grads.x_ring.start(1)
    grads.lay_y(1, refs.dr1, refs.mixed1)
    grads.y_ring.start(1)
    for i in range(NZ):
        back0.finish(i)
    back0.arrive()
    unpack_tokens(refs.homeb, refs.route_col0[...], refs.tokens)
    for i in range(NZ):
        out1.finish(i)
    grads.x_ring.relay(1)
    grads.y_ring.relay(1)
    attend_back(
        refs.grad1[...], refs.x[section], *[ref[...] for ref in kept_refs(refs, 0)], w, wait_w,
        refs.tokens, refs.n0, refs.dl0, refs.dq0, refs.dr0, refs.grad0,
    )
    grads.lay_x(0, refs.n0, refs.dl0, refs.latent0, refs.dq0)
    grads.x_ring.start(0)
    grads.x_ring.own()
    grads.lay_y(0, refs.dr0, refs.mixed0)
    grads.y_ring.start(0)
    grads.y_ring.own()
    grads.trade(1, refs.grad_o, refs.grad0, refs.grad1)
    out1.arrive()
    unpack_tokens(refs.homea, refs.route_col1[...], refs.tokens)
    refs.act1[...] = (
        refs.resid1[...].astype(f32) + refs.gate_col1[...] * refs.tokens[...]
    ).astype(bf16)
    grads.trade(0, refs.act_o, refs.act0, refs.act1)
    grads.x_ring.relay(0)
    grads.y_ring.relay(0)
    grads.sums()
    for each in (again, out1, back0, experts, grads):
        each.drain()


def factor_scratch(layer):
    return {
        f"n{layer}": pltpu.VMEM(TOKENS, bf16),
        f"dl{layer}": pltpu.VMEM((SEQ, LAT), bf16),
        f"dq{layer}": pltpu.VMEM((SEQ, LAT), bf16),
        f"dr{layer}": pltpu.VMEM(TOKENS, bf16),
        f"grad{layer}": pltpu.VMEM(TOKENS, bf16),
    }


ROUND = 1792
SIDE = 1280


def quarter_matrix(first_is_dp):
    out = lax.broadcasted_iota(jnp.int32, (1, 1024), 1)
    one, two, zz, i = out // 256, (out // 64) % 4, (out // 32) % 2, out % 32
    y, x = (two, one) if first_is_dp else (one, two)
    source = jnp.where(i < 28, zz * 448 + y * 112 + x * 28 + i, -1)
    return (lax.broadcasted_iota(jnp.int32, (896, 1024), 0) == source).astype(f32).astype(bf16)


def small_matrix():
    out = lax.broadcasted_iota(jnp.int32, (1, 1024), 1)
    x, y, z, i = out // 256, (out // 64) % 4, (out // 8) % 8, out % 8
    source = jnp.where(i < 2, z * 32 + y * 8 + x * 2 + i, -1)
    return (lax.broadcasted_iota(jnp.int32, (LAT, 1024), 0) == source).astype(f32).astype(bf16)


def lay_out(factor, matrix, sent, layer):
    stacked = jnp.concatenate([factor[:, c * 896 : (c + 1) * 896] for c in range(4)], axis=0)
    moved = dot(stacked, matrix).astype(bf16)
    for q in range(4):
        for c in range(4):
            sent[layer, q, :, c * 256 : (c + 1) * 256] = moved[
                c * SEQ : (c + 1) * SEQ, q * 256 : (q + 1) * 256
            ]


class Ring:
    def __init__(self, section, position, near, sent, got, relay, ssem, fsem, rsem):
        self.section, self.position, self.near = section, position, near
        self.sent, self.got, self.relay_buf = sent, got, relay
        self.ssem, self.fsem, self.rsem = ssem, fsem, rsem

    def start(self, layer):
        pos, s = self.position, self.section
        way = 1 if layer == 0 else 3
        remote(
            self.sent.at[layer, (pos + 2) % 4],
            self.relay_buf.at[layer],
            self.ssem,
            self.rsem.at[layer],
            self.near(way),
        ).start()
        for step, back in ((1, 1), (3, 0)):
            remote(
                self.sent.at[layer, (pos + step) % 4],
                self.got.at[s, pos],
                self.ssem,
                self.fsem.at[s, back],
                {**self.near(step), "section": layer},
            ).start()

    def own(self):
        pos, s = self.position, self.section
        pltpu.make_async_copy(self.sent.at[s, pos], self.got.at[s, pos], self.fsem.at[s, 3]).start()
        remote(
            self.sent.at[1 - s, pos],
            self.got.at[s, pos],
            self.ssem,
            self.fsem.at[s, 3],
            {"section": 1 - s},
        ).start()

    def relay(self, layer):
        way = 1 if layer == 0 else 3
        buf = self.relay_buf.at[layer]
        remote(buf, buf, self.ssem, self.rsem.at[layer], self.near(1)).wait_recv()
        origin = (self.position + 4 - way) % 4
        remote(
            buf,
            self.got.at[self.section, origin],
            self.ssem,
            self.fsem.at[self.section, 2],
            {**self.near(way), "section": layer},
        ).start()

    def arrive(self):
        for m in range(2):
            for k, step in enumerate((1, 3, 2, 0)):
                ref = self.got.at[m, (self.position + step) % 4]
                remote(ref, ref, self.ssem, self.fsem.at[m, k], self.near(1)).wait_recv()

    def drain(self):
        for layer in range(2):
            ref = self.sent.at[layer]
            remote(ref, ref, self.ssem, self.rsem.at[0], self.near(1)).wait_send()
        ref = self.sent.at[0, 0]
        remote(ref, ref, self.ssem, self.rsem.at[0], self.near(1)).wait_send()


def fold(pieces):
    total = pieces[0].astype(f32)
    for piece in pieces[1:]:
        total = total + piece.astype(f32)
    return total


class Grads:
    def __init__(self, refs):
        self.refs = refs
        self.s = lax.axis_index("section")
        _, self.d, self.z, self.y, _, _, _ = places()
        self.x_ring = Ring(
            self.s, self.d, self.near_x, refs.xs, refs.xg, refs.xr, refs.xssem, refs.xfsem, refs.xrsem
        )
        self.y_ring = Ring(
            self.s, self.y, self.near_y, refs.ys, refs.yg, refs.yr, refs.yssem, refs.yfsem, refs.yrsem
        )

    def near_x(self, k):
        return {"dp": (self.d + k) % 4}

    def near_y(self, k):
        return {"expert": self.z * NY + (self.y + k) % 4}

    def near_z(self, k):
        return {"expert": ((self.z + k) % NZ) * NY + self.y}

    def peers(self):
        other = {"section": 1 - self.s}
        return [
            {**self.near_x(1), **other},
            {**self.near_x(3), **other},
            {**self.near_y(1), **other},
            {**self.near_y(3), **other},
            self.near_x(2),
        ]

    def lay_x(self, layer, n, dl, la, dq):
        xs = self.refs.xs
        lay_out(n[...], quarter_matrix(True), xs, layer)
        moved = dot(la[...], small_matrix()).astype(bf16)
        for q in range(4):
            xs[layer, q, :, 1024:1280] = dl[...]
            xs[layer, q, :, 1280:1536] = moved[:, q * 256 : (q + 1) * 256]
            xs[layer, q, :, 1536:1792] = dq[...]

    def lay_y(self, layer, dres, mx):
        lay_out(dres[...], quarter_matrix(False), self.refs.ys, layer)
        for q in range(4):
            self.refs.ys[layer, q, :, 1024:1280] = mx[...]

    def trade(self, k, out, first_layer, second_layer):
        refs, s = self.refs, self.s
        for here, keep, give in ((0, first_layer, second_layer), (1, second_layer, first_layer)):

            @pl.when(s == here)
            def _():
                pltpu.make_async_copy(keep, out.at[s], refs.asem.at[k]).start()
                remote(give, out.at[s], refs.psem, refs.qsem.at[k], {"section": 1 - s}).start()

    def sums(self):
        refs, s, d, z, y = self.refs, self.s, self.d, self.z, self.y

        def rows(ring, start, width):
            got = ring.got
            return jnp.concatenate(
                [got[m, q, :, start : start + width] for m in range(2) for q in range(4)], axis=0
            )

        x_ring, y_ring = self.x_ring, self.y_ring
        y_ring.arrive()
        total = t_times(rows(y_ring, 0, 1024), rows(y_ring, 1024, 256)).astype(bf16)
        for q in range(4):
            for c in range(4):
                refs.tu[q, c * 64 : (c + 1) * 64, :] = total[c * 256 + q * 64 : c * 256 + (q + 1) * 64]
        for k in (2, 1, 3):
            remote(refs.tu.at[(d + k) % 4], refs.su.at[d], refs.usem, refs.ur.at[4 - k - 1], self.near_x(k)).start()
        x_ring.arrive()
        total = t_times(rows(x_ring, 0, 1024), rows(x_ring, 1024, 256)).astype(bf16)
        total_qk = t_times(rows(x_ring, 1280, 256), rows(x_ring, 1536, 256)).astype(bf16)
        for q in range(4):
            for c in range(4):
                refs.td[q, c * 64 : (c + 1) * 64, :] = total[c * 256 + q * 64 : c * 256 + (q + 1) * 64]
            refs.td[q, 256:320, :] = total_qk[q * 64 : (q + 1) * 64]
        for k in (2, 1, 3):
            remote(refs.td.at[(y + k) % 4], refs.sd.at[y], refs.dsem, refs.dr.at[4 - k - 1], self.near_y(k)).start()

        def gathered(buf, recv, position):
            for k in (1, 2, 3):
                ref = buf.at[(position + k) % 4]
                remote(ref, ref, refs.dsem, recv.at[k - 1], self.near_x(1)).wait_recv()
            return [buf[(position + k) % 4] for k in (1, 2, 3)]

        summed = fold([refs.td[y]] + gathered(refs.sd, refs.dr, y)).astype(bf16)
        for k in range(NZ):
            refs.zd[k, 0:32, :] = summed[k * 32 : (k + 1) * 32]
            refs.zd[k, 32:40, :] = summed[256 + k * 8 : 264 + k * 8]
        for k in range(1, NZ):
            remote(refs.zd.at[(z + k) % NZ], refs.zr.at[z], refs.zsem.at[0], refs.zrecv.at[0, NZ - k - 1], self.near_z(k)).start()
        summed = fold([refs.tu[d]] + gathered(refs.su, refs.ur, d)).astype(bf16)
        for k in range(NZ):
            refs.zu[k] = summed[k * 32 : (k + 1) * 32]
        for k in range(1, NZ):
            remote(refs.zu.at[(z + k) % NZ], refs.zv.at[z], refs.zsem.at[1], refs.zrecv.at[1, NZ - k - 1], self.near_z(k)).start()

        def last(own, buf, which):
            for k in range(1, NZ):
                ref = buf.at[(z + k) % NZ]
                remote(ref, ref, refs.zsem.at[0], refs.zrecv.at[which, k - 1], self.near_z(1)).wait_recv()
            return fold([own[z]] + [buf[(z + k) % NZ] for k in range(1, NZ)])

        mine = last(refs.zd, refs.zr, 0)
        refs.down_o[...] = mine[0:28]
        refs.qk_o[...] = mine[32:34]
        mine = last(refs.zu, refs.zv, 1)
        refs.up_o[...] = mine[0:28]

    def drain(self):
        refs = self.refs
        self.x_ring.drain()
        self.y_ring.drain()
        for k, (out, some) in enumerate(((refs.act_o, refs.act0), (refs.grad_o, refs.grad0))):
            pltpu.make_async_copy(some, out.at[self.s], refs.asem.at[k]).wait()
            remote(some, out.at[1 - self.s], refs.psem, refs.qsem.at[k], {"section": 1 - self.s}).wait_recv()
        whole = refs.act_o
        remote(whole, whole, refs.psem, refs.qsem.at[0], {"section": 1 - self.s}).wait_send()
        ref = refs.td.at[pl.ds(0, 3)]
        remote(ref, ref, refs.dsem, refs.dr.at[0], self.near_x(1)).wait_send()
        ref = refs.tu.at[pl.ds(0, 3)]
        remote(ref, ref, refs.usem, refs.ur.at[0], self.near_x(1)).wait_send()
        ref = refs.zd.at[pl.ds(0, NZ - 1)]
        remote(ref, ref, refs.zsem.at[0], refs.dr.at[0], self.near_x(1)).wait_send()
        ref = refs.zu.at[pl.ds(0, NZ - 1)]
        remote(ref, ref, refs.zsem.at[1], refs.dr.at[0], self.near_x(1)).wait_send()


def grads_scratch():
    dma = pltpu.SemaphoreType.DMA
    buffers = {
        "xs": (2, 4, SEQ, ROUND),
        "xg": (2, 4, SEQ, ROUND),
        "xr": (2, SEQ, ROUND),
        "ys": (2, 4, SEQ, SIDE),
        "yg": (2, 4, SEQ, SIDE),
        "yr": (2, SEQ, SIDE),
        "td": (4, 320, LAT),
        "sd": (4, 320, LAT),
        "zd": (NZ, 40, LAT),
        "zr": (NZ, 40, LAT),
        "tu": (4, 256, LAT),
        "su": (4, 256, LAT),
        "zu": (NZ, 32, LAT),
        "zv": (NZ, 32, LAT),
    }
    sems = {
        "xssem": dma,
        "xfsem": dma((2, 4)),
        "xrsem": dma((2,)),
        "yssem": dma,
        "yfsem": dma((2, 4)),
        "yrsem": dma((2,)),
        "psem": dma,
        "qsem": dma((2,)),
        "asem": dma((2,)),
        "dsem": dma,
        "dr": dma((3,)),
        "usem": dma,
        "ur": dma((3,)),
        "zsem": dma((2,)),
        "zrecv": dma((2, NZ - 1)),
    }
    return {**{k: pltpu.VMEM(v, bf16) for k, v in buffers.items()}, **sems}


def place_kernel(act, grad, down, qk, up, act_o, grad_o, down_o, qk_o, up_o):
    act_o[...] = act[...]
    grad_o[...] = grad[...]
    down_o[...] = down[...].reshape(28, 1, LAT)
    qk_o[...] = qk[...]
    up_o[...] = up[...].reshape(28, 1, LAT)


def place_results(results):
    return pl.pallas_call(
        place_kernel,
        name="place_results",
        out_shape=[
            shaped(2, *TOKENS),
            shaped(2, *TOKENS),
            shaped(28, 1, LAT, dtype=f32),
            shaped(2, LAT, dtype=f32),
            shaped(28, 1, LAT, dtype=f32),
        ],
        in_specs=[VMEM] * 5,
        out_specs=[VMEM] * 5,
    )(*results)


def swap(value):
    return lax.ppermute(value, "section", [(0, 1), (1, 0)])


def body(x_in, dy_out, routes, gates, w_down, w_qk, w_up, e_gate, e_up, e_down):
    section = lax.axis_index("section")
    attn_own = (w_down[0], w_qk[0], w_up[0])
    experts_own = (e_gate[0, 0], e_up[0, 0], e_down[0, 0])
    attn = attn_own + tuple(swap(w) for w in attn_own)
    def both_layers(table):
        other = swap(lax.dynamic_index_in_dim(table, 1 - section, 0, keepdims=False))
        own = lax.dynamic_index_in_dim(table, section, 0, keepdims=False)
        return (jnp.where(section == 0, own, other), jnp.where(section == 0, other, own))

    route_cols = both_layers(routes[0, :, 0])
    gate_cols = both_layers(gates[0, :, 0])
    route_rows = tuple(r.reshape(1, SEQ) for r in route_cols)

    whole = {
        "x": (x_in[:, 0], VMEM),
        "dy": (dy_out[:, 0], VMEM),
        **{f"route_row{k}": (route_rows[k], VMEM) for k in range(2)},
        **{f"route_col{k}": (route_cols[k], VMEM) for k in range(2)},
        **{f"gate_col{k}": (gate_cols[k], VMEM) for k in range(2)},
        **named("attn", [(w, ANY) for w in attn]),
        **named("expert", [(w, ANY) for w in experts_own]),
    }
    kept = fused(
        forward_run,
        "forward",
        whole,
        {
            "act0": shaped(*TOKENS),
            **kept_shapes(0),
            **kept_shapes(1),
            "gate0": shaped(*PRE, dtype=f32),
            "up0": shaped(*PRE, dtype=f32),
            "part1": shaped(*ROWS),
            "homeb": shaped(*HOME),
        },
        {
            **COMMON,
            **Experts.scratch(2),
            "hidden": pltpu.VMEM(PRE, bf16),
            **dispatch_scratch("a"),
            **dispatch_scratch("b"),
            **dispatch_scratch("c"),
            **combine_scratch("a"),
            **combine_scratch("b", skip=("homeb",)),
        },
        0,
    )
    part1, back1 = kept.pop("part1"), kept.pop("homeb")
    done = fused(
        backward_run,
        "backward",
        {
            **whole,
            **{k: (v, VMEM) for k, v in kept.items()},
            "parta": (part1, VMEM),
            "back1": (back1, VMEM),
        },
        {
            "act_o": shaped(2, *TOKENS),
            "grad_o": shaped(2, *TOKENS),
            "down_o": shaped(28, LAT, dtype=f32),
            "qk_o": shaped(2, LAT, dtype=f32),
            "up_o": shaped(28, LAT, dtype=f32),
        },
        {
            **COMMON,
            "act1": pltpu.VMEM(TOKENS, bf16),
            **factor_scratch(0),
            **factor_scratch(1),
            **grads_scratch(),
            **Experts.scratch(1),
            **dispatch_scratch("a"),
            **combine_scratch("a", skip=("parta",)),
            **combine_scratch("b"),
        },
        1,
    )
    activations, grads_in, g_down, g_qk, g_up_t = place_results(list(done.values()))
    return (
        activations[None, :, None],
        grads_in[None, :, None],
        jnp.swapaxes(g_down, 0, 1),
        g_qk[None],
        jnp.swapaxes(g_up_t, 0, 1),
    )


def solution(mesh):
    placed = (
        P(None, ("expert", "dp"), None, None),
        P(None, ("expert", "dp"), None, None),
        P("section", None, ("expert", "dp"), None, None),
        P("section", None, ("expert", "dp"), None, None),
        P("section", None, None),
        P("section", None, None),
        P("section", None, None),
        P("section", "expert", None, "dp"),
        P("section", "expert", None, "dp"),
        P("section", "expert", "dp", None),
    )
    return jax.shard_map(
        body,
        mesh=mesh,
        in_specs=placed,
        out_specs=(
            P("section", None, ("expert", "dp"), None, None),
            P("section", None, ("expert", "dp"), None, None),
            P("section", ("expert", "dp"), None),
            P("section", ("expert", "dp"), None),
            P("section", ("expert", "dp"), None),
        ),
        check_vma=False,
    )
```
